128 devices in a mesh: gx: 16 (over z_hi, x, core), gy: 4 (over y), gz: 2 (over z_lo).
Axes of the slice: x: 4, y: 4, z: 4 (z_hi: 2, z_lo: 2; z = z_hi * 2 + z_lo), core: 2. Of those that a mesh axis runs over, the one named last changes fastest.
Arguments:
- cells: bfloat16 [4, 64, 256, 256], P(None, 'gx', 'gy', 'gz'), may hold values from -6 to 6
- weight: bfloat16 [32, 4, 3, 3, 3], replicated, may hold values from -0.625 to 0.625
- bias: float32 [32], replicated, may hold values from -3 to 3
- cotangent: bfloat16 [32, 32, 128, 128], P(None, 'gx', 'gy', 'gz'), may hold values from -6 to 6
Outputs:
- pooled: bfloat16 [32, 32, 128, 128], P(None, 'gx', 'gy', 'gz')
- weight_grad: float32 [32, 4, 3, 3, 3], replicated
- bias_grad: float32 [32], replicated
- input_grad: float32 [4, 64, 256, 256], P(None, 'gx', 'gy', 'gz')
The draws below stay inside these ranges and needn't reach their ends.
All inputs are finite; a program needn't handle non-finite values.
Results may differ from the reference program's by a relative error of at most 0.0029.
Values may be sent and summed in bfloat16 or wider, within the bound.
A program may use at most 128 MiB of HBM per device.

```python
import jax
import jax.numpy as jnp
from jax import lax

CIN = 4
COUT = 32
CX = 4
NX = 64
NY = 256
NZ = 256
N_GX = 16


def block_levels(rng, dims, split, least, top_value):
    loudness = 1.0
    for axis_at, parts in split:
        draws = jax.random.uniform(jax.random.fold_in(jax.random.fold_in(rng, 6), axis_at), (parts,), jnp.float32, least / len(split), top_value / len(split))
        loudness = loudness * jnp.repeat(jnp.exp(draws), dims[axis_at] // parts).reshape((-1,) + (1,) * (len(dims) - 1 - axis_at))
    return loudness


def scatter_about(rng, extent, scale, limit, split=(), kind=jnp.bfloat16):
    factor_of = block_levels(rng, extent, split, -0.22, 0.18) if split else 1.0
    entries = jax.random.normal(rng, extent, jnp.float32) * scale * factor_of
    return jnp.minimum(jnp.maximum(entries, -limit), limit).astype(kind)


def setup_inputs(seed: int = 0) -> dict:
    seeds = jax.random.split(jax.random.key(seed), 5)
    cells = scatter_about(seeds[0], (CIN, NX, NY, NZ), 1.0, 6.0, ((1, 16), (2, 4), (3, 2)))
    weight = scatter_about(seeds[1], (COUT, CIN, 3, 3, 3), (CIN * 27) ** -0.5, 0.625)
    bias = scatter_about(seeds[2], (COUT,), 0.5, 3.0, (), jnp.float32)
    cotangent = scatter_about(seeds[3], (COUT, NX // 2, NY // 2, NZ // 2), 1.0, 6.0, ((1, 16), (2, 4), (3, 2)))
    return {"cells": cells, "weight": weight, "bias": bias, "cotangent": cotangent}


leak_slope = 0.3
soft_scale = 10.0


def activate(preact):
    return leak_slope * preact + (1.0 - leak_slope) / soft_scale * jax.nn.softplus(soft_scale * preact)


def slope_of(preact):
    return leak_slope + (1.0 - leak_slope) * jax.nn.sigmoid(soft_scale * preact)


def correlate(volume, kernel):
    return lax.conv_general_dilated(volume[None], kernel, (1, 1, 1), "VALID", dimension_numbers=("NCDHW", "OIDHW", "NCDHW"), precision=lax.Precision.HIGHEST)[0]


def reference(cells, weight, bias, cotangent):
    kernel = weight.astype(jnp.float32)
    flipped = jnp.transpose(kernel[:, :, ::-1, ::-1, ::-1], (1, 0, 2, 3, 4))
    wrapped = jnp.pad(cells.astype(jnp.float32), ((0, 0), (0, 0), (1, 1), (1, 1)), mode="wrap")
    cot_full = cotangent.astype(jnp.float32)

    def one_slab(index):
        start = index * CX
        rows_in = (start - 2 + jnp.arange(CX + 4, dtype=jnp.int32)) % NX
        slab_in = jnp.take(wrapped, rows_in, axis=1)
        preact = correlate(slab_in, kernel) + bias.astype(jnp.float32)[:, None, None, None]
        activated = activate(preact)[:, 1:CX + 1]
        pooled = activated.reshape(COUT, CX // 2, 2, NY // 2, 2, NZ // 2, 2).mean(axis=(2, 4, 6)).astype(jnp.bfloat16)
        rows_pre = (start - 1 + jnp.arange(CX + 2, dtype=jnp.int32)) % NX
        spread = jnp.take(cot_full, rows_pre // 2, axis=1)
        spread = jnp.repeat(jnp.repeat(spread, 2, axis=2), 2, axis=3)
        delta = (slope_of(preact) * spread * 0.125).astype(jnp.bfloat16).astype(jnp.float32)
        delta_pad = jnp.pad(delta, ((0, 0), (0, 0), (1, 1), (1, 1)), mode="wrap")
        grad_slab = correlate(delta_pad, flipped)
        central = delta[:, 1:CX + 1]
        padded_central = slab_in[:, 1:CX + 3]
        terms = []
        for shift_a in range(3):
            for shift_b in range(3):
                for shift_e in range(3):
                    window = padded_central[:, shift_a:shift_a + CX, shift_b:shift_b + NY, shift_e:shift_e + NZ]
                    terms.append(jnp.einsum("oxyz,cxyz->oc", central, window, precision=lax.Precision.HIGHEST))
        weight_part = jnp.stack(terms, axis=2).reshape(COUT, CIN, 3, 3, 3)
        bias_part = jnp.sum(central, axis=(1, 2, 3))
        return pooled, grad_slab, weight_part, bias_part

    pooled, grads, weight_parts, bias_parts = lax.map(one_slab, jnp.arange(N_GX, dtype=jnp.int32))
    pooled = jnp.moveaxis(pooled, 0, 1).reshape(COUT, NX // 2, NY // 2, NZ // 2)
    input_grad = jnp.moveaxis(grads, 0, 1).reshape(CIN, NX, NY, NZ)
    return pooled, jnp.sum(weight_parts, axis=0), jnp.sum(bias_parts, axis=0), input_grad
```

```python
import jax
import jax.numpy as jnp
from jax import lax
from jax.experimental import pallas as pl
from jax.experimental.pallas import tpu as pltpu
from jax.sharding import PartitionSpec as P

MESH = pl.DeviceIdType.MESH
AXES = ("gx", "gy", "gz")

leak_slope = 0.3
soft_scale = 10.0


def extended(cells, sides, width):
    for axis, dim in sides:
        count = lax.axis_size(axis)
        head = lax.slice_in_dim(cells, 0, width, axis=dim)
        tail = lax.slice_in_dim(cells, cells.shape[dim] - width, cells.shape[dim], axis=dim)
        cells = jnp.concatenate(
            [
                lax.ppermute(tail, axis, [(i, (i + 1) % count) for i in range(count)]),
                cells,
                lax.ppermute(head, axis, [((i + 1) % count, i) for i in range(count)]),
            ],
            axis=dim,
        )
    return cells


def allreduce_kernel(sizes, x_ref, o_ref, slots_x, slots_y, slots_z, acc_x, acc_y,
                     send_x, recv_x, send_y, recv_y, send_z, recv_z):
    me = tuple(lax.axis_index(a) for a in AXES)
    slots = (slots_x, slots_y, slots_z)
    sends = (send_x, send_y, send_z)
    recvs = (recv_x, recv_y, recv_z)
    sources = (x_ref, acc_x, acc_y)
    sinks = (acc_x, acc_y, o_ref)

    def peer(axis, index):
        return tuple(index if k == axis else me[k] for k in range(3))

    barrier = pltpu.get_barrier_semaphore()
    count = 0
    for axis, n in enumerate(sizes):
        for d in range(1, n):
            target = lax.rem(me[axis] + d, n)
            pl.semaphore_signal(barrier, inc=1, device_id=peer(axis, target), device_id_type=MESH)
            count += 1
    pl.semaphore_wait(barrier, count)

    for axis, n in enumerate(sizes):
        src, held, sink = sources[axis], slots[axis], sinks[axis]
        mine = me[axis]
        copies = []
        for d in range(1, n):
            target = lax.rem(mine + d, n)
            copy = pltpu.make_async_remote_copy(
                src_ref=src,
                dst_ref=held.at[mine],
                send_sem=sends[axis].at[d],
                recv_sem=recvs[axis].at[mine],
                device_id=peer(axis, target),
                device_id_type=MESH,
            )
            copy.start()
            copies.append(copy)
        held[mine] = src[...]
        for d in range(1, n):
            origin = lax.rem(mine + n - d, n)
            incoming = pltpu.make_async_remote_copy(
                src_ref=src,
                dst_ref=held.at[origin],
                send_sem=sends[axis].at[d],
                recv_sem=recvs[axis].at[origin],
                device_id=peer(axis, origin),
                device_id_type=MESH,
            )
            incoming.wait_recv()
        for copy in copies:
            copy.wait_send()
        total = held[0]
        for k in range(1, n):
            total = total + held[k]
        sink[...] = total


def allreduce(x, sizes):
    shape = x.shape
    return pl.pallas_call(
        lambda *refs: allreduce_kernel(sizes, *refs),
        out_shape=jax.ShapeDtypeStruct(shape, jnp.float32),
        in_specs=[pl.BlockSpec(memory_space=pltpu.VMEM)],
        out_specs=pl.BlockSpec(memory_space=pltpu.VMEM),
        scratch_shapes=[
            pltpu.VMEM((sizes[0],) + shape, jnp.float32),
            pltpu.VMEM((sizes[1],) + shape, jnp.float32),
            pltpu.VMEM((sizes[2],) + shape, jnp.float32),
            pltpu.VMEM(shape, jnp.float32),
            pltpu.VMEM(shape, jnp.float32),
            pltpu.SemaphoreType.DMA((sizes[0],)),
            pltpu.SemaphoreType.DMA((sizes[0],)),
            pltpu.SemaphoreType.DMA((sizes[1],)),
            pltpu.SemaphoreType.DMA((sizes[1],)),
            pltpu.SemaphoreType.DMA((sizes[2],)),
            pltpu.SemaphoreType.DMA((sizes[2],)),
        ],
        compiler_params=pltpu.CompilerParams(collective_id=0, has_side_effects=True),
    )(x)


def activate(preact):
    return leak_slope * preact + (1.0 - leak_slope) / soft_scale * jax.nn.softplus(
        soft_scale * preact
    )


def slope_of(preact):
    return leak_slope + (1.0 - leak_slope) * jax.nn.sigmoid(soft_scale * preact)


def on_device(cells, weight, bias, cotangent):
    chan_in, cells_x, cells_y, cells_z = cells.shape
    chan_out = weight.shape[0]
    stencil = [
        (shift_a, shift_b, shift_e)
        for shift_a in range(3)
        for shift_b in range(3)
        for shift_e in range(3)
    ]
    widened = extended(cells, (("gx", 1), ("gy", 2), ("gz", 3)), 1)
    patches = jnp.stack(
        [
            widened[:, sa : sa + cells_x, sb : sb + cells_y, se : se + cells_z]
            for sa, sb, se in stencil
        ],
        axis=1,
    )
    patches = patches.reshape(chan_in * 27, cells_x, cells_y, cells_z)
    weight_mat = weight.reshape(chan_out, chan_in * 27)
    preact = (
        jnp.einsum("ok,kxyz->oxyz", weight_mat, patches, preferred_element_type=jnp.float32)
        + bias[:, None, None, None]
    )
    activated = activate(preact)
    pooled = (
        activated.reshape(chan_out, cells_x // 2, 2, cells_y // 2, 2, cells_z // 2, 2)
        .mean(axis=(2, 4, 6))
        .astype(jnp.bfloat16)
    )
    spread = jnp.broadcast_to(
        cotangent.astype(jnp.float32)[:, :, None, :, None, :, None],
        (chan_out, cells_x // 2, 2, cells_y // 2, 2, cells_z // 2, 2),
    )
    spread = spread.reshape(chan_out, cells_x, cells_y, cells_z)
    delta = (slope_of(preact) * spread * 0.125).astype(jnp.bfloat16)
    weight_local = jnp.einsum("oxyz,kxyz->ok", delta, patches, preferred_element_type=jnp.float32)
    bias_local = jnp.sum(delta, axis=(1, 2, 3), dtype=jnp.float32)
    taps = chan_in * 27
    width = -(-(taps + 1) // 128) * 128
    partial = jnp.concatenate(
        [weight_local, bias_local[:, None], jnp.zeros((chan_out, width - taps - 1), jnp.float32)],
        axis=1,
    )
    sizes = tuple(lax.axis_size(a) for a in AXES)
    both = allreduce(partial, sizes)
    weight_grad = both[:, :taps].reshape(chan_out, chan_in, 3, 3, 3)
    bias_grad = both[:, taps]
    delta_wide = extended(delta, (("gx", 1), ("gy", 2), ("gz", 3)), 1)
    input_grad = jnp.zeros((chan_in, cells_x, cells_y, cells_z), jnp.float32)
    for sa, sb, se in stencil:
        window = delta_wide[:, sa : sa + cells_x, sb : sb + cells_y, se : se + cells_z]
        input_grad = input_grad + jnp.einsum(
            "oc,oxyz->cxyz",
            weight[:, :, 2 - sa, 2 - sb, 2 - se],
            window,
            preferred_element_type=jnp.float32,
        )
    return (pooled, weight_grad, bias_grad, input_grad)


def solution(mesh):
    in_specs = (P(None, "gx", "gy", "gz"), P(), P(), P(None, "gx", "gy", "gz"))
    out_specs = (P(None, "gx", "gy", "gz"), P(), P(), P(None, "gx", "gy", "gz"))
    return jax.shard_map(
        on_device, mesh=mesh, in_specs=in_specs, out_specs=out_specs, check_vma=False
    )
```

```python
import jax
import jax.numpy as jnp
from jax import lax
from jax.experimental import pallas as pl
from jax.experimental.pallas import tpu as pltpu
from jax.sharding import PartitionSpec as P

MESH = pl.DeviceIdType.MESH
AXES = ("gx", "gy", "gz")

leak_slope = 0.3
soft_scale = 10.0


def extended(cells, sides, width):
    for axis, dim in sides:
        count = lax.axis_size(axis)
        head = lax.slice_in_dim(cells, 0, width, axis=dim)
        tail = lax.slice_in_dim(cells, cells.shape[dim] - width, cells.shape[dim], axis=dim)
        cells = jnp.concatenate(
            [
                lax.ppermute(tail, axis, [(i, (i + 1) % count) for i in range(count)]),
                cells,
                lax.ppermute(head, axis, [((i + 1) % count, i) for i in range(count)]),
            ],
            axis=dim,
        )
    return cells


def allreduce_kernel(sizes, x_ref, o_ref, slots_x, slots_y, slots_z, acc_x, acc_y,
                     send_x, recv_x, send_y, recv_y, send_z, recv_z):
    me = tuple(lax.axis_index(a) for a in AXES)
    slots = (slots_x, slots_y, slots_z)
    sends = (send_x, send_y, send_z)
    recvs = (recv_x, recv_y, recv_z)
    sources = (x_ref, acc_x, acc_y)
    sinks = (acc_x, acc_y, o_ref)

    def peer(axis, index):
        return tuple(index if k == axis else me[k] for k in range(3))

    barrier = pltpu.get_barrier_semaphore()
    count = 0
    for axis, n in enumerate(sizes):
        for d in range(1, n):
            target = lax.rem(me[axis] + d, n)
            pl.semaphore_signal(barrier, inc=1, device_id=peer(axis, target), device_id_type=MESH)
            count += 1
    pl.semaphore_wait(barrier, count)

    for axis, n in enumerate(sizes):
        src, held, sink = sources[axis], slots[axis], sinks[axis]
        mine = me[axis]
        copies = []
        for d in range(1, n):
            target = lax.rem(mine + d, n)
            copy = pltpu.make_async_remote_copy(
                src_ref=src,
                dst_ref=held.at[mine],
                send_sem=sends[axis].at[d],
                recv_sem=recvs[axis].at[mine],
                device_id=peer(axis, target),
                device_id_type=MESH,
            )
            copy.start()
            copies.append(copy)
        held[mine] = src[...]
        for d in range(1, n):
            origin = lax.rem(mine + n - d, n)
            incoming = pltpu.make_async_remote_copy(
                src_ref=src,
                dst_ref=held.at[origin],
                send_sem=sends[axis].at[d],
                recv_sem=recvs[axis].at[origin],
                device_id=peer(axis, origin),
                device_id_type=MESH,
            )
            incoming.wait_recv()
        for copy in copies:
            copy.wait_send()
        total = held[0]
        for k in range(1, n):
            total = total + held[k]
        sink[...] = total


def allreduce(x, sizes):
    shape = x.shape
    return pl.pallas_call(
        lambda *refs: allreduce_kernel(sizes, *refs),
        out_shape=jax.ShapeDtypeStruct(shape, jnp.float32),
        in_specs=[pl.BlockSpec(memory_space=pltpu.VMEM)],
        out_specs=pl.BlockSpec(memory_space=pltpu.VMEM),
        scratch_shapes=[
            pltpu.VMEM((sizes[0],) + shape, jnp.float32),
            pltpu.VMEM((sizes[1],) + shape, jnp.float32),
            pltpu.VMEM((sizes[2],) + shape, jnp.float32),
            pltpu.VMEM(shape, jnp.float32),
            pltpu.VMEM(shape, jnp.float32),
            pltpu.SemaphoreType.DMA((sizes[0],)),
            pltpu.SemaphoreType.DMA((sizes[0],)),
            pltpu.SemaphoreType.DMA((sizes[1],)),
            pltpu.SemaphoreType.DMA((sizes[1],)),
            pltpu.SemaphoreType.DMA((sizes[2],)),
            pltpu.SemaphoreType.DMA((sizes[2],)),
        ],
        compiler_params=pltpu.CompilerParams(collective_id=0, has_side_effects=True),
    )(x)


def activate(preact):
    return leak_slope * preact + (1.0 - leak_slope) / soft_scale * jax.nn.softplus(
        soft_scale * preact
    )


def slope_of(preact):
    return leak_slope + (1.0 - leak_slope) * jax.nn.sigmoid(soft_scale * preact)


def forward_kernel(chunk, w_ref, b_ref, p_ref, cot_ref, pooled_ref, delta_ref, wg_ref, bg_ref,
                   pool_acc, wg_acc, bg_acc):
    step = pl.program_id(0)
    steps = pl.num_programs(0)
    lanes = p_ref.shape[-1]

    @pl.when(step == 0)
    def _():
        pool_acc[...] = jnp.zeros_like(pool_acc)
        wg_acc[...] = jnp.zeros_like(wg_acc)
        bg_acc[...] = jnp.zeros_like(bg_acc)

    weight = w_ref[...]
    bias = b_ref[...]

    @pl.loop(0, lanes // chunk)
    def _(q):
        cols = pl.ds(pl.multiple_of(q * chunk, chunk), chunk)
        patch = p_ref[0, :, cols]
        preact = jnp.dot(weight, patch, preferred_element_type=jnp.float32) + bias
        scaled = soft_scale * preact
        e = jnp.exp(-jnp.abs(scaled))
        softplus = jnp.maximum(scaled, 0.0) + jnp.log1p(e)
        activated = leak_slope * preact + (1.0 - leak_slope) / soft_scale * softplus
        pool_acc[:, cols] += activated
        sigmoid = jnp.where(scaled >= 0.0, 1.0, e) / (1.0 + e)
        slope = leak_slope + (1.0 - leak_slope) * sigmoid
        delta = (slope * cot_ref[:, cols].astype(jnp.float32) * 0.125).astype(jnp.bfloat16)
        delta_ref[0, :, cols] = delta
        wg_acc[...] += lax.dot_general(
            delta, patch, (((1,), (1,)), ((), ())), preferred_element_type=jnp.float32
        )
        bg_acc[...] += jnp.sum(delta.astype(jnp.float32), axis=1, keepdims=True)

    @pl.when(step == steps - 1)
    def _():
        pooled_ref[...] = (pool_acc[...] * 0.125).astype(pooled_ref.dtype)
        wg_ref[...] = wg_acc[...]
        bg_ref[...] = bg_acc[...]


def forward(weight_mat, bias, patches, cot):
    parities, taps, lanes = patches.shape
    chan_out = weight_mat.shape[0]
    full = lambda shape: pl.BlockSpec(shape, lambda p: (0,) * len(shape))
    return pl.pallas_call(
        lambda *refs: forward_kernel(512, *refs),
        grid=(parities,),
        out_shape=(
            jax.ShapeDtypeStruct((chan_out, lanes), jnp.bfloat16),
            jax.ShapeDtypeStruct((parities, chan_out, lanes), jnp.bfloat16),
            jax.ShapeDtypeStruct((chan_out, taps), jnp.float32),
            jax.ShapeDtypeStruct((chan_out, 1), jnp.float32),
        ),
        in_specs=[
            full((chan_out, taps)),
            full((chan_out, 1)),
            pl.BlockSpec((1, taps, lanes), lambda p: (p, 0, 0)),
            full((chan_out, lanes)),
        ],
        out_specs=(
            full((chan_out, lanes)),
            pl.BlockSpec((1, chan_out, lanes), lambda p: (p, 0, 0)),
            full((chan_out, taps)),
            full((chan_out, 1)),
        ),
        scratch_shapes=[
            pltpu.VMEM((chan_out, lanes), jnp.float32),
            pltpu.VMEM((chan_out, taps), jnp.float32),
            pltpu.VMEM((chan_out, 1), jnp.float32),
        ],
    )(weight_mat, bias, patches, cot)


def on_device(cells, weight, bias, cotangent):
    chan_in, cells_x, cells_y, cells_z = cells.shape
    chan_out = weight.shape[0]
    hx, hy, hz = cells_x // 2, cells_y // 2, cells_z // 2
    stencil = [
        (shift_a, shift_b, shift_e)
        for shift_a in range(3)
        for shift_b in range(3)
        for shift_e in range(3)
    ]
    widened = extended(cells, (("gx", 1), ("gy", 2), ("gz", 3)), 1)
    subgrids = {}
    for ox in range(4):
        for oy in range(4):
            for oz in range(4):
                sub = widened[:, ox : ox + cells_x - 1 : 2, oy : oy + cells_y - 1 : 2, oz : oz + cells_z - 1 : 2]
                subgrids[ox, oy, oz] = sub.reshape(chan_in, 1, hx * hy * hz)
    patches = jnp.stack(
        [
            jnp.concatenate(
                [subgrids[px + sa, py + sb, pz + se] for sa, sb, se in stencil], axis=1
            ).reshape(chan_in * 27, hx * hy * hz)
            for px in range(2)
            for py in range(2)
            for pz in range(2)
        ],
        axis=0,
    )
    weight_mat = weight.reshape(chan_out, chan_in * 27)
    cot = cotangent.reshape(chan_out, hx * hy * hz)
    pooled, delta_par, weight_local, bias_local = forward(
        weight_mat, bias.reshape(chan_out, 1), patches, cot
    )
    pooled = pooled.reshape(chan_out, hx, hy, hz)
    delta = jnp.zeros((chan_out, cells_x, cells_y, cells_z), jnp.bfloat16)
    for px in range(2):
        for py in range(2):
            for pz in range(2):
                block = delta_par[px * 4 + py * 2 + pz].reshape(chan_out, hx, hy, hz)
                delta = delta.at[:, px::2, py::2, pz::2].set(block)
    taps = chan_in * 27
    width = -(-(taps + 1) // 128) * 128
    partial = jnp.concatenate(
        [weight_local, bias_local, jnp.zeros((chan_out, width - taps - 1), jnp.float32)],
        axis=1,
    )
    sizes = tuple(lax.axis_size(a) for a in AXES)
    both = allreduce(partial, sizes)
    weight_grad = both[:, :taps].reshape(chan_out, chan_in, 3, 3, 3)
    bias_grad = both[:, taps]
    delta_wide = extended(delta, (("gx", 1), ("gy", 2), ("gz", 3)), 1)
    input_grad = jnp.zeros((chan_in, cells_x, cells_y, cells_z), jnp.float32)
    for sa, sb, se in stencil:
        window = delta_wide[:, sa : sa + cells_x, sb : sb + cells_y, se : se + cells_z]
        input_grad = input_grad + jnp.einsum(
            "oc,oxyz->cxyz",
            weight[:, :, 2 - sa, 2 - sb, 2 - se],
            window,
            preferred_element_type=jnp.float32,
        )
    return (pooled, weight_grad, bias_grad, input_grad)


def solution(mesh):
    in_specs = (P(None, "gx", "gy", "gz"), P(), P(), P(None, "gx", "gy", "gz"))
    out_specs = (P(None, "gx", "gy", "gz"), P(), P(), P(None, "gx", "gy", "gz"))
    return jax.shard_map(
        on_device, mesh=mesh, in_specs=in_specs, out_specs=out_specs, check_vma=False
    )
```

```python
import jax
import jax.numpy as jnp
from jax import lax
from jax.experimental import pallas as pl
from jax.experimental.pallas import tpu as pltpu
from jax.sharding import PartitionSpec as P

MESH = pl.DeviceIdType.MESH
AXES = ("gx", "gy", "gz")

leak_slope = 0.3
soft_scale = 10.0


def extended(cells, sides, width):
    for axis, dim in sides:
        count = lax.axis_size(axis)
        head = lax.slice_in_dim(cells, 0, width, axis=dim)
        tail = lax.slice_in_dim(cells, cells.shape[dim] - width, cells.shape[dim], axis=dim)
        cells = jnp.concatenate(
            [
                lax.ppermute(tail, axis, [(i, (i + 1) % count) for i in range(count)]),
                cells,
                lax.ppermute(head, axis, [((i + 1) % count, i) for i in range(count)]),
            ],
            axis=dim,
        )
    return cells


def allreduce_kernel(sizes, x_ref, o_ref, slots_x, slots_y, slots_z, acc_x, acc_y,
                     send_x, recv_x, send_y, recv_y, send_z, recv_z):
    me = tuple(lax.axis_index(a) for a in AXES)
    slots = (slots_x, slots_y, slots_z)
    sends = (send_x, send_y, send_z)
    recvs = (recv_x, recv_y, recv_z)
    sources = (x_ref, acc_x, acc_y)
    sinks = (acc_x, acc_y, o_ref)

    def peer(axis, index):
        return tuple(index if k == axis else me[k] for k in range(3))

    barrier = pltpu.get_barrier_semaphore()
    count = 0
    for axis, n in enumerate(sizes):
        for d in range(1, n):
            target = lax.rem(me[axis] + d, n)
            pl.semaphore_signal(barrier, inc=1, device_id=peer(axis, target), device_id_type=MESH)
            count += 1
    pl.semaphore_wait(barrier, count)

    for axis, n in enumerate(sizes):
        src, held, sink = sources[axis], slots[axis], sinks[axis]
        mine = me[axis]
        copies = []
        for d in range(1, n):
            target = lax.rem(mine + d, n)
            copy = pltpu.make_async_remote_copy(
                src_ref=src,
                dst_ref=held.at[mine],
                send_sem=sends[axis].at[d],
                recv_sem=recvs[axis].at[mine],
                device_id=peer(axis, target),
                device_id_type=MESH,
            )
            copy.start()
            copies.append(copy)
        held[mine] = src[...]
        for d in range(1, n):
            origin = lax.rem(mine + n - d, n)
            incoming = pltpu.make_async_remote_copy(
                src_ref=src,
                dst_ref=held.at[origin],
                send_sem=sends[axis].at[d],
                recv_sem=recvs[axis].at[origin],
                device_id=peer(axis, origin),
                device_id_type=MESH,
            )
            incoming.wait_recv()
        for copy in copies:
            copy.wait_send()
        total = held[0]
        for k in range(1, n):
            total = total + held[k]
        sink[...] = total


def allreduce(x, sizes):
    shape = x.shape
    return pl.pallas_call(
        lambda *refs: allreduce_kernel(sizes, *refs),
        out_shape=jax.ShapeDtypeStruct(shape, jnp.float32),
        in_specs=[pl.BlockSpec(memory_space=pltpu.VMEM)],
        out_specs=pl.BlockSpec(memory_space=pltpu.VMEM),
        scratch_shapes=[
            pltpu.VMEM((sizes[0],) + shape, jnp.float32),
            pltpu.VMEM((sizes[1],) + shape, jnp.float32),
            pltpu.VMEM((sizes[2],) + shape, jnp.float32),
            pltpu.VMEM(shape, jnp.float32),
            pltpu.VMEM(shape, jnp.float32),
            pltpu.SemaphoreType.DMA((sizes[0],)),
            pltpu.SemaphoreType.DMA((sizes[0],)),
            pltpu.SemaphoreType.DMA((sizes[1],)),
            pltpu.SemaphoreType.DMA((sizes[1],)),
            pltpu.SemaphoreType.DMA((sizes[2],)),
            pltpu.SemaphoreType.DMA((sizes[2],)),
        ],
        compiler_params=pltpu.CompilerParams(collective_id=0, has_side_effects=True),
    )(x)


def activate(preact):
    return leak_slope * preact + (1.0 - leak_slope) / soft_scale * jax.nn.softplus(
        soft_scale * preact
    )


def slope_of(preact):
    return leak_slope + (1.0 - leak_slope) * jax.nn.sigmoid(soft_scale * preact)


def forward_kernel(rows, w_ref, b_ref, q_ref, u_ref, p_ref, cot_ref,
                   pooled_ref, delta_ref, wg_ref, bg_ref, wg_acc, bg_acc):
    step = pl.program_id(0)
    plane = p_ref.shape[-1] // 2
    chunk = 4 * rows

    @pl.when(step == 0)
    def _():
        wg_acc[...] = jnp.zeros_like(wg_acc)
        bg_acc[...] = jnp.zeros_like(bg_acc)

    weight = w_ref[...]
    bias = b_ref[...]

    @pl.loop(0, plane // chunk)
    def _(j):
        cot = cot_ref[:, pl.ds(pl.multiple_of(j * rows, rows), rows)]
        up_lo = jnp.dot(cot, u_ref[0], preferred_element_type=jnp.float32) * 0.125
        up_hi = jnp.dot(cot, u_ref[1], preferred_element_type=jnp.float32) * 0.125
        spread = jnp.concatenate([up_lo, up_lo, up_hi, up_hi], axis=1)
        total = None
        for base in (0, plane):
            cols = pl.ds(pl.multiple_of(base + j * chunk, chunk), chunk)
            patch = p_ref[:, cols]
            preact = jnp.dot(weight, patch, preferred_element_type=jnp.float32) + bias
            scaled = soft_scale * preact
            e = jnp.exp(-jnp.abs(scaled))
            softplus = jnp.maximum(scaled, 0.0) + jnp.log1p(e)
            activated = leak_slope * preact + (1.0 - leak_slope) / soft_scale * softplus
            total = activated if total is None else total + activated
            sigmoid = jnp.where(scaled >= 0.0, 1.0, e) / (1.0 + e)
            slope = leak_slope + (1.0 - leak_slope) * sigmoid
            delta = (slope * spread).astype(jnp.bfloat16)
            delta_ref[:, cols] = delta
            wg_acc[...] += lax.dot_general(
                delta, patch, (((1,), (1,)), ((), ())), preferred_element_type=jnp.float32
            )
            bg_acc[...] += jnp.sum(delta.astype(jnp.float32), axis=1, keepdims=True)
        pair_lo = total[:, 0:rows] + total[:, rows : 2 * rows]
        pair_hi = total[:, 2 * rows : 3 * rows] + total[:, 3 * rows : 4 * rows]
        pooled = jnp.dot(
            pair_lo, q_ref[0], preferred_element_type=jnp.float32, precision=lax.Precision.HIGHEST
        ) + jnp.dot(
            pair_hi, q_ref[1], preferred_element_type=jnp.float32, precision=lax.Precision.HIGHEST
        )
        pooled_ref[:, pl.ds(pl.multiple_of(j * rows, rows), rows)] = (pooled * 0.125).astype(
            pooled_ref.dtype
        )

    @pl.when(step == pl.num_programs(0) - 1)
    def _():
        wg_ref[...] = wg_acc[...]
        bg_ref[...] = bg_acc[...]


def forward(weight_mat, bias, patches, cot, rows, pairs):
    taps, lanes = patches.shape
    chan_out = weight_mat.shape[0]
    half = rows // 2
    z = jnp.arange(rows)
    k = jnp.arange(rows)
    pool = jnp.stack(
        [(k[None, :] == z[:, None] // 2), (k[None, :] == half + z[:, None] // 2)]
    ).astype(jnp.float32)
    spread = jnp.stack(
        [(z[None, :] // 2 == k[:, None]), (z[None, :] // 2 + half == k[:, None])]
    ).astype(jnp.bfloat16)
    full = lambda shape: pl.BlockSpec(shape, lambda p: (0,) * len(shape))
    return pl.pallas_call(
        lambda *refs: forward_kernel(rows, *refs),
        grid=(pairs,),
        out_shape=(
            jax.ShapeDtypeStruct(cot.shape, jnp.bfloat16),
            jax.ShapeDtypeStruct((chan_out, lanes), jnp.bfloat16),
            jax.ShapeDtypeStruct((chan_out, taps), jnp.float32),
            jax.ShapeDtypeStruct((chan_out, 1), jnp.float32),
        ),
        in_specs=[
            full((chan_out, taps)),
            full((chan_out, 1)),
            full((2, rows, rows)),
            full((2, rows, rows)),
            pl.BlockSpec((taps, lanes // pairs), lambda p: (0, p)),
            pl.BlockSpec((chan_out, cot.shape[1] // pairs), lambda p: (0, p)),
        ],
        out_specs=(
            pl.BlockSpec((chan_out, cot.shape[1] // pairs), lambda p: (0, p)),
            pl.BlockSpec((chan_out, lanes // pairs), lambda p: (0, p)),
            full((chan_out, taps)),
            full((chan_out, 1)),
        ),
        scratch_shapes=[
            pltpu.VMEM((chan_out, taps), jnp.float32),
            pltpu.VMEM((chan_out, 1), jnp.float32),
        ],
    )(weight_mat, bias, pool, spread, patches, cot)


def on_device(cells, weight, bias, cotangent):
    chan_in, cells_x, cells_y, cells_z = cells.shape
    chan_out = weight.shape[0]
    stencil = [
        (shift_a, shift_b, shift_e)
        for shift_a in range(3)
        for shift_b in range(3)
        for shift_e in range(3)
    ]
    widened = extended(cells, (("gx", 1), ("gy", 2), ("gz", 3)), 1)
    patches = jnp.stack(
        [
            widened[:, sa : sa + cells_x, sb : sb + cells_y, se : se + cells_z]
            for sa, sb, se in stencil
        ],
        axis=1,
    )
    patches = patches.reshape(chan_in * 27, cells_x * cells_y * cells_z)
    weight_mat = weight.reshape(chan_out, chan_in * 27)
    cot = cotangent.reshape(chan_out, -1)
    pooled, delta, weight_local, bias_local = forward(
        weight_mat, bias.reshape(chan_out, 1), patches, cot, cells_z, cells_x // 2
    )
    pooled = pooled.reshape(cotangent.shape)
    delta = delta.reshape(chan_out, cells_x, cells_y, cells_z)
    taps = chan_in * 27
    width = -(-(taps + 1) // 128) * 128
    partial = jnp.concatenate(
        [weight_local, bias_local, jnp.zeros((chan_out, width - taps - 1), jnp.float32)],
        axis=1,
    )
    sizes = tuple(lax.axis_size(a) for a in AXES)
    both = allreduce(partial, sizes)
    weight_grad = both[:, :taps].reshape(chan_out, chan_in, 3, 3, 3)
    bias_grad = both[:, taps]
    delta_wide = extended(delta, (("gx", 1), ("gy", 2), ("gz", 3)), 1)
    input_grad = jnp.zeros((chan_in, cells_x, cells_y, cells_z), jnp.float32)
    for sa, sb, se in stencil:
        window = delta_wide[:, sa : sa + cells_x, sb : sb + cells_y, se : se + cells_z]
        input_grad = input_grad + jnp.einsum(
            "oc,oxyz->cxyz",
            weight[:, :, 2 - sa, 2 - sb, 2 - se],
            window,
            preferred_element_type=jnp.float32,
        )
    return (pooled, weight_grad, bias_grad, input_grad)


def solution(mesh):
    in_specs = (P(None, "gx", "gy", "gz"), P(), P(), P(None, "gx", "gy", "gz"))
    out_specs = (P(None, "gx", "gy", "gz"), P(), P(), P(None, "gx", "gy", "gz"))
    return jax.shard_map(
        on_device, mesh=mesh, in_specs=in_specs, out_specs=out_specs, check_vma=False
    )
```

```python
import jax
import jax.numpy as jnp
from jax import lax
from jax.experimental import pallas as pl
from jax.experimental.pallas import tpu as pltpu
from jax.sharding import PartitionSpec as P

MESH = pl.DeviceIdType.MESH
AXES = ("gx", "gy", "gz")

leak_slope = 0.3
soft_scale = 10.0


def extended(cells, sides, width):
    for axis, dim in sides:
        count = lax.axis_size(axis)
        head = lax.slice_in_dim(cells, 0, width, axis=dim)
        tail = lax.slice_in_dim(cells, cells.shape[dim] - width, cells.shape[dim], axis=dim)
        cells = jnp.concatenate(
            [
                lax.ppermute(tail, axis, [(i, (i + 1) % count) for i in range(count)]),
                cells,
                lax.ppermute(head, axis, [((i + 1) % count, i) for i in range(count)]),
            ],
            axis=dim,
        )
    return cells


def allreduce_kernel(sizes, x_ref, o_ref, slots_x, slots_y, slots_z, acc_x, acc_y,
                     send_x, recv_x, send_y, recv_y, send_z, recv_z):
    me = tuple(lax.axis_index(a) for a in AXES)
    slots = (slots_x, slots_y, slots_z)
    sends = (send_x, send_y, send_z)
    recvs = (recv_x, recv_y, recv_z)
    sources = (x_ref, acc_x, acc_y)
    sinks = (acc_x, acc_y, o_ref)

    def peer(axis, index):
        return tuple(index if k == axis else me[k] for k in range(3))

    barrier = pltpu.get_barrier_semaphore()
    count = 0
    for axis, n in enumerate(sizes):
        for d in range(1, n):
            target = lax.rem(me[axis] + d, n)
            pl.semaphore_signal(barrier, inc=1, device_id=peer(axis, target), device_id_type=MESH)
            count += 1
    pl.semaphore_wait(barrier, count)

    for axis, n in enumerate(sizes):
        src, held, sink = sources[axis], slots[axis], sinks[axis]
        mine = me[axis]
        copies = []
        for d in range(1, n):
            target = lax.rem(mine + d, n)
            copy = pltpu.make_async_remote_copy(
                src_ref=src,
                dst_ref=held.at[mine],
                send_sem=sends[axis].at[d],
                recv_sem=recvs[axis].at[mine],
                device_id=peer(axis, target),
                device_id_type=MESH,
            )
            copy.start()
            copies.append(copy)
        held[mine] = src[...]
        for d in range(1, n):
            origin = lax.rem(mine + n - d, n)
            incoming = pltpu.make_async_remote_copy(
                src_ref=src,
                dst_ref=held.at[origin],
                send_sem=sends[axis].at[d],
                recv_sem=recvs[axis].at[origin],
                device_id=peer(axis, origin),
                device_id_type=MESH,
            )
            incoming.wait_recv()
        for copy in copies:
            copy.wait_send()
        total = held[0]
        for k in range(1, n):
            total = total + held[k]
        sink[...] = total


def allreduce(x, sizes):
    shape = x.shape
    return pl.pallas_call(
        lambda *refs: allreduce_kernel(sizes, *refs),
        out_shape=jax.ShapeDtypeStruct(shape, jnp.float32),
        in_specs=[pl.BlockSpec(memory_space=pltpu.VMEM)],
        out_specs=pl.BlockSpec(memory_space=pltpu.VMEM),
        scratch_shapes=[
            pltpu.VMEM((sizes[0],) + shape, jnp.float32),
            pltpu.VMEM((sizes[1],) + shape, jnp.float32),
            pltpu.VMEM((sizes[2],) + shape, jnp.float32),
            pltpu.VMEM(shape, jnp.float32),
            pltpu.VMEM(shape, jnp.float32),
            pltpu.SemaphoreType.DMA((sizes[0],)),
            pltpu.SemaphoreType.DMA((sizes[0],)),
            pltpu.SemaphoreType.DMA((sizes[1],)),
            pltpu.SemaphoreType.DMA((sizes[1],)),
            pltpu.SemaphoreType.DMA((sizes[2],)),
            pltpu.SemaphoreType.DMA((sizes[2],)),
        ],
        compiler_params=pltpu.CompilerParams(collective_id=0, has_side_effects=True),
    )(x)


def activate(preact):
    return leak_slope * preact + (1.0 - leak_slope) / soft_scale * jax.nn.softplus(
        soft_scale * preact
    )


def slope_of(preact):
    return leak_slope + (1.0 - leak_slope) * jax.nn.sigmoid(soft_scale * preact)


def forward_kernel(rows, w_ref, b_ref, q_ref, u_ref, p_ref, cot_ref,
                   pooled_ref, delta_ref, wg_ref, bg_ref, wg_acc, bg_acc):
    step = pl.program_id(0)
    plane = p_ref.shape[0] // 2

    @pl.when(step == 0)
    def _():
        wg_acc[...] = jnp.zeros_like(wg_acc)
        bg_acc[...] = jnp.zeros_like(bg_acc)

    weight = w_ref[...]
    bias = b_ref[...]

    @pl.loop(0, plane // 4)
    def _(j):
        cot = cot_ref[:, pl.ds(pl.multiple_of(j * rows, rows), rows)]
        ups = (
            jnp.dot(cot, u_ref[0], preferred_element_type=jnp.float32) * 0.125,
            jnp.dot(cot, u_ref[1], preferred_element_type=jnp.float32) * 0.125,
        )
        totals = [None, None]
        wg = None
        bg = None
        for base in (0, plane):
            for r in range(4):
                row = base + j * 4 + r
                patch = p_ref[row]
                preact = jnp.dot(weight, patch, preferred_element_type=jnp.float32) + bias
                scaled = soft_scale * preact
                e = jnp.exp(-jnp.abs(scaled))
                softplus = jnp.maximum(scaled, 0.0) + jnp.log1p(e)
                activated = leak_slope * preact + (1.0 - leak_slope) / soft_scale * softplus
                half = r // 2
                totals[half] = activated if totals[half] is None else totals[half] + activated
                sigmoid = jnp.where(scaled >= 0.0, 1.0, e) / (1.0 + e)
                slope = leak_slope + (1.0 - leak_slope) * sigmoid
                delta = (slope * ups[half]).astype(jnp.bfloat16)
                delta_ref[row] = delta
                term = lax.dot_general(
                    delta, patch, (((1,), (1,)), ((), ())), preferred_element_type=jnp.float32
                )
                wg = term if wg is None else wg + term
                part = delta.astype(jnp.float32)
                bg = part if bg is None else bg + part
        wg_acc[...] += wg
        bg_acc[...] += jnp.sum(bg, axis=1, keepdims=True)
        pooled = jnp.dot(
            totals[0], q_ref[0], preferred_element_type=jnp.float32, precision=lax.Precision.HIGHEST
        ) + jnp.dot(
            totals[1], q_ref[1], preferred_element_type=jnp.float32, precision=lax.Precision.HIGHEST
        )
        pooled_ref[:, pl.ds(pl.multiple_of(j * rows, rows), rows)] = (pooled * 0.125).astype(
            pooled_ref.dtype
        )

    @pl.when(step == pl.num_programs(0) - 1)
    def _():
        wg_ref[...] = wg_acc[...]
        bg_ref[...] = bg_acc[...]


def forward(weight_mat, bias, patches, cot, pairs):
    lines, taps, rows = patches.shape
    chan_out = weight_mat.shape[0]
    half = rows // 2
    z = jnp.arange(rows)
    k = jnp.arange(rows)
    pool = jnp.stack(
        [(k[None, :] == z[:, None] // 2), (k[None, :] == half + z[:, None] // 2)]
    ).astype(jnp.float32)
    spread = jnp.stack(
        [(z[None, :] // 2 == k[:, None]), (z[None, :] // 2 + half == k[:, None])]
    ).astype(jnp.bfloat16)
    full = lambda shape: pl.BlockSpec(shape, lambda p: (0,) * len(shape))
    block = lines // pairs
    return pl.pallas_call(
        lambda *refs: forward_kernel(rows, *refs),
        grid=(pairs,),
        out_shape=(
            jax.ShapeDtypeStruct(cot.shape, jnp.bfloat16),
            jax.ShapeDtypeStruct((lines, chan_out, rows), jnp.bfloat16),
            jax.ShapeDtypeStruct((chan_out, taps), jnp.float32),
            jax.ShapeDtypeStruct((chan_out, 1), jnp.float32),
        ),
        in_specs=[
            full((chan_out, taps)),
            full((chan_out, 1)),
            full((2, rows, rows)),
            full((2, rows, rows)),
            pl.BlockSpec((block, taps, rows), lambda p: (p, 0, 0)),
            pl.BlockSpec((chan_out, cot.shape[1] // pairs), lambda p: (0, p)),
        ],
        out_specs=(
            pl.BlockSpec((chan_out, cot.shape[1] // pairs), lambda p: (0, p)),
            pl.BlockSpec((block, chan_out, rows), lambda p: (p, 0, 0)),
            full((chan_out, taps)),
            full((chan_out, 1)),
        ),
        scratch_shapes=[
            pltpu.VMEM((chan_out, taps), jnp.float32),
            pltpu.VMEM((chan_out, 1), jnp.float32),
        ],
    )(weight_mat, bias, pool, spread, patches, cot)


def on_device(cells, weight, bias, cotangent):
    chan_in, cells_x, cells_y, cells_z = cells.shape
    chan_out = weight.shape[0]
    stencil = [
        (shift_a, shift_b, shift_e)
        for shift_a in range(3)
        for shift_b in range(3)
        for shift_e in range(3)
    ]
    widened = extended(cells, (("gx", 1), ("gy", 2), ("gz", 3)), 1)
    patches = jnp.stack(
        [
            jnp.transpose(
                widened[:, sa : sa + cells_x, sb : sb + cells_y, se : se + cells_z], (1, 2, 0, 3)
            )
            for sa, sb, se in stencil
        ],
        axis=3,
    )
    patches = patches.reshape(cells_x * cells_y, chan_in * 27, cells_z)
    weight_mat = weight.reshape(chan_out, chan_in * 27)
    cot = cotangent.reshape(chan_out, -1)
    pooled, delta, weight_local, bias_local = forward(
        weight_mat, bias.reshape(chan_out, 1), patches, cot, cells_x // 2
    )
    pooled = pooled.reshape(cotangent.shape)
    delta = jnp.transpose(delta.reshape(cells_x, cells_y, chan_out, cells_z), (2, 0, 1, 3))
    taps = chan_in * 27
    width = -(-(taps + 1) // 128) * 128
    partial = jnp.concatenate(
        [weight_local, bias_local, jnp.zeros((chan_out, width - taps - 1), jnp.float32)],
        axis=1,
    )
    sizes = tuple(lax.axis_size(a) for a in AXES)
    both = allreduce(partial, sizes)
    weight_grad = both[:, :taps].reshape(chan_out, chan_in, 3, 3, 3)
    bias_grad = both[:, taps]
    delta_wide = extended(delta, (("gx", 1), ("gy", 2), ("gz", 3)), 1)
    input_grad = jnp.zeros((chan_in, cells_x, cells_y, cells_z), jnp.float32)
    for sa, sb, se in stencil:
        window = delta_wide[:, sa : sa + cells_x, sb : sb + cells_y, se : se + cells_z]
        input_grad = input_grad + jnp.einsum(
            "oc,oxyz->cxyz",
            weight[:, :, 2 - sa, 2 - sb, 2 - se],
            window,
            preferred_element_type=jnp.float32,
        )
    return (pooled, weight_grad, bias_grad, input_grad)


def solution(mesh):
    in_specs = (P(None, "gx", "gy", "gz"), P(), P(), P(None, "gx", "gy", "gz"))
    out_specs = (P(None, "gx", "gy", "gz"), P(), P(), P(None, "gx", "gy", "gz"))
    return jax.shard_map(
        on_device, mesh=mesh, in_specs=in_specs, out_specs=out_specs, check_vma=False
    )
```

```python
import jax
import jax.numpy as jnp
from jax import lax
from jax.experimental import pallas as pl
from jax.experimental.pallas import tpu as pltpu
from jax.sharding import PartitionSpec as P

MESH = pl.DeviceIdType.MESH
AXES = ("gx", "gy", "gz")

leak_slope = 0.3
soft_scale = 10.0


def extended(cells, sides, width):
    for axis, dim in sides:
        count = lax.axis_size(axis)
        head = lax.slice_in_dim(cells, 0, width, axis=dim)
        tail = lax.slice_in_dim(cells, cells.shape[dim] - width, cells.shape[dim], axis=dim)
        cells = jnp.concatenate(
            [
                lax.ppermute(tail, axis, [(i, (i + 1) % count) for i in range(count)]),
                cells,
                lax.ppermute(head, axis, [((i + 1) % count, i) for i in range(count)]),
            ],
            axis=dim,
        )
    return cells


def allreduce_kernel(sizes, x_ref, o_ref, slots_x, slots_y, slots_z, acc_x, acc_y,
                     send_x, recv_x, send_y, recv_y, send_z, recv_z):
    me = tuple(lax.axis_index(a) for a in AXES)
    slots = (slots_x, slots_y, slots_z)
    sends = (send_x, send_y, send_z)
    recvs = (recv_x, recv_y, recv_z)
    sources = (x_ref, acc_x, acc_y)
    sinks = (acc_x, acc_y, o_ref)

    def peer(axis, index):
        return tuple(index if k == axis else me[k] for k in range(3))

    barrier = pltpu.get_barrier_semaphore()
    count = 0
    for axis, n in enumerate(sizes):
        for d in range(1, n):
            target = lax.rem(me[axis] + d, n)
            pl.semaphore_signal(barrier, inc=1, device_id=peer(axis, target), device_id_type=MESH)
            count += 1
    pl.semaphore_wait(barrier, count)

    for axis, n in enumerate(sizes):
        src, held, sink = sources[axis], slots[axis], sinks[axis]
        mine = me[axis]
        copies = []
        for d in range(1, n):
            target = lax.rem(mine + d, n)
            copy = pltpu.make_async_remote_copy(
                src_ref=src,
                dst_ref=held.at[mine],
                send_sem=sends[axis].at[d],
                recv_sem=recvs[axis].at[mine],
                device_id=peer(axis, target),
                device_id_type=MESH,
            )
            copy.start()
            copies.append(copy)
        held[mine] = src[...]
        for d in range(1, n):
            origin = lax.rem(mine + n - d, n)
            incoming = pltpu.make_async_remote_copy(
                src_ref=src,
                dst_ref=held.at[origin],
                send_sem=sends[axis].at[d],
                recv_sem=recvs[axis].at[origin],
                device_id=peer(axis, origin),
                device_id_type=MESH,
            )
            incoming.wait_recv()
        for copy in copies:
            copy.wait_send()
        total = held[0]
        for k in range(1, n):
            total = total + held[k]
        sink[...] = total


def allreduce(x, sizes):
    shape = x.shape
    return pl.pallas_call(
        lambda *refs: allreduce_kernel(sizes, *refs),
        out_shape=jax.ShapeDtypeStruct(shape, jnp.float32),
        in_specs=[pl.BlockSpec(memory_space=pltpu.VMEM)],
        out_specs=pl.BlockSpec(memory_space=pltpu.VMEM),
        scratch_shapes=[
            pltpu.VMEM((sizes[0],) + shape, jnp.float32),
            pltpu.VMEM((sizes[1],) + shape, jnp.float32),
            pltpu.VMEM((sizes[2],) + shape, jnp.float32),
            pltpu.VMEM(shape, jnp.float32),
            pltpu.VMEM(shape, jnp.float32),
            pltpu.SemaphoreType.DMA((sizes[0],)),
            pltpu.SemaphoreType.DMA((sizes[0],)),
            pltpu.SemaphoreType.DMA((sizes[1],)),
            pltpu.SemaphoreType.DMA((sizes[1],)),
            pltpu.SemaphoreType.DMA((sizes[2],)),
            pltpu.SemaphoreType.DMA((sizes[2],)),
        ],
        compiler_params=pltpu.CompilerParams(collective_id=0, has_side_effects=True),
    )(x)


def activate(preact):
    return leak_slope * preact + (1.0 - leak_slope) / soft_scale * jax.nn.softplus(
        soft_scale * preact
    )


def slope_of(preact):
    return leak_slope + (1.0 - leak_slope) * jax.nn.sigmoid(soft_scale * preact)


def forward_kernel(rows, wide_y, w_ref, b_ref, q_ref, u_ref, wt_ref, p_ref, cot_ref,
                   pooled_ref, wg_ref, bg_ref, main_ref, lo_ref, hi_ref, wg_acc, bg_acc):
    step = pl.program_id(0)
    plane = p_ref.shape[0] // 2
    lines = plane // 4

    @pl.when(step == 0)
    def _():
        wg_acc[...] = jnp.zeros_like(wg_acc)
        bg_acc[...] = jnp.zeros_like(bg_acc)
        main_ref[...] = jnp.zeros_like(main_ref)
        lo_ref[...] = jnp.zeros_like(lo_ref)
        hi_ref[...] = jnp.zeros_like(hi_ref)

    weight = w_ref[...]
    bias = b_ref[...]
    spread_w = wt_ref[...]
    slots = spread_w.shape[0] // 27
    lane = lax.broadcasted_iota(jnp.int32, (slots, rows), 1)
    first = lane == 0
    last = lane == rows - 1

    @pl.loop(0, lines)
    def _(j):
        cot = cot_ref[:, pl.ds(pl.multiple_of(j * rows, rows), rows)]
        ups = (
            jnp.dot(cot, u_ref[0], preferred_element_type=jnp.float32) * 0.125,
            jnp.dot(cot, u_ref[1], preferred_element_type=jnp.float32) * 0.125,
        )
        totals = [None, None]
        wg = None
        bg = None
        for px, base in enumerate((0, plane)):
            deltas = []
            for r in range(4):
                row = base + j * 4 + r
                patch = p_ref[row]
                preact = jnp.dot(weight, patch, preferred_element_type=jnp.float32) + bias
                scaled = soft_scale * preact
                e = jnp.exp(-jnp.abs(scaled))
                softplus = jnp.maximum(scaled, 0.0) + jnp.log1p(e)
                activated = leak_slope * preact + (1.0 - leak_slope) / soft_scale * softplus
                half = r // 2
                totals[half] = activated if totals[half] is None else totals[half] + activated
                sigmoid = jnp.where(scaled >= 0.0, 1.0, e) / (1.0 + e)
                slope = leak_slope + (1.0 - leak_slope) * sigmoid
                delta = (slope * ups[half]).astype(jnp.bfloat16)
                deltas.append(delta)
                term = lax.dot_general(
                    delta, patch, (((1,), (1,)), ((), ())), preferred_element_type=jnp.float32
                )
                wg = term if wg is None else wg + term
                part = delta.astype(jnp.float32)
                bg = part if bg is None else bg + part
            spread = jnp.dot(
                spread_w, jnp.concatenate(deltas, axis=1), preferred_element_type=jnp.float32
            )
            x = step * 2 + px
            for r in range(4):
                y = j * 4 + r
                for a in range(3):
                    for b in range(3):
                        at = (a * 3 + b) * 3 * slots
                        cols = slice(r * rows, (r + 1) * rows)
                        v0 = pltpu.roll(spread[at : at + slots, cols], rows - 1, 1)
                        v1 = spread[at + slots : at + 2 * slots, cols]
                        v2 = pltpu.roll(spread[at + 2 * slots : at + 3 * slots, cols], 1, 1)
                        out = (x + a) * wide_y + (y + b)
                        main_ref[out] += (
                            jnp.where(last, 0.0, v0) + v1 + jnp.where(first, 0.0, v2)
                        )
                        lo_ref[out] += jnp.where(last, v0, 0.0)
                        hi_ref[out] += jnp.where(first, v2, 0.0)
        wg_acc[...] += wg
        bg_acc[...] += jnp.sum(bg, axis=1, keepdims=True)
        pooled = jnp.dot(
            totals[0], q_ref[0], preferred_element_type=jnp.float32, precision=lax.Precision.HIGHEST
        ) + jnp.dot(
            totals[1], q_ref[1], preferred_element_type=jnp.float32, precision=lax.Precision.HIGHEST
        )
        pooled_ref[:, pl.ds(pl.multiple_of(j * rows, rows), rows)] = (pooled * 0.125).astype(
            pooled_ref.dtype
        )

    @pl.when(step == pl.num_programs(0) - 1)
    def _():
        wg_ref[...] = wg_acc[...]
        bg_ref[...] = bg_acc[...]


def forward(weight, bias, patches, cot, pairs, wide_x, wide_y):
    lines, taps, rows = patches.shape
    chan_out, chan_in = weight.shape[:2]
    weight_mat = weight.reshape(chan_out, taps)
    slots = 8
    spread_w = jnp.transpose(weight, (2, 3, 4, 1, 0))
    spread_w = jnp.pad(spread_w, ((0, 0), (0, 0), (0, 0), (0, slots - chan_in), (0, 0)))
    spread_w = spread_w.reshape(27 * slots, chan_out)
    half = rows // 2
    z = jnp.arange(rows)
    k = jnp.arange(rows)
    pool = jnp.stack(
        [(k[None, :] == z[:, None] // 2), (k[None, :] == half + z[:, None] // 2)]
    ).astype(jnp.float32)
    spread = jnp.stack(
        [(z[None, :] // 2 == k[:, None]), (z[None, :] // 2 + half == k[:, None])]
    ).astype(jnp.bfloat16)
    full = lambda shape: pl.BlockSpec(shape, lambda p: (0,) * len(shape))
    block = lines // pairs
    acc_shape = (wide_x * wide_y, slots, rows)
    return pl.pallas_call(
        lambda *refs: forward_kernel(rows, wide_y, *refs),
        grid=(pairs,),
        out_shape=(
            jax.ShapeDtypeStruct(cot.shape, jnp.bfloat16),
            jax.ShapeDtypeStruct((chan_out, taps), jnp.float32),
            jax.ShapeDtypeStruct((chan_out, 1), jnp.float32),
            jax.ShapeDtypeStruct(acc_shape, jnp.float32),
            jax.ShapeDtypeStruct(acc_shape, jnp.float32),
            jax.ShapeDtypeStruct(acc_shape, jnp.float32),
        ),
        in_specs=[
            full((chan_out, taps)),
            full((chan_out, 1)),
            full((2, rows, rows)),
            full((2, rows, rows)),
            full((27 * slots, chan_out)),
            pl.BlockSpec((block, taps, rows), lambda p: (p, 0, 0)),
            pl.BlockSpec((chan_out, cot.shape[1] // pairs), lambda p: (0, p)),
        ],
        out_specs=(
            pl.BlockSpec((chan_out, cot.shape[1] // pairs), lambda p: (0, p)),
            full((chan_out, taps)),
            full((chan_out, 1)),
            full(acc_shape),
            full(acc_shape),
            full(acc_shape),
        ),
        scratch_shapes=[
            pltpu.VMEM((chan_out, taps), jnp.float32),
            pltpu.VMEM((chan_out, 1), jnp.float32),
        ],
    )(weight_mat, bias, pool, spread, spread_w, patches, cot)


def fold_halo(main, axis, dim, width):
    count = lax.axis_size(axis)
    size = main.shape[dim]
    head = lax.slice_in_dim(main, 0, width, axis=dim)
    tail = lax.slice_in_dim(main, size - width, size, axis=dim)
    from_left = lax.ppermute(tail, axis, [(i, (i + 1) % count) for i in range(count)])
    from_right = lax.ppermute(head, axis, [((i + 1) % count, i) for i in range(count)])
    inner = lax.slice_in_dim(main, width, size - width, axis=dim)
    inner_size = size - 2 * width
    start = [0] * main.ndim
    inner = lax.dynamic_update_slice(
        inner, lax.slice_in_dim(inner, 0, width, axis=dim) + from_left, start
    )
    start[dim] = inner_size - width
    inner = lax.dynamic_update_slice(
        inner, lax.slice_in_dim(inner, inner_size - width, inner_size, axis=dim) + from_right, start
    )
    return inner


def on_device(cells, weight, bias, cotangent):
    chan_in, cells_x, cells_y, cells_z = cells.shape
    chan_out = weight.shape[0]
    stencil = [
        (shift_a, shift_b, shift_e)
        for shift_a in range(3)
        for shift_b in range(3)
        for shift_e in range(3)
    ]
    widened = extended(cells, (("gx", 1), ("gy", 2), ("gz", 3)), 1)
    patches = jnp.stack(
        [
            jnp.transpose(
                widened[:, sa : sa + cells_x, sb : sb + cells_y, se : se + cells_z], (1, 2, 0, 3)
            )
            for sa, sb, se in stencil
        ],
        axis=3,
    )
    patches = patches.reshape(cells_x * cells_y, chan_in * 27, cells_z)
    cot = cotangent.reshape(chan_out, -1)
    wide_x, wide_y = cells_x + 2, cells_y + 2
    pooled, weight_local, bias_local, main, lo, hi = forward(
        weight, bias.reshape(chan_out, 1), patches, cot, cells_x // 2, wide_x, wide_y
    )
    pooled = pooled.reshape(cotangent.shape)
    taps = chan_in * 27
    width = -(-(taps + 1) // 128) * 128
    partial = jnp.concatenate(
        [weight_local, bias_local, jnp.zeros((chan_out, width - taps - 1), jnp.float32)],
        axis=1,
    )
    sizes = tuple(lax.axis_size(a) for a in AXES)
    both = allreduce(partial, sizes)
    weight_grad = both[:, :taps].reshape(chan_out, chan_in, 3, 3, 3)
    bias_grad = both[:, taps]
    main = main.reshape(wide_x, wide_y, -1, cells_z)[:, :, :chan_in]
    lo = lo.reshape(wide_x, wide_y, -1, cells_z)[:, :, :chan_in, cells_z - 1 :]
    hi = hi.reshape(wide_x, wide_y, -1, cells_z)[:, :, :chan_in, :1]
    count = lax.axis_size("gz")
    from_left = lax.ppermute(hi, "gz", [(i, (i + 1) % count) for i in range(count)])
    from_right = lax.ppermute(lo, "gz", [((i + 1) % count, i) for i in range(count)])
    main = jnp.concatenate(
        [
            main[..., :1] + from_left,
            main[..., 1 : cells_z - 1],
            main[..., cells_z - 1 :] + from_right,
        ],
        axis=3,
    )
    main = fold_halo(main, "gy", 1, 1)
    main = fold_halo(main, "gx", 0, 1)
    input_grad = jnp.transpose(main, (2, 0, 1, 3))
    return (pooled, weight_grad, bias_grad, input_grad)


def solution(mesh):
    in_specs = (P(None, "gx", "gy", "gz"), P(), P(), P(None, "gx", "gy", "gz"))
    out_specs = (P(None, "gx", "gy", "gz"), P(), P(), P(None, "gx", "gy", "gz"))
    return jax.shard_map(
        on_device, mesh=mesh, in_specs=in_specs, out_specs=out_specs, check_vma=False
    )
```

```python
import jax
import jax.numpy as jnp
from jax import lax
from jax.experimental import pallas as pl
from jax.experimental.pallas import tpu as pltpu
from jax.sharding import PartitionSpec as P

MESH = pl.DeviceIdType.MESH
AXES = ("gx", "gy", "gz")

leak_slope = 0.3
soft_scale = 10.0


def extended(cells, sides, width):
    for axis, dim in sides:
        count = lax.axis_size(axis)
        head = lax.slice_in_dim(cells, 0, width, axis=dim)
        tail = lax.slice_in_dim(cells, cells.shape[dim] - width, cells.shape[dim], axis=dim)
        cells = jnp.concatenate(
            [
                lax.ppermute(tail, axis, [(i, (i + 1) % count) for i in range(count)]),
                cells,
                lax.ppermute(head, axis, [((i + 1) % count, i) for i in range(count)]),
            ],
            axis=dim,
        )
    return cells


def allreduce_kernel(sizes, x_ref, o_ref, slots_x, slots_y, slots_z, acc_x, acc_y,
                     send_x, recv_x, send_y, recv_y, send_z, recv_z):
    me = tuple(lax.axis_index(a) for a in AXES)
    slots = (slots_x, slots_y, slots_z)
    sends = (send_x, send_y, send_z)
    recvs = (recv_x, recv_y, recv_z)
    sources = (x_ref, acc_x, acc_y)
    sinks = (acc_x, acc_y, o_ref)

    def peer(axis, index):
        return tuple(index if k == axis else me[k] for k in range(3))

    barrier = pltpu.get_barrier_semaphore()
    count = 0
    for axis, n in enumerate(sizes):
        for d in range(1, n):
            target = lax.rem(me[axis] + d, n)
            pl.semaphore_signal(barrier, inc=1, device_id=peer(axis, target), device_id_type=MESH)
            count += 1
    pl.semaphore_wait(barrier, count)

    for axis, n in enumerate(sizes):
        src, held, sink = sources[axis], slots[axis], sinks[axis]
        mine = me[axis]
        copies = []
        for d in range(1, n):
            target = lax.rem(mine + d, n)
            copy = pltpu.make_async_remote_copy(
                src_ref=src,
                dst_ref=held.at[mine],
                send_sem=sends[axis].at[d],
                recv_sem=recvs[axis].at[mine],
                device_id=peer(axis, target),
                device_id_type=MESH,
            )
            copy.start()
            copies.append(copy)
        held[mine] = src[...]
        for d in range(1, n):
            origin = lax.rem(mine + n - d, n)
            incoming = pltpu.make_async_remote_copy(
                src_ref=src,
                dst_ref=held.at[origin],
                send_sem=sends[axis].at[d],
                recv_sem=recvs[axis].at[origin],
                device_id=peer(axis, origin),
                device_id_type=MESH,
            )
            incoming.wait_recv()
        for copy in copies:
            copy.wait_send()
        total = held[0]
        for k in range(1, n):
            total = total + held[k]
        sink[...] = total


def allreduce(x, sizes):
    shape = x.shape
    return pl.pallas_call(
        lambda *refs: allreduce_kernel(sizes, *refs),
        out_shape=jax.ShapeDtypeStruct(shape, jnp.float32),
        in_specs=[pl.BlockSpec(memory_space=pltpu.VMEM)],
        out_specs=pl.BlockSpec(memory_space=pltpu.VMEM),
        scratch_shapes=[
            pltpu.VMEM((sizes[0],) + shape, jnp.float32),
            pltpu.VMEM((sizes[1],) + shape, jnp.float32),
            pltpu.VMEM((sizes[2],) + shape, jnp.float32),
            pltpu.VMEM(shape, jnp.float32),
            pltpu.VMEM(shape, jnp.float32),
            pltpu.SemaphoreType.DMA((sizes[0],)),
            pltpu.SemaphoreType.DMA((sizes[0],)),
            pltpu.SemaphoreType.DMA((sizes[1],)),
            pltpu.SemaphoreType.DMA((sizes[1],)),
            pltpu.SemaphoreType.DMA((sizes[2],)),
            pltpu.SemaphoreType.DMA((sizes[2],)),
        ],
        compiler_params=pltpu.CompilerParams(collective_id=0, has_side_effects=True),
    )(x)


def activate(preact):
    return leak_slope * preact + (1.0 - leak_slope) / soft_scale * jax.nn.softplus(
        soft_scale * preact
    )


def slope_of(preact):
    return leak_slope + (1.0 - leak_slope) * jax.nn.sigmoid(soft_scale * preact)


def forward_kernel(rows, wide_y, w_ref, b_ref, q_ref, u_ref, wt_ref, p_ref, cot_ref,
                   pooled_ref, wg_ref, bg_ref, main_ref, edge_ref, wg_acc, bg_acc):
    step = pl.program_id(0)
    plane = p_ref.shape[0] // 2
    lines = plane // 4

    @pl.when(step == 0)
    def _():
        wg_acc[...] = jnp.zeros_like(wg_acc)
        bg_acc[...] = jnp.zeros_like(bg_acc)
        main_ref[...] = jnp.zeros_like(main_ref)
        edge_ref[...] = jnp.zeros_like(edge_ref)

    weight = w_ref[...]
    bias = b_ref[...]
    spread_w = wt_ref[...]
    slots = spread_w.shape[0] // 27
    lane = lax.broadcasted_iota(jnp.int32, (slots, rows), 1)
    first = lane == 0
    last = lane == rows - 1

    @pl.loop(0, lines)
    def _(j):
        cot = cot_ref[:, pl.ds(pl.multiple_of(j * rows, rows), rows)]
        ups = (
            jnp.dot(cot, u_ref[0], preferred_element_type=jnp.float32) * 0.125,
            jnp.dot(cot, u_ref[1], preferred_element_type=jnp.float32) * 0.125,
        )
        totals = [None, None]
        wg = None
        bg = None
        spreads = []
        for px, base in enumerate((0, plane)):
            deltas = []
            for r in range(4):
                row = base + j * 4 + r
                patch = p_ref[row]
                preact = jnp.dot(weight, patch, preferred_element_type=jnp.float32) + bias
                scaled = soft_scale * preact
                e = jnp.exp(-jnp.abs(scaled))
                softplus = jnp.maximum(scaled, 0.0) + jnp.log1p(e)
                activated = leak_slope * preact + (1.0 - leak_slope) / soft_scale * softplus
                half = r // 2
                totals[half] = activated if totals[half] is None else totals[half] + activated
                sigmoid = jnp.where(scaled >= 0.0, 1.0, e) / (1.0 + e)
                slope = leak_slope + (1.0 - leak_slope) * sigmoid
                delta = (slope * ups[half]).astype(jnp.bfloat16)
                deltas.append(delta)
                term = lax.dot_general(
                    delta, patch, (((1,), (1,)), ((), ())), preferred_element_type=jnp.float32
                )
                wg = term if wg is None else wg + term
                part = delta.astype(jnp.float32)
                bg = part if bg is None else bg + part
            spreads.append(
                jnp.dot(
                    spread_w, jnp.concatenate(deltas, axis=1), preferred_element_type=jnp.float32
                )
            )
        acc_main = {}
        acc_edge = {}
        for px in range(2):
            for r in range(4):
                cols = slice(r * rows, (r + 1) * rows)
                for a in range(3):
                    for b in range(3):
                        at = (a * 3 + b) * 3 * slots
                        g = spreads[px]
                        v0 = pltpu.roll(g[at : at + slots, cols], rows - 1, 1)
                        v1 = g[at + slots : at + 2 * slots, cols]
                        v2 = pltpu.roll(g[at + 2 * slots : at + 3 * slots, cols], 1, 1)
                        inner = jnp.where(last, 0.0, v0) + v1 + jnp.where(first, 0.0, v2)
                        edge = jnp.where(last, v0, 0.0) + jnp.where(first, v2, 0.0)
                        key = (px + a, r + b)
                        if key in acc_main:
                            acc_main[key] = acc_main[key] + inner
                            acc_edge[key] = acc_edge[key] + edge
                        else:
                            acc_main[key] = inner
                            acc_edge[key] = edge
        for (dx, dy), value in acc_main.items():
            out = (step * 2 + dx) * wide_y + (j * 4 + dy)
            main_ref[out] += value[: main_ref.shape[1]]
            edge_ref[out] += acc_edge[dx, dy][: edge_ref.shape[1]]
        wg_acc[...] += wg
        bg_acc[...] += jnp.sum(bg, axis=1, keepdims=True)
        pooled = jnp.dot(
            totals[0], q_ref[0], preferred_element_type=jnp.float32, precision=lax.Precision.HIGHEST
        ) + jnp.dot(
            totals[1], q_ref[1], preferred_element_type=jnp.float32, precision=lax.Precision.HIGHEST
        )
        pooled_ref[:, pl.ds(pl.multiple_of(j * rows, rows), rows)] = (pooled * 0.125).astype(
            pooled_ref.dtype
        )

    @pl.when(step == pl.num_programs(0) - 1)
    def _():
        wg_ref[...] = wg_acc[...]
        bg_ref[...] = bg_acc[...]


def forward(weight, bias, patches, cot, pairs, wide_x, wide_y):
    lines, taps, rows = patches.shape
    chan_out, chan_in = weight.shape[:2]
    weight_mat = weight.reshape(chan_out, taps)
    slots = 8
    spread_w = jnp.transpose(weight, (2, 3, 4, 1, 0))
    spread_w = jnp.pad(spread_w, ((0, 0), (0, 0), (0, 0), (0, slots - chan_in), (0, 0)))
    spread_w = spread_w.reshape(27 * slots, chan_out)
    half = rows // 2
    z = jnp.arange(rows)
    k = jnp.arange(rows)
    pool = jnp.stack(
        [(k[None, :] == z[:, None] // 2), (k[None, :] == half + z[:, None] // 2)]
    ).astype(jnp.float32)
    spread = jnp.stack(
        [(z[None, :] // 2 == k[:, None]), (z[None, :] // 2 + half == k[:, None])]
    ).astype(jnp.bfloat16)
    full = lambda shape: pl.BlockSpec(shape, lambda p: (0,) * len(shape))
    block = lines // pairs
    acc_shape = (wide_x * wide_y, chan_in, rows)
    return pl.pallas_call(
        lambda *refs: forward_kernel(rows, wide_y, *refs),
        grid=(pairs,),
        out_shape=(
            jax.ShapeDtypeStruct(cot.shape, jnp.bfloat16),
            jax.ShapeDtypeStruct((chan_out, taps), jnp.float32),
            jax.ShapeDtypeStruct((chan_out, 1), jnp.float32),
            jax.ShapeDtypeStruct(acc_shape, jnp.float32),
            jax.ShapeDtypeStruct(acc_shape, jnp.float32),
        ),
        in_specs=[
            full((chan_out, taps)),
            full((chan_out, 1)),
            full((2, rows, rows)),
            full((2, rows, rows)),
            full((27 * slots, chan_out)),
            pl.BlockSpec((block, taps, rows), lambda p: (p, 0, 0)),
            pl.BlockSpec((chan_out, cot.shape[1] // pairs), lambda p: (0, p)),
        ],
        out_specs=(
            pl.BlockSpec((chan_out, cot.shape[1] // pairs), lambda p: (0, p)),
            full((chan_out, taps)),
            full((chan_out, 1)),
            full(acc_shape),
            full(acc_shape),
        ),
        scratch_shapes=[
            pltpu.VMEM((chan_out, taps), jnp.float32),
            pltpu.VMEM((chan_out, 1), jnp.float32),
        ],
    )(weight_mat, bias, pool, spread, spread_w, patches, cot)


def fold_halo(main, axis, dim, width):
    count = lax.axis_size(axis)
    size = main.shape[dim]
    head = lax.slice_in_dim(main, 0, width, axis=dim)
    tail = lax.slice_in_dim(main, size - width, size, axis=dim)
    from_left = lax.ppermute(tail, axis, [(i, (i + 1) % count) for i in range(count)])
    from_right = lax.ppermute(head, axis, [((i + 1) % count, i) for i in range(count)])
    inner = lax.slice_in_dim(main, width, size - width, axis=dim)
    inner_size = size - 2 * width
    start = [0] * main.ndim
    inner = lax.dynamic_update_slice(
        inner, lax.slice_in_dim(inner, 0, width, axis=dim) + from_left, start
    )
    start[dim] = inner_size - width
    inner = lax.dynamic_update_slice(
        inner, lax.slice_in_dim(inner, inner_size - width, inner_size, axis=dim) + from_right, start
    )
    return inner


def on_device(cells, weight, bias, cotangent):
    chan_in, cells_x, cells_y, cells_z = cells.shape
    chan_out = weight.shape[0]
    stencil = [
        (shift_a, shift_b, shift_e)
        for shift_a in range(3)
        for shift_b in range(3)
        for shift_e in range(3)
    ]
    widened = extended(cells, (("gx", 1), ("gy", 2), ("gz", 3)), 1)
    patches = jnp.stack(
        [
            jnp.transpose(
                widened[:, sa : sa + cells_x, sb : sb + cells_y, se : se + cells_z], (1, 2, 0, 3)
            )
            for sa, sb, se in stencil
        ],
        axis=3,
    )
    patches = patches.reshape(cells_x * cells_y, chan_in * 27, cells_z)
    cot = cotangent.reshape(chan_out, -1)
    wide_x, wide_y = cells_x + 2, cells_y + 2
    pooled, weight_local, bias_local, main, edge = forward(
        weight, bias.reshape(chan_out, 1), patches, cot, cells_x // 2, wide_x, wide_y
    )
    pooled = pooled.reshape(cotangent.shape)
    taps = chan_in * 27
    width = -(-(taps + 1) // 128) * 128
    partial = jnp.concatenate(
        [weight_local, bias_local, jnp.zeros((chan_out, width - taps - 1), jnp.float32)],
        axis=1,
    )
    sizes = tuple(lax.axis_size(a) for a in AXES)
    both = allreduce(partial, sizes)
    weight_grad = both[:, :taps].reshape(chan_out, chan_in, 3, 3, 3)
    bias_grad = both[:, taps]
    main = main.reshape(wide_x, wide_y, chan_in, cells_z)
    edge = edge.reshape(wide_x, wide_y, chan_in, cells_z)
    lo = edge[..., cells_z - 1 :]
    hi = edge[..., :1]
    count = lax.axis_size("gz")
    from_left = lax.ppermute(hi, "gz", [(i, (i + 1) % count) for i in range(count)])
    from_right = lax.ppermute(lo, "gz", [((i + 1) % count, i) for i in range(count)])
    main = jnp.concatenate(
        [
            main[..., :1] + from_left,
            main[..., 1 : cells_z - 1],
            main[..., cells_z - 1 :] + from_right,
        ],
        axis=3,
    )
    main = fold_halo(main, "gy", 1, 1)
    main = fold_halo(main, "gx", 0, 1)
    input_grad = jnp.transpose(main, (2, 0, 1, 3))
    return (pooled, weight_grad, bias_grad, input_grad)


def solution(mesh):
    in_specs = (P(None, "gx", "gy", "gz"), P(), P(), P(None, "gx", "gy", "gz"))
    out_specs = (P(None, "gx", "gy", "gz"), P(), P(), P(None, "gx", "gy", "gz"))
    return jax.shard_map(
        on_device, mesh=mesh, in_specs=in_specs, out_specs=out_specs, check_vma=False
    )
```

```python
import jax
import jax.numpy as jnp
from jax import lax
from jax.experimental import pallas as pl
from jax.experimental.pallas import tpu as pltpu
from jax.sharding import PartitionSpec as P

MESH = pl.DeviceIdType.MESH
AXES = ("gx", "gy", "gz")

leak_slope = 0.3
soft_scale = 10.0


def shift(piece, axis, dim, step):
    count = lax.axis_size(axis)
    pairs = [(i, (i + step) % count) for i in range(count)]
    if piece.shape[dim] == 1:
        moved = lax.ppermute(jnp.squeeze(piece, dim), axis, pairs)
        return jnp.expand_dims(moved, dim)
    return lax.ppermute(piece, axis, pairs)


def extended(cells, sides, width):
    for axis, dim in sides:
        head = lax.slice_in_dim(cells, 0, width, axis=dim)
        tail = lax.slice_in_dim(cells, cells.shape[dim] - width, cells.shape[dim], axis=dim)
        cells = jnp.concatenate(
            [shift(tail, axis, dim, 1), cells, shift(head, axis, dim, -1)],
            axis=dim,
        )
    return cells


def allreduce_kernel(sizes, x_ref, o_ref, slots_x, slots_y, slots_z, acc_x, acc_y,
                     send_x, recv_x, send_y, recv_y, send_z, recv_z):
    me = tuple(lax.axis_index(a) for a in AXES)
    slots = (slots_x, slots_y, slots_z)
    sends = (send_x, send_y, send_z)
    recvs = (recv_x, recv_y, recv_z)
    sources = (x_ref, acc_x, acc_y)
    sinks = (acc_x, acc_y, o_ref)

    def peer(axis, index):
        return tuple(index if k == axis else me[k] for k in range(3))

    barrier = pltpu.get_barrier_semaphore()
    count = 0
    for axis, n in enumerate(sizes):
        for d in range(1, n):
            target = lax.rem(me[axis] + d, n)
            pl.semaphore_signal(barrier, inc=1, device_id=peer(axis, target), device_id_type=MESH)
            count += 1
    pl.semaphore_wait(barrier, count)

    for axis, n in enumerate(sizes):
        src, held, sink = sources[axis], slots[axis], sinks[axis]
        mine = me[axis]
        copies = []
        for d in range(1, n):
            target = lax.rem(mine + d, n)
            copy = pltpu.make_async_remote_copy(
                src_ref=src,
                dst_ref=held.at[mine],
                send_sem=sends[axis].at[d],
                recv_sem=recvs[axis].at[mine],
                device_id=peer(axis, target),
                device_id_type=MESH,
            )
            copy.start()
            copies.append(copy)
        held[mine] = src[...]
        for d in range(1, n):
            origin = lax.rem(mine + n - d, n)
            incoming = pltpu.make_async_remote_copy(
                src_ref=src,
                dst_ref=held.at[origin],
                send_sem=sends[axis].at[d],
                recv_sem=recvs[axis].at[origin],
                device_id=peer(axis, origin),
                device_id_type=MESH,
            )
            incoming.wait_recv()
        for copy in copies:
            copy.wait_send()
        total = held[0]
        for k in range(1, n):
            total = total + held[k]
        sink[...] = total


def allreduce(x, sizes):
    shape = x.shape
    return pl.pallas_call(
        lambda *refs: allreduce_kernel(sizes, *refs),
        out_shape=jax.ShapeDtypeStruct(shape, jnp.float32),
        in_specs=[pl.BlockSpec(memory_space=pltpu.VMEM)],
        out_specs=pl.BlockSpec(memory_space=pltpu.VMEM),
        scratch_shapes=[
            pltpu.VMEM((sizes[0],) + shape, jnp.float32),
            pltpu.VMEM((sizes[1],) + shape, jnp.float32),
            pltpu.VMEM((sizes[2],) + shape, jnp.float32),
            pltpu.VMEM(shape, jnp.float32),
            pltpu.VMEM(shape, jnp.float32),
            pltpu.SemaphoreType.DMA((sizes[0],)),
            pltpu.SemaphoreType.DMA((sizes[0],)),
            pltpu.SemaphoreType.DMA((sizes[1],)),
            pltpu.SemaphoreType.DMA((sizes[1],)),
            pltpu.SemaphoreType.DMA((sizes[2],)),
            pltpu.SemaphoreType.DMA((sizes[2],)),
        ],
        compiler_params=pltpu.CompilerParams(collective_id=0, has_side_effects=True),
    )(x)


def activate(preact):
    return leak_slope * preact + (1.0 - leak_slope) / soft_scale * jax.nn.softplus(
        soft_scale * preact
    )


def slope_of(preact):
    return leak_slope + (1.0 - leak_slope) * jax.nn.sigmoid(soft_scale * preact)


def forward_kernel(rows, wide_y, w_ref, b_ref, q_ref, u_ref, wt_ref, p_ref, cot_ref,
                   pooled_ref, wg_ref, bg_ref, main_ref, edge_ref, wg_acc, bg_acc):
    step = pl.program_id(0)
    plane = p_ref.shape[0] // 2
    lines = plane // 4

    @pl.when(step == 0)
    def _():
        wg_acc[...] = jnp.zeros_like(wg_acc)
        bg_acc[...] = jnp.zeros_like(bg_acc)
        main_ref[...] = jnp.zeros_like(main_ref)
        edge_ref[...] = jnp.zeros_like(edge_ref)

    weight = w_ref[...]
    bias = b_ref[...]
    spread_w = wt_ref[...]
    slots = spread_w.shape[0] // 27
    lane = lax.broadcasted_iota(jnp.int32, (slots, rows), 1)
    first = lane == 0
    last = lane == rows - 1

    @pl.loop(0, lines)
    def _(j):
        cot = cot_ref[:, pl.ds(pl.multiple_of(j * rows, rows), rows)]
        ups = (
            jnp.dot(cot, u_ref[0], preferred_element_type=jnp.float32) * 0.125,
            jnp.dot(cot, u_ref[1], preferred_element_type=jnp.float32) * 0.125,
        )
        totals = [None, None]
        wg = None
        bg = None
        spreads = []
        for px, base in enumerate((0, plane)):
            deltas = []
            for r in range(4):
                row = base + j * 4 + r
                patch = p_ref[row]
                preact = jnp.dot(weight, patch, preferred_element_type=jnp.float32) + bias
                scaled = soft_scale * preact
                e = jnp.exp(-jnp.abs(scaled))
                softplus = jnp.maximum(scaled, 0.0) + jnp.log1p(e)
                activated = leak_slope * preact + (1.0 - leak_slope) / soft_scale * softplus
                half = r // 2
                totals[half] = activated if totals[half] is None else totals[half] + activated
                sigmoid = jnp.where(scaled >= 0.0, 1.0, e) / (1.0 + e)
                slope = leak_slope + (1.0 - leak_slope) * sigmoid
                delta = (slope * ups[half]).astype(jnp.bfloat16)
                deltas.append(delta)
                term = lax.dot_general(
                    delta, patch, (((1,), (1,)), ((), ())), preferred_element_type=jnp.float32
                )
                wg = term if wg is None else wg + term
                part = delta.astype(jnp.float32)
                bg = part if bg is None else bg + part
            spreads.append(
                jnp.dot(
                    spread_w, jnp.concatenate(deltas, axis=1), preferred_element_type=jnp.float32
                )
            )
        acc_main = {}
        acc_edge = {}
        for px in range(2):
            for r in range(4):
                cols = slice(r * rows, (r + 1) * rows)
                for a in range(3):
                    for b in range(3):
                        at = (a * 3 + b) * 3 * slots
                        g = spreads[px]
                        v0 = pltpu.roll(g[at : at + slots, cols], rows - 1, 1)
                        v1 = g[at + slots : at + 2 * slots, cols]
                        v2 = pltpu.roll(g[at + 2 * slots : at + 3 * slots, cols], 1, 1)
                        inner = jnp.where(last, 0.0, v0) + v1 + jnp.where(first, 0.0, v2)
                        edge = jnp.where(last, v0, 0.0) + jnp.where(first, v2, 0.0)
                        key = (px + a, r + b)
                        if key in acc_main:
                            acc_main[key] = acc_main[key] + inner
                            acc_edge[key] = acc_edge[key] + edge
                        else:
                            acc_main[key] = inner
                            acc_edge[key] = edge
        for (dx, dy), value in acc_main.items():
            out = (step * 2 + dx) * wide_y + (j * 4 + dy)
            main_ref[out] += value[: main_ref.shape[1]]
            edge_ref[out] += acc_edge[dx, dy][: edge_ref.shape[1]]
        wg_acc[...] += wg
        bg_acc[...] += jnp.sum(bg, axis=1, keepdims=True)
        pooled = jnp.dot(
            totals[0], q_ref[0], preferred_element_type=jnp.float32, precision=lax.Precision.HIGHEST
        ) + jnp.dot(
            totals[1], q_ref[1], preferred_element_type=jnp.float32, precision=lax.Precision.HIGHEST
        )
        pooled_ref[:, pl.ds(pl.multiple_of(j * rows, rows), rows)] = (pooled * 0.125).astype(
            pooled_ref.dtype
        )

    @pl.when(step == pl.num_programs(0) - 1)
    def _():
        wg_ref[...] = wg_acc[...]
        bg_ref[...] = bg_acc[...]


def forward(weight, bias, patches, cot, pairs, wide_x, wide_y):
    lines, taps, rows = patches.shape
    chan_out, chan_in = weight.shape[:2]
    weight_mat = weight.reshape(chan_out, taps)
    slots = 8
    spread_w = jnp.transpose(weight, (2, 3, 4, 1, 0))
    spread_w = jnp.pad(spread_w, ((0, 0), (0, 0), (0, 0), (0, slots - chan_in), (0, 0)))
    spread_w = spread_w.reshape(27 * slots, chan_out)
    half = rows // 2
    z = jnp.arange(rows)
    k = jnp.arange(rows)
    pool = jnp.stack(
        [(k[None, :] == z[:, None] // 2), (k[None, :] == half + z[:, None] // 2)]
    ).astype(jnp.float32)
    spread = jnp.stack(
        [(z[None, :] // 2 == k[:, None]), (z[None, :] // 2 + half == k[:, None])]
    ).astype(jnp.bfloat16)
    full = lambda shape: pl.BlockSpec(shape, lambda p: (0,) * len(shape))
    block = lines // pairs
    acc_shape = (wide_x * wide_y, chan_in, rows)
    return pl.pallas_call(
        lambda *refs: forward_kernel(rows, wide_y, *refs),
        grid=(pairs,),
        out_shape=(
            jax.ShapeDtypeStruct(cot.shape, jnp.bfloat16),
            jax.ShapeDtypeStruct((chan_out, taps), jnp.float32),
            jax.ShapeDtypeStruct((chan_out, 1), jnp.float32),
            jax.ShapeDtypeStruct(acc_shape, jnp.float32),
            jax.ShapeDtypeStruct(acc_shape, jnp.float32),
        ),
        in_specs=[
            full((chan_out, taps)),
            full((chan_out, 1)),
            full((2, rows, rows)),
            full((2, rows, rows)),
            full((27 * slots, chan_out)),
            pl.BlockSpec((block, taps, rows), lambda p: (p, 0, 0)),
            pl.BlockSpec((chan_out, cot.shape[1] // pairs), lambda p: (0, p)),
        ],
        out_specs=(
            pl.BlockSpec((chan_out, cot.shape[1] // pairs), lambda p: (0, p)),
            full((chan_out, taps)),
            full((chan_out, 1)),
            full(acc_shape),
            full(acc_shape),
        ),
        scratch_shapes=[
            pltpu.VMEM((chan_out, taps), jnp.float32),
            pltpu.VMEM((chan_out, 1), jnp.float32),
        ],
    )(weight_mat, bias, pool, spread, spread_w, patches, cot)


def fold_halo(main, axis, dim, width):
    size = main.shape[dim]
    head = lax.slice_in_dim(main, 0, width, axis=dim)
    tail = lax.slice_in_dim(main, size - width, size, axis=dim)
    from_left = shift(tail, axis, dim, 1)
    from_right = shift(head, axis, dim, -1)
    inner = lax.slice_in_dim(main, width, size - width, axis=dim)
    inner_size = size - 2 * width
    start = [0] * main.ndim
    inner = lax.dynamic_update_slice(
        inner, lax.slice_in_dim(inner, 0, width, axis=dim) + from_left, start
    )
    start[dim] = inner_size - width
    inner = lax.dynamic_update_slice(
        inner, lax.slice_in_dim(inner, inner_size - width, inner_size, axis=dim) + from_right, start
    )
    return inner


def on_device(cells, weight, bias, cotangent):
    chan_in, cells_x, cells_y, cells_z = cells.shape
    chan_out = weight.shape[0]
    stencil = [
        (shift_a, shift_b, shift_e)
        for shift_a in range(3)
        for shift_b in range(3)
        for shift_e in range(3)
    ]
    widened = extended(cells, (("gx", 1), ("gy", 2), ("gz", 3)), 1)
    patches = jnp.stack(
        [
            widened[c, sa : sa + cells_x, sb : sb + cells_y, se : se + cells_z]
            for c in range(chan_in)
            for sa, sb, se in stencil
        ],
        axis=2,
    )
    patches = patches.reshape(cells_x * cells_y, chan_in * 27, cells_z)
    cot = cotangent.reshape(chan_out, -1)
    wide_x, wide_y = cells_x + 2, cells_y + 2
    pooled, weight_local, bias_local, main, edge = forward(
        weight, bias.reshape(chan_out, 1), patches, cot, cells_x // 2, wide_x, wide_y
    )
    pooled = pooled.reshape(cotangent.shape)
    taps = chan_in * 27
    width = -(-(taps + 1) // 128) * 128
    partial = jnp.concatenate(
        [weight_local, bias_local, jnp.zeros((chan_out, width - taps - 1), jnp.float32)],
        axis=1,
    )
    sizes = tuple(lax.axis_size(a) for a in AXES)
    both = allreduce(partial, sizes)
    weight_grad = both[:, :taps].reshape(chan_out, chan_in, 3, 3, 3)
    bias_grad = both[:, taps]
    main = main.reshape(wide_x, wide_y, chan_in, cells_z)
    edge = edge.reshape(wide_x, wide_y, chan_in, cells_z)
    lo = edge[..., cells_z - 1 :]
    hi = edge[..., :1]
    from_left = shift(hi, "gz", 3, 1)
    from_right = shift(lo, "gz", 3, -1)
    main = jnp.concatenate(
        [
            main[..., :1] + from_left,
            main[..., 1 : cells_z - 1],
            main[..., cells_z - 1 :] + from_right,
        ],
        axis=3,
    )
    main = fold_halo(main, "gy", 1, 1)
    main = fold_halo(main, "gx", 0, 1)
    input_grad = jnp.transpose(main, (2, 0, 1, 3))
    return (pooled, weight_grad, bias_grad, input_grad)


def solution(mesh):
    in_specs = (P(None, "gx", "gy", "gz"), P(), P(), P(None, "gx", "gy", "gz"))
    out_specs = (P(None, "gx", "gy", "gz"), P(), P(), P(None, "gx", "gy", "gz"))
    return jax.shard_map(
        on_device, mesh=mesh, in_specs=in_specs, out_specs=out_specs, check_vma=False
    )
```

```python
import jax
import jax.numpy as jnp
from jax import lax
from jax.experimental import pallas as pl
from jax.experimental.pallas import tpu as pltpu
from jax.sharding import PartitionSpec as P

MESH = pl.DeviceIdType.MESH
AXES = ("gx", "gy", "gz")

leak_slope = 0.3
soft_scale = 10.0


def shift(piece, axis, dim, step):
    count = lax.axis_size(axis)
    pairs = [(i, (i + step) % count) for i in range(count)]
    if piece.shape[dim] == 1:
        moved = lax.ppermute(jnp.squeeze(piece, dim), axis, pairs)
        return jnp.expand_dims(moved, dim)
    return lax.ppermute(piece, axis, pairs)


def extended(cells, sides, width):
    for axis, dim in sides:
        head = lax.slice_in_dim(cells, 0, width, axis=dim)
        tail = lax.slice_in_dim(cells, cells.shape[dim] - width, cells.shape[dim], axis=dim)
        cells = jnp.concatenate(
            [shift(tail, axis, dim, 1), cells, shift(head, axis, dim, -1)],
            axis=dim,
        )
    return cells


def allreduce_kernel(sizes, x_ref, o_ref, slots_x, slots_y, slots_z, acc_x, acc_y,
                     send_x, recv_x, send_y, recv_y, send_z, recv_z):
    me = tuple(lax.axis_index(a) for a in AXES)
    slots = (slots_x, slots_y, slots_z)
    sends = (send_x, send_y, send_z)
    recvs = (recv_x, recv_y, recv_z)
    sources = (x_ref, acc_x, acc_y)
    sinks = (acc_x, acc_y, o_ref)

    def peer(axis, index):
        return tuple(index if k == axis else me[k] for k in range(3))

    barrier = pltpu.get_barrier_semaphore()
    count = 0
    for axis, n in enumerate(sizes):
        for d in range(1, n):
            target = lax.rem(me[axis] + d, n)
            pl.semaphore_signal(barrier, inc=1, device_id=peer(axis, target), device_id_type=MESH)
            count += 1
    pl.semaphore_wait(barrier, count)

    for axis, n in enumerate(sizes):
        src, held, sink = sources[axis], slots[axis], sinks[axis]
        mine = me[axis]
        copies = []
        for d in range(1, n):
            target = lax.rem(mine + d, n)
            copy = pltpu.make_async_remote_copy(
                src_ref=src,
                dst_ref=held.at[mine],
                send_sem=sends[axis].at[d],
                recv_sem=recvs[axis].at[mine],
                device_id=peer(axis, target),
                device_id_type=MESH,
            )
            copy.start()
            copies.append(copy)
        held[mine] = src[...]
        for d in range(1, n):
            origin = lax.rem(mine + n - d, n)
            incoming = pltpu.make_async_remote_copy(
                src_ref=src,
                dst_ref=held.at[origin],
                send_sem=sends[axis].at[d],
                recv_sem=recvs[axis].at[origin],
                device_id=peer(axis, origin),
                device_id_type=MESH,
            )
            incoming.wait_recv()
        for copy in copies:
            copy.wait_send()
        total = held[0]
        for k in range(1, n):
            total = total + held[k]
        sink[...] = total


def allreduce(x, sizes):
    shape = x.shape
    return pl.pallas_call(
        lambda *refs: allreduce_kernel(sizes, *refs),
        out_shape=jax.ShapeDtypeStruct(shape, jnp.float32),
        in_specs=[pl.BlockSpec(memory_space=pltpu.VMEM)],
        out_specs=pl.BlockSpec(memory_space=pltpu.VMEM),
        scratch_shapes=[
            pltpu.VMEM((sizes[0],) + shape, jnp.float32),
            pltpu.VMEM((sizes[1],) + shape, jnp.float32),
            pltpu.VMEM((sizes[2],) + shape, jnp.float32),
            pltpu.VMEM(shape, jnp.float32),
            pltpu.VMEM(shape, jnp.float32),
            pltpu.SemaphoreType.DMA((sizes[0],)),
            pltpu.SemaphoreType.DMA((sizes[0],)),
            pltpu.SemaphoreType.DMA((sizes[1],)),
            pltpu.SemaphoreType.DMA((sizes[1],)),
            pltpu.SemaphoreType.DMA((sizes[2],)),
            pltpu.SemaphoreType.DMA((sizes[2],)),
        ],
        compiler_params=pltpu.CompilerParams(collective_id=0, has_side_effects=True),
    )(x)


def activate(preact):
    return leak_slope * preact + (1.0 - leak_slope) / soft_scale * jax.nn.softplus(
        soft_scale * preact
    )


def slope_of(preact):
    return leak_slope + (1.0 - leak_slope) * jax.nn.sigmoid(soft_scale * preact)


def forward_kernel(rows, wide_y, w_ref, b_ref, q_ref, u_ref, wt_ref, p_ref, cot_ref,
                   pooled_ref, wg_ref, bg_ref, main_ref, edge_ref, wg_acc, bg_acc):
    step = pl.program_id(0)
    plane = p_ref.shape[0] // 2
    lines = plane // 4

    @pl.when(step == 0)
    def _():
        wg_acc[...] = jnp.zeros_like(wg_acc)
        bg_acc[...] = jnp.zeros_like(bg_acc)
        main_ref[...] = jnp.zeros_like(main_ref)
        edge_ref[...] = jnp.zeros_like(edge_ref)

    weight = w_ref[...]
    bias = b_ref[...]
    spread_w = wt_ref[...]
    slots = spread_w.shape[0] // 27
    lane = lax.broadcasted_iota(jnp.int32, (slots, rows), 1)
    first = lane == 0
    last = lane == rows - 1

    @pl.loop(0, lines)
    def _(j):
        cot = cot_ref[:, pl.ds(pl.multiple_of(j * rows, rows), rows)]
        ups = (
            jnp.dot(cot, u_ref[0], preferred_element_type=jnp.float32) * 0.125,
            jnp.dot(cot, u_ref[1], preferred_element_type=jnp.float32) * 0.125,
        )
        totals = [None, None]
        wg = None
        bg = None
        spreads = []
        for px, base in enumerate((0, plane)):
            deltas = []
            for r in range(4):
                row = base + j * 4 + r
                patch = p_ref[row]
                preact = jnp.dot(weight, patch, preferred_element_type=jnp.float32) + bias
                scaled = soft_scale * preact
                e = jnp.exp(-jnp.abs(scaled))
                softplus = jnp.maximum(scaled, 0.0) + jnp.log1p(e)
                activated = leak_slope * preact + (1.0 - leak_slope) / soft_scale * softplus
                half = r // 2
                totals[half] = activated if totals[half] is None else totals[half] + activated
                sigmoid = jnp.where(scaled >= 0.0, 1.0, e) / (1.0 + e)
                slope = leak_slope + (1.0 - leak_slope) * sigmoid
                delta = (slope * ups[half]).astype(jnp.bfloat16)
                deltas.append(delta)
                term = lax.dot_general(
                    delta, patch, (((1,), (1,)), ((), ())), preferred_element_type=jnp.float32
                )
                wg = term if wg is None else wg + term
                part = delta.astype(jnp.float32)
                bg = part if bg is None else bg + part
            spreads.append(
                jnp.dot(
                    spread_w, jnp.concatenate(deltas, axis=1), preferred_element_type=jnp.float32
                )
            )
        acc_main = {}
        acc_edge = {}
        for px in range(2):
            for r in range(4):
                cols = slice(r * rows, (r + 1) * rows)
                for a in range(3):
                    for b in range(3):
                        at = (a * 3 + b) * 3 * slots
                        g = spreads[px]
                        v0 = pltpu.roll(g[at : at + slots, cols], rows - 1, 1)
                        v1 = g[at + slots : at + 2 * slots, cols]
                        v2 = pltpu.roll(g[at + 2 * slots : at + 3 * slots, cols], 1, 1)
                        inner = jnp.where(last, 0.0, v0) + v1 + jnp.where(first, 0.0, v2)
                        edge = jnp.where(last, v0, 0.0) + jnp.where(first, v2, 0.0)
                        key = (px + a, r + b)
                        if key in acc_main:
                            acc_main[key] = acc_main[key] + inner
                            acc_edge[key] = acc_edge[key] + edge
                        else:
                            acc_main[key] = inner
                            acc_edge[key] = edge
        for (dx, dy), value in acc_main.items():
            out = (step * 2 + dx) * wide_y + (j * 4 + dy)
            main_ref[out] += value[: main_ref.shape[1]]
            edge_ref[out] += acc_edge[dx, dy][: edge_ref.shape[1]]
        wg_acc[...] += wg
        bg_acc[...] += jnp.sum(bg, axis=1, keepdims=True)
        pooled = jnp.dot(
            totals[0], q_ref[0], preferred_element_type=jnp.float32, precision=lax.Precision.HIGHEST
        ) + jnp.dot(
            totals[1], q_ref[1], preferred_element_type=jnp.float32, precision=lax.Precision.HIGHEST
        )
        pooled_ref[:, pl.ds(pl.multiple_of(j * rows, rows), rows)] = (pooled * 0.125).astype(
            pooled_ref.dtype
        )

    @pl.when(step == pl.num_programs(0) - 1)
    def _():
        wg_ref[...] = wg_acc[...]
        bg_ref[...] = bg_acc[...]


def forward(weight, bias, patches, cot, pairs, wide_x, wide_y):
    lines, taps, rows = patches.shape
    chan_out, chan_in = weight.shape[:2]
    weight_mat = weight.reshape(chan_out, taps)
    slots = 8
    spread_w = jnp.transpose(weight, (2, 3, 4, 1, 0))
    spread_w = jnp.pad(spread_w, ((0, 0), (0, 0), (0, 0), (0, slots - chan_in), (0, 0)))
    spread_w = spread_w.reshape(27 * slots, chan_out)
    half = rows // 2
    z = jnp.arange(rows)
    k = jnp.arange(rows)
    pool = jnp.stack(
        [(k[None, :] == z[:, None] // 2), (k[None, :] == half + z[:, None] // 2)]
    ).astype(jnp.float32)
    spread = jnp.stack(
        [(z[None, :] // 2 == k[:, None]), (z[None, :] // 2 + half == k[:, None])]
    ).astype(jnp.bfloat16)
    full = lambda shape: pl.BlockSpec(shape, lambda p: (0,) * len(shape))
    block = lines // pairs
    acc_shape = (wide_x * wide_y, chan_in, rows)
    return pl.pallas_call(
        lambda *refs: forward_kernel(rows, wide_y, *refs),
        grid=(pairs,),
        out_shape=(
            jax.ShapeDtypeStruct(cot.shape, jnp.bfloat16),
            jax.ShapeDtypeStruct((chan_out, taps), jnp.float32),
            jax.ShapeDtypeStruct((chan_out, 1), jnp.float32),
            jax.ShapeDtypeStruct(acc_shape, jnp.float32),
            jax.ShapeDtypeStruct(acc_shape, jnp.float32),
        ),
        in_specs=[
            full((chan_out, taps)),
            full((chan_out, 1)),
            full((2, rows, rows)),
            full((2, rows, rows)),
            full((27 * slots, chan_out)),
            pl.BlockSpec((block, taps, rows), lambda p: (p, 0, 0)),
            pl.BlockSpec((chan_out, cot.shape[1] // pairs), lambda p: (0, p)),
        ],
        out_specs=(
            pl.BlockSpec((chan_out, cot.shape[1] // pairs), lambda p: (0, p)),
            full((chan_out, taps)),
            full((chan_out, 1)),
            full(acc_shape),
            full(acc_shape),
        ),
        scratch_shapes=[
            pltpu.VMEM((chan_out, taps), jnp.float32),
            pltpu.VMEM((chan_out, 1), jnp.float32),
        ],
    )(weight_mat, bias, pool, spread, spread_w, patches, cot)


def fold_halo(main, axis, dim, width):
    size = main.shape[dim]
    head = lax.slice_in_dim(main, 0, width, axis=dim)
    tail = lax.slice_in_dim(main, size - width, size, axis=dim)
    from_left = shift(tail, axis, dim, 1)
    from_right = shift(head, axis, dim, -1)
    inner = lax.slice_in_dim(main, width, size - width, axis=dim)
    inner_size = size - 2 * width
    start = [0] * main.ndim
    inner = lax.dynamic_update_slice(
        inner, lax.slice_in_dim(inner, 0, width, axis=dim) + from_left, start
    )
    start[dim] = inner_size - width
    inner = lax.dynamic_update_slice(
        inner, lax.slice_in_dim(inner, inner_size - width, inner_size, axis=dim) + from_right, start
    )
    return inner


def on_device(cells, weight, bias, cotangent):
    chan_in, cells_x, cells_y, cells_z = cells.shape
    chan_out = weight.shape[0]
    stencil = [
        (shift_a, shift_b, shift_e)
        for shift_a in range(3)
        for shift_b in range(3)
        for shift_e in range(3)
    ]
    widened = extended(cells, (("gx", 1), ("gy", 2), ("gz", 3)), 1)
    patches = jnp.stack(
        [
            jnp.transpose(
                widened[:, sa : sa + cells_x, sb : sb + cells_y, se : se + cells_z], (1, 2, 0, 3)
            )
            for sa, sb, se in stencil
        ],
        axis=3,
    )
    patches = patches.reshape(cells_x * cells_y, chan_in * 27, cells_z)
    cot = cotangent.reshape(chan_out, -1)
    wide_x, wide_y = cells_x + 2, cells_y + 2
    pooled, weight_local, bias_local, main, edge = forward(
        weight, bias.reshape(chan_out, 1), patches, cot, cells_x // 2, wide_x, wide_y
    )
    pooled = pooled.reshape(cotangent.shape)
    taps = chan_in * 27
    width = -(-(taps + 1) // 128) * 128
    partial = jnp.concatenate(
        [weight_local, bias_local, jnp.zeros((chan_out, width - taps - 1), jnp.float32)],
        axis=1,
    )
    sizes = tuple(lax.axis_size(a) for a in AXES)
    both = allreduce(partial, sizes)
    weight_grad = both[:, :taps].reshape(chan_out, chan_in, 3, 3, 3)
    bias_grad = both[:, taps]
    main = main.reshape(wide_x, wide_y, chan_in, cells_z)
    edge = edge.reshape(wide_x, wide_y, chan_in, cells_z)
    lo = edge[..., cells_z - 1 :]
    hi = edge[..., :1]
    from_left = shift(hi, "gz", 3, 1)
    from_right = shift(lo, "gz", 3, -1)
    main = jnp.concatenate(
        [
            main[..., :1] + from_left,
            main[..., 1 : cells_z - 1],
            main[..., cells_z - 1 :] + from_right,
        ],
        axis=3,
    )
    main = fold_halo(main, "gy", 1, 1)
    main = fold_halo(main, "gx", 0, 1)
    input_grad = jnp.transpose(main, (2, 0, 1, 3))
    return (pooled, weight_grad, bias_grad, input_grad)


def solution(mesh):
    in_specs = (P(None, "gx", "gy", "gz"), P(), P(), P(None, "gx", "gy", "gz"))
    out_specs = (P(None, "gx", "gy", "gz"), P(), P(), P(None, "gx", "gy", "gz"))
    return jax.shard_map(
        on_device, mesh=mesh, in_specs=in_specs, out_specs=out_specs, check_vma=False
    )
```

```python
import jax
import jax.numpy as jnp
from jax import lax
from jax.experimental import pallas as pl
from jax.experimental.pallas import tpu as pltpu
from jax.sharding import PartitionSpec as P

MESH = pl.DeviceIdType.MESH
AXES = ("gx", "gy", "gz")

leak_slope = 0.3
soft_scale = 10.0


def extended(cells, sides, width):
    for axis, dim in sides:
        count = lax.axis_size(axis)
        head = lax.slice_in_dim(cells, 0, width, axis=dim)
        tail = lax.slice_in_dim(cells, cells.shape[dim] - width, cells.shape[dim], axis=dim)
        cells = jnp.concatenate(
            [
                lax.ppermute(tail, axis, [(i, (i + 1) % count) for i in range(count)]),
                cells,
                lax.ppermute(head, axis, [((i + 1) % count, i) for i in range(count)]),
            ],
            axis=dim,
        )
    return cells


def allreduce_kernel(sizes, x_ref, o_ref, slots_a, slots_b, acc_a, send_a, recv_a, send_b, recv_b):
    me = tuple(lax.axis_index(a) for a in AXES)
    groups = (
        [(k,) for k in range(sizes[0])],
        [(k, m) for k in range(sizes[1]) for m in range(sizes[2])],
    )
    places = ((0,), (1, 2))

    def device(phase, member):
        coords = list(me)
        for axis, value in zip(places[phase], member):
            coords[axis] = value
        return tuple(coords)

    def rank(phase):
        out = 0
        for axis in places[phase]:
            out = out * sizes[axis] + me[axis]
        return out

    def member_of(phase, index):
        out = []
        for axis in reversed(places[phase]):
            out.append(lax.rem(index, sizes[axis]))
            index = index // sizes[axis]
        return tuple(reversed(out))

    barrier = pltpu.get_barrier_semaphore()
    count = 0
    for phase in range(2):
        n = len(groups[phase])
        for d in range(1, n):
            target = member_of(phase, lax.rem(rank(phase) + d, n))
            pl.semaphore_signal(barrier, inc=1, device_id=device(phase, target), device_id_type=MESH)
            count += 1
    pl.semaphore_wait(barrier, count)

    slots = (slots_a, slots_b)
    sends = (send_a, send_b)
    recvs = (recv_a, recv_b)
    sources = (x_ref, acc_a)
    sinks = (acc_a, o_ref)
    for phase in range(2):
        n = len(groups[phase])
        src, held, sink = sources[phase], slots[phase], sinks[phase]
        mine = rank(phase)
        copies = []
        for d in range(1, n):
            target = member_of(phase, lax.rem(mine + d, n))
            copy = pltpu.make_async_remote_copy(
                src_ref=src,
                dst_ref=held.at[mine],
                send_sem=sends[phase].at[d],
                recv_sem=recvs[phase].at[mine],
                device_id=device(phase, target),
                device_id_type=MESH,
            )
            copy.start()
            copies.append(copy)
        held[mine] = src[...]
        for d in range(1, n):
            origin = lax.rem(mine + n - d, n)
            incoming = pltpu.make_async_remote_copy(
                src_ref=src,
                dst_ref=held.at[origin],
                send_sem=sends[phase].at[d],
                recv_sem=recvs[phase].at[origin],
                device_id=device(phase, member_of(phase, origin)),
                device_id_type=MESH,
            )
            incoming.wait_recv()
        for copy in copies:
            copy.wait_send()
        total = held[0]
        for k in range(1, n):
            total = total + held[k]
        sink[...] = total


def allreduce(x, sizes):
    shape = x.shape
    first, second = sizes[0], sizes[1] * sizes[2]
    return pl.pallas_call(
        lambda *refs: allreduce_kernel(sizes, *refs),
        out_shape=jax.ShapeDtypeStruct(shape, jnp.float32),
        in_specs=[pl.BlockSpec(memory_space=pltpu.VMEM)],
        out_specs=pl.BlockSpec(memory_space=pltpu.VMEM),
        scratch_shapes=[
            pltpu.VMEM((first,) + shape, jnp.float32),
            pltpu.VMEM((second,) + shape, jnp.float32),
            pltpu.VMEM(shape, jnp.float32),
            pltpu.SemaphoreType.DMA((first,)),
            pltpu.SemaphoreType.DMA((first,)),
            pltpu.SemaphoreType.DMA((second,)),
            pltpu.SemaphoreType.DMA((second,)),
        ],
        compiler_params=pltpu.CompilerParams(collective_id=0, has_side_effects=True),
    )(x)


def forward_kernel(rows, wide_y, w_ref, b_ref, q_ref, u_ref, wt_ref, p_ref, cot_ref,
                   pooled_ref, wg_ref, bg_ref, main_ref, edge_ref, wg_acc, bg_acc):
    step = pl.program_id(0)
    plane = p_ref.shape[0] // 2
    lines = plane // 4

    @pl.when(step == 0)
    def _():
        wg_acc[...] = jnp.zeros_like(wg_acc)
        bg_acc[...] = jnp.zeros_like(bg_acc)
        main_ref[...] = jnp.zeros_like(main_ref)
        edge_ref[...] = jnp.zeros_like(edge_ref)

    weight = w_ref[...]
    bias = b_ref[...]
    spread_w = wt_ref[...]
    slots = spread_w.shape[0] // 27
    lane = lax.broadcasted_iota(jnp.int32, (slots, rows), 1)
    first = lane == 0
    last = lane == rows - 1

    @pl.loop(0, lines)
    def _(j):
        cot = cot_ref[:, pl.ds(pl.multiple_of(j * rows, rows), rows)]
        ups = (
            jnp.dot(cot, u_ref[0], preferred_element_type=jnp.float32) * 0.125,
            jnp.dot(cot, u_ref[1], preferred_element_type=jnp.float32) * 0.125,
        )
        totals = [None, None]
        wg = None
        bg = None
        spreads = []
        for px, base in enumerate((0, plane)):
            deltas = []
            for r in range(4):
                row = base + j * 4 + r
                patch = p_ref[row]
                preact = jnp.dot(weight, patch, preferred_element_type=jnp.float32) + bias
                scaled = soft_scale * preact
                e = jnp.exp(-jnp.abs(scaled))
                softplus = jnp.maximum(scaled, 0.0) + jnp.log1p(e)
                activated = leak_slope * preact + (1.0 - leak_slope) / soft_scale * softplus
                half = r // 2
                totals[half] = activated if totals[half] is None else totals[half] + activated
                sigmoid = jnp.where(scaled >= 0.0, 1.0, e) / (1.0 + e)
                slope = leak_slope + (1.0 - leak_slope) * sigmoid
                delta = (slope * ups[half]).astype(jnp.bfloat16)
                deltas.append(delta)
                term = lax.dot_general(
                    delta, patch, (((1,), (1,)), ((), ())), preferred_element_type=jnp.float32
                )
                wg = term if wg is None else wg + term
                part = delta.astype(jnp.float32)
                bg = part if bg is None else bg + part
            spreads.append(
                jnp.dot(
                    spread_w, jnp.concatenate(deltas, axis=1), preferred_element_type=jnp.float32
                )
            )
        acc_main = {}
        acc_edge = {}
        for px in range(2):
            for r in range(4):
                cols = slice(r * rows, (r + 1) * rows)
                for a in range(3):
                    for b in range(3):
                        at = (a * 3 + b) * 3 * slots
                        g = spreads[px]
                        v0 = pltpu.roll(g[at : at + slots, cols], rows - 1, 1)
                        v1 = g[at + slots : at + 2 * slots, cols]
                        v2 = pltpu.roll(g[at + 2 * slots : at + 3 * slots, cols], 1, 1)
                        inner = jnp.where(last, 0.0, v0) + v1 + jnp.where(first, 0.0, v2)
                        edge = jnp.where(last, v0, 0.0) + jnp.where(first, v2, 0.0)
                        key = (px + a, r + b)
                        if key in acc_main:
                            acc_main[key] = acc_main[key] + inner
                            acc_edge[key] = acc_edge[key] + edge
                        else:
                            acc_main[key] = inner
                            acc_edge[key] = edge
        for (dx, dy), value in acc_main.items():
            out = (step * 2 + dx) * wide_y + (j * 4 + dy)
            main_ref[out] += value[: main_ref.shape[1]]
            edge_ref[out] += acc_edge[dx, dy][: edge_ref.shape[1]]
        wg_acc[...] += wg
        bg_acc[...] += jnp.sum(bg, axis=1, keepdims=True)
        pooled = jnp.dot(
            totals[0], q_ref[0], preferred_element_type=jnp.float32, precision=lax.Precision.HIGHEST
        ) + jnp.dot(
            totals[1], q_ref[1], preferred_element_type=jnp.float32, precision=lax.Precision.HIGHEST
        )
        pooled_ref[:, pl.ds(pl.multiple_of(j * rows, rows), rows)] = (pooled * 0.125).astype(
            pooled_ref.dtype
        )

    @pl.when(step == pl.num_programs(0) - 1)
    def _():
        wg_ref[...] = wg_acc[...]
        bg_ref[...] = bg_acc[...]


def forward(weight, bias, patches, cot, pairs, wide_x, wide_y):
    lines, taps, rows = patches.shape
    chan_out, chan_in = weight.shape[:2]
    weight_mat = weight.reshape(chan_out, taps)
    slots = 8
    spread_w = jnp.transpose(weight, (2, 3, 4, 1, 0))
    spread_w = jnp.pad(spread_w, ((0, 0), (0, 0), (0, 0), (0, slots - chan_in), (0, 0)))
    spread_w = spread_w.reshape(27 * slots, chan_out)
    half = rows // 2
    z = jnp.arange(rows)
    k = jnp.arange(rows)
    pool = jnp.stack(
        [(k[None, :] == z[:, None] // 2), (k[None, :] == half + z[:, None] // 2)]
    ).astype(jnp.float32)
    spread = jnp.stack(
        [(z[None, :] // 2 == k[:, None]), (z[None, :] // 2 + half == k[:, None])]
    ).astype(jnp.bfloat16)
    full = lambda shape: pl.BlockSpec(shape, lambda p: (0,) * len(shape))
    block = lines // pairs
    acc_shape = (wide_x * wide_y, chan_in, rows)
    return pl.pallas_call(
        lambda *refs: forward_kernel(rows, wide_y, *refs),
        grid=(pairs,),
        out_shape=(
            jax.ShapeDtypeStruct(cot.shape, jnp.bfloat16),
            jax.ShapeDtypeStruct((chan_out, taps), jnp.float32),
            jax.ShapeDtypeStruct((chan_out, 1), jnp.float32),
            jax.ShapeDtypeStruct(acc_shape, jnp.float32),
            jax.ShapeDtypeStruct(acc_shape, jnp.float32),
        ),
        in_specs=[
            full((chan_out, taps)),
            full((chan_out, 1)),
            full((2, rows, rows)),
            full((2, rows, rows)),
            full((27 * slots, chan_out)),
            pl.BlockSpec((block, taps, rows), lambda p: (p, 0, 0)),
            pl.BlockSpec((chan_out, cot.shape[1] // pairs), lambda p: (0, p)),
        ],
        out_specs=(
            pl.BlockSpec((chan_out, cot.shape[1] // pairs), lambda p: (0, p)),
            full((chan_out, taps)),
            full((chan_out, 1)),
            full(acc_shape),
            full(acc_shape),
        ),
        scratch_shapes=[
            pltpu.VMEM((chan_out, taps), jnp.float32),
            pltpu.VMEM((chan_out, 1), jnp.float32),
        ],
    )(weight_mat, bias, pool, spread, spread_w, patches, cot)


def fold_halo(main, axis, dim, width):
    count = lax.axis_size(axis)
    size = main.shape[dim]
    head = lax.slice_in_dim(main, 0, width, axis=dim)
    tail = lax.slice_in_dim(main, size - width, size, axis=dim)
    from_left = lax.ppermute(tail, axis, [(i, (i + 1) % count) for i in range(count)])
    from_right = lax.ppermute(head, axis, [((i + 1) % count, i) for i in range(count)])
    inner = lax.slice_in_dim(main, width, size - width, axis=dim)
    inner_size = size - 2 * width
    start = [0] * main.ndim
    inner = lax.dynamic_update_slice(
        inner, lax.slice_in_dim(inner, 0, width, axis=dim) + from_left, start
    )
    start[dim] = inner_size - width
    inner = lax.dynamic_update_slice(
        inner, lax.slice_in_dim(inner, inner_size - width, inner_size, axis=dim) + from_right, start
    )
    return inner


def on_device(cells, weight, bias, cotangent):
    chan_in, cells_x, cells_y, cells_z = cells.shape
    chan_out = weight.shape[0]
    stencil = [
        (shift_a, shift_b, shift_e)
        for shift_a in range(3)
        for shift_b in range(3)
        for shift_e in range(3)
    ]
    widened = extended(cells, (("gx", 1), ("gy", 2), ("gz", 3)), 1)
    patches = jnp.stack(
        [
            jnp.transpose(
                widened[:, sa : sa + cells_x, sb : sb + cells_y, se : se + cells_z], (1, 2, 0, 3)
            )
            for sa, sb, se in stencil
        ],
        axis=3,
    )
    patches = patches.reshape(cells_x * cells_y, chan_in * 27, cells_z)
    cot = cotangent.reshape(chan_out, -1)
    wide_x, wide_y = cells_x + 2, cells_y + 2
    pooled, weight_local, bias_local, main, edge = forward(
        weight, bias.reshape(chan_out, 1), patches, cot, cells_x // 2, wide_x, wide_y
    )
    pooled = pooled.reshape(cotangent.shape)
    taps = chan_in * 27
    width = -(-(taps + 1) // 128) * 128
    partial = jnp.concatenate(
        [weight_local, bias_local, jnp.zeros((chan_out, width - taps - 1), jnp.float32)],
        axis=1,
    )
    sizes = tuple(lax.axis_size(a) for a in AXES)
    both = allreduce(partial, sizes)
    weight_grad = both[:, :taps].reshape(chan_out, chan_in, 3, 3, 3)
    bias_grad = both[:, taps]
    main = main.reshape(wide_x, wide_y, chan_in, cells_z)
    edge = edge.reshape(wide_x, wide_y, chan_in, cells_z)
    lo = edge[..., cells_z - 1 :]
    hi = edge[..., :1]
    count = lax.axis_size("gz")
    from_left = lax.ppermute(hi, "gz", [(i, (i + 1) % count) for i in range(count)])
    from_right = lax.ppermute(lo, "gz", [((i + 1) % count, i) for i in range(count)])
    main = jnp.concatenate(
        [
            main[..., :1] + from_left,
            main[..., 1 : cells_z - 1],
            main[..., cells_z - 1 :] + from_right,
        ],
        axis=3,
    )
    main = fold_halo(main, "gy", 1, 1)
    main = fold_halo(main, "gx", 0, 1)
    input_grad = jnp.transpose(main, (2, 0, 1, 3))
    return (pooled, weight_grad, bias_grad, input_grad)


def solution(mesh):
    in_specs = (P(None, "gx", "gy", "gz"), P(), P(), P(None, "gx", "gy", "gz"))
    out_specs = (P(None, "gx", "gy", "gz"), P(), P(), P(None, "gx", "gy", "gz"))
    return jax.shard_map(
        on_device, mesh=mesh, in_specs=in_specs, out_specs=out_specs, check_vma=False
    )
```

```python
import jax
import jax.numpy as jnp
from jax import lax
from jax.experimental import pallas as pl
from jax.experimental.pallas import tpu as pltpu
from jax.sharding import PartitionSpec as P

MESH = pl.DeviceIdType.MESH
AXES = ("gx", "gy", "gz")

leak_slope = 0.3
soft_scale = 10.0


def extended(cells, sides, width):
    for axis, dim in sides:
        count = lax.axis_size(axis)
        head = lax.slice_in_dim(cells, 0, width, axis=dim)
        tail = lax.slice_in_dim(cells, cells.shape[dim] - width, cells.shape[dim], axis=dim)
        cells = jnp.concatenate(
            [
                lax.ppermute(tail, axis, [(i, (i + 1) % count) for i in range(count)]),
                cells,
                lax.ppermute(head, axis, [((i + 1) % count, i) for i in range(count)]),
            ],
            axis=dim,
        )
    return cells


def allreduce_kernel(sizes, x_ref, o_ref, slots_a, slots_b, acc_a, send_a, recv_a, send_b, recv_b):
    me = tuple(lax.axis_index(a) for a in AXES)
    groups = (
        [(k,) for k in range(sizes[0])],
        [(k, m) for k in range(sizes[1]) for m in range(sizes[2])],
    )
    places = ((0,), (1, 2))

    def device(phase, member):
        coords = list(me)
        for axis, value in zip(places[phase], member):
            coords[axis] = value
        return tuple(coords)

    def rank(phase):
        out = 0
        for axis in places[phase]:
            out = out * sizes[axis] + me[axis]
        return out

    def member_of(phase, index):
        out = []
        for axis in reversed(places[phase]):
            out.append(lax.rem(index, sizes[axis]))
            index = index // sizes[axis]
        return tuple(reversed(out))

    barrier = pltpu.get_barrier_semaphore()
    count = 0
    for phase in range(2):
        n = len(groups[phase])
        for d in range(1, n):
            target = member_of(phase, lax.rem(rank(phase) + d, n))
            pl.semaphore_signal(barrier, inc=1, device_id=device(phase, target), device_id_type=MESH)
            count += 1
    pl.semaphore_wait(barrier, count)

    slots = (slots_a, slots_b)
    sends = (send_a, send_b)
    recvs = (recv_a, recv_b)
    sources = (x_ref, acc_a)
    sinks = (acc_a, o_ref)
    for phase in range(2):
        n = len(groups[phase])
        src, held, sink = sources[phase], slots[phase], sinks[phase]
        mine = rank(phase)
        copies = []
        for d in range(1, n):
            target = member_of(phase, lax.rem(mine + d, n))
            copy = pltpu.make_async_remote_copy(
                src_ref=src,
                dst_ref=held.at[mine],
                send_sem=sends[phase].at[d],
                recv_sem=recvs[phase].at[mine],
                device_id=device(phase, target),
                device_id_type=MESH,
            )
            copy.start()
            copies.append(copy)
        held[mine] = src[...]
        for d in range(1, n):
            origin = lax.rem(mine + n - d, n)
            incoming = pltpu.make_async_remote_copy(
                src_ref=src,
                dst_ref=held.at[origin],
                send_sem=sends[phase].at[d],
                recv_sem=recvs[phase].at[origin],
                device_id=device(phase, member_of(phase, origin)),
                device_id_type=MESH,
            )
            incoming.wait_recv()
        for copy in copies:
            copy.wait_send()
        total = held[0]
        for k in range(1, n):
            total = total + held[k]
        sink[...] = total


def allreduce(x, sizes):
    shape = x.shape
    first, second = sizes[0], sizes[1] * sizes[2]
    return pl.pallas_call(
        lambda *refs: allreduce_kernel(sizes, *refs),
        out_shape=jax.ShapeDtypeStruct(shape, jnp.float32),
        in_specs=[pl.BlockSpec(memory_space=pltpu.VMEM)],
        out_specs=pl.BlockSpec(memory_space=pltpu.VMEM),
        scratch_shapes=[
            pltpu.VMEM((first,) + shape, jnp.float32),
            pltpu.VMEM((second,) + shape, jnp.float32),
            pltpu.VMEM(shape, jnp.float32),
            pltpu.SemaphoreType.DMA((first,)),
            pltpu.SemaphoreType.DMA((first,)),
            pltpu.SemaphoreType.DMA((second,)),
            pltpu.SemaphoreType.DMA((second,)),
        ],
        compiler_params=pltpu.CompilerParams(collective_id=0, has_side_effects=True),
    )(x)


def forward_kernel(rows, wide_y, w_ref, b_ref, q_ref, u_ref, wt_ref, p_ref, cot_ref,
                   pooled_ref, wg_ref, bg_ref, main_ref, edge_ref, wg_acc, bg_acc):
    step = pl.program_id(0)
    plane = p_ref.shape[0] // 2
    lines = plane // 4

    @pl.when(step == 0)
    def _():
        wg_acc[...] = jnp.zeros_like(wg_acc)
        bg_acc[...] = jnp.zeros_like(bg_acc)
        main_ref[...] = jnp.zeros_like(main_ref)
        edge_ref[...] = jnp.zeros_like(edge_ref)

    weight = w_ref[...]
    bias = b_ref[...]
    spread_w = wt_ref[...]
    slots = spread_w.shape[0] // 27
    lane = lax.broadcasted_iota(jnp.int32, (slots, rows), 1)
    first = lane == 0
    last = lane == rows - 1

    @pl.loop(0, lines)
    def _(j):
        cot = cot_ref[:, pl.ds(pl.multiple_of(j * rows, rows), rows)]
        ups = (
            jnp.dot(cot, u_ref[0], preferred_element_type=jnp.float32) * 0.125,
            jnp.dot(cot, u_ref[1], preferred_element_type=jnp.float32) * 0.125,
        )
        spread4 = jnp.concatenate([ups[0], ups[0], ups[1], ups[1]], axis=1)
        totals = [None, None]
        wg = None
        bg = None
        spreads = []
        for px, base in enumerate((0, plane)):
            patch = jnp.concatenate([p_ref[base + j * 4 + r] for r in range(4)], axis=1)
            preact = jnp.dot(weight, patch, preferred_element_type=jnp.float32) + bias
            scaled = soft_scale * preact
            e = jnp.exp(-jnp.abs(scaled))
            softplus = jnp.maximum(scaled, 0.0) + jnp.log1p(e)
            activated = leak_slope * preact + (1.0 - leak_slope) / soft_scale * softplus
            for half in range(2):
                pair = (
                    activated[:, 2 * half * rows : (2 * half + 1) * rows]
                    + activated[:, (2 * half + 1) * rows : (2 * half + 2) * rows]
                )
                totals[half] = pair if totals[half] is None else totals[half] + pair
            sigmoid = jnp.where(scaled >= 0.0, 1.0, e) / (1.0 + e)
            slope = leak_slope + (1.0 - leak_slope) * sigmoid
            delta = (slope * spread4).astype(jnp.bfloat16)
            term = lax.dot_general(
                delta, patch, (((1,), (1,)), ((), ())), preferred_element_type=jnp.float32
            )
            wg = term if wg is None else wg + term
            part = delta.astype(jnp.float32)
            bg = part if bg is None else bg + part
            spreads.append(jnp.dot(spread_w, delta, preferred_element_type=jnp.float32))
        acc_main = {}
        acc_edge = {}
        for px in range(2):
            for r in range(4):
                cols = slice(r * rows, (r + 1) * rows)
                for a in range(3):
                    for b in range(3):
                        at = (a * 3 + b) * 3 * slots
                        g = spreads[px]
                        v0 = pltpu.roll(g[at : at + slots, cols], rows - 1, 1)
                        v1 = g[at + slots : at + 2 * slots, cols]
                        v2 = pltpu.roll(g[at + 2 * slots : at + 3 * slots, cols], 1, 1)
                        inner = jnp.where(last, 0.0, v0) + v1 + jnp.where(first, 0.0, v2)
                        edge = jnp.where(last, v0, 0.0) + jnp.where(first, v2, 0.0)
                        key = (px + a, r + b)
                        if key in acc_main:
                            acc_main[key] = acc_main[key] + inner
                            acc_edge[key] = acc_edge[key] + edge
                        else:
                            acc_main[key] = inner
                            acc_edge[key] = edge
        for (dx, dy), value in acc_main.items():
            out = (step * 2 + dx) * wide_y + (j * 4 + dy)
            main_ref[out] += value[: main_ref.shape[1]]
            edge_ref[out] += acc_edge[dx, dy][: edge_ref.shape[1]]
        wg_acc[...] += wg
        bg_acc[...] += jnp.sum(bg, axis=1, keepdims=True)
        pooled = jnp.dot(
            totals[0], q_ref[0], preferred_element_type=jnp.float32, precision=lax.Precision.HIGHEST
        ) + jnp.dot(
            totals[1], q_ref[1], preferred_element_type=jnp.float32, precision=lax.Precision.HIGHEST
        )
        pooled_ref[:, pl.ds(pl.multiple_of(j * rows, rows), rows)] = (pooled * 0.125).astype(
            pooled_ref.dtype
        )

    @pl.when(step == pl.num_programs(0) - 1)
    def _():
        wg_ref[...] = wg_acc[...]
        bg_ref[...] = bg_acc[...]


def forward(weight, bias, patches, cot, pairs, wide_x, wide_y):
    lines, taps, rows = patches.shape
    chan_out, chan_in = weight.shape[:2]
    weight_mat = weight.reshape(chan_out, taps)
    slots = 8
    spread_w = jnp.transpose(weight, (2, 3, 4, 1, 0))
    spread_w = jnp.pad(spread_w, ((0, 0), (0, 0), (0, 0), (0, slots - chan_in), (0, 0)))
    spread_w = spread_w.reshape(27 * slots, chan_out)
    half = rows // 2
    z = jnp.arange(rows)
    k = jnp.arange(rows)
    pool = jnp.stack(
        [(k[None, :] == z[:, None] // 2), (k[None, :] == half + z[:, None] // 2)]
    ).astype(jnp.float32)
    spread = jnp.stack(
        [(z[None, :] // 2 == k[:, None]), (z[None, :] // 2 + half == k[:, None])]
    ).astype(jnp.bfloat16)
    full = lambda shape: pl.BlockSpec(shape, lambda p: (0,) * len(shape))
    block = lines // pairs
    acc_shape = (wide_x * wide_y, chan_in, rows)
    return pl.pallas_call(
        lambda *refs: forward_kernel(rows, wide_y, *refs),
        grid=(pairs,),
        out_shape=(
            jax.ShapeDtypeStruct(cot.shape, jnp.bfloat16),
            jax.ShapeDtypeStruct((chan_out, taps), jnp.float32),
            jax.ShapeDtypeStruct((chan_out, 1), jnp.float32),
            jax.ShapeDtypeStruct(acc_shape, jnp.float32),
            jax.ShapeDtypeStruct(acc_shape, jnp.float32),
        ),
        in_specs=[
            full((chan_out, taps)),
            full((chan_out, 1)),
            full((2, rows, rows)),
            full((2, rows, rows)),
            full((27 * slots, chan_out)),
            pl.BlockSpec((block, taps, rows), lambda p: (p, 0, 0)),
            pl.BlockSpec((chan_out, cot.shape[1] // pairs), lambda p: (0, p)),
        ],
        out_specs=(
            pl.BlockSpec((chan_out, cot.shape[1] // pairs), lambda p: (0, p)),
            full((chan_out, taps)),
            full((chan_out, 1)),
            full(acc_shape),
            full(acc_shape),
        ),
        scratch_shapes=[
            pltpu.VMEM((chan_out, taps), jnp.float32),
            pltpu.VMEM((chan_out, 1), jnp.float32),
        ],
    )(weight_mat, bias, pool, spread, spread_w, patches, cot)


def fold_halo(main, axis, dim, width):
    count = lax.axis_size(axis)
    size = main.shape[dim]
    head = lax.slice_in_dim(main, 0, width, axis=dim)
    tail = lax.slice_in_dim(main, size - width, size, axis=dim)
    from_left = lax.ppermute(tail, axis, [(i, (i + 1) % count) for i in range(count)])
    from_right = lax.ppermute(head, axis, [((i + 1) % count, i) for i in range(count)])
    inner = lax.slice_in_dim(main, width, size - width, axis=dim)
    inner_size = size - 2 * width
    start = [0] * main.ndim
    inner = lax.dynamic_update_slice(
        inner, lax.slice_in_dim(inner, 0, width, axis=dim) + from_left, start
    )
    start[dim] = inner_size - width
    inner = lax.dynamic_update_slice(
        inner, lax.slice_in_dim(inner, inner_size - width, inner_size, axis=dim) + from_right, start
    )
    return inner


def on_device(cells, weight, bias, cotangent):
    chan_in, cells_x, cells_y, cells_z = cells.shape
    chan_out = weight.shape[0]
    stencil = [
        (shift_a, shift_b, shift_e)
        for shift_a in range(3)
        for shift_b in range(3)
        for shift_e in range(3)
    ]
    widened = extended(cells, (("gx", 1), ("gy", 2), ("gz", 3)), 1)
    patches = jnp.stack(
        [
            jnp.transpose(
                widened[:, sa : sa + cells_x, sb : sb + cells_y, se : se + cells_z], (1, 2, 0, 3)
            )
            for sa, sb, se in stencil
        ],
        axis=3,
    )
    patches = patches.reshape(cells_x * cells_y, chan_in * 27, cells_z)
    cot = cotangent.reshape(chan_out, -1)
    wide_x, wide_y = cells_x + 2, cells_y + 2
    pooled, weight_local, bias_local, main, edge = forward(
        weight, bias.reshape(chan_out, 1), patches, cot, cells_x // 2, wide_x, wide_y
    )
    pooled = pooled.reshape(cotangent.shape)
    taps = chan_in * 27
    width = -(-(taps + 1) // 128) * 128
    partial = jnp.concatenate(
        [weight_local, bias_local, jnp.zeros((chan_out, width - taps - 1), jnp.float32)],
        axis=1,
    )
    sizes = tuple(lax.axis_size(a) for a in AXES)
    both = allreduce(partial, sizes)
    weight_grad = both[:, :taps].reshape(chan_out, chan_in, 3, 3, 3)
    bias_grad = both[:, taps]
    main = main.reshape(wide_x, wide_y, chan_in, cells_z)
    edge = edge.reshape(wide_x, wide_y, chan_in, cells_z)
    lo = edge[..., cells_z - 1 :]
    hi = edge[..., :1]
    count = lax.axis_size("gz")
    from_left = lax.ppermute(hi, "gz", [(i, (i + 1) % count) for i in range(count)])
    from_right = lax.ppermute(lo, "gz", [((i + 1) % count, i) for i in range(count)])
    main = jnp.concatenate(
        [
            main[..., :1] + from_left,
            main[..., 1 : cells_z - 1],
            main[..., cells_z - 1 :] + from_right,
        ],
        axis=3,
    )
    main = fold_halo(main, "gy", 1, 1)
    main = fold_halo(main, "gx", 0, 1)
    input_grad = jnp.transpose(main, (2, 0, 1, 3))
    return (pooled, weight_grad, bias_grad, input_grad)


def solution(mesh):
    in_specs = (P(None, "gx", "gy", "gz"), P(), P(), P(None, "gx", "gy", "gz"))
    out_specs = (P(None, "gx", "gy", "gz"), P(), P(), P(None, "gx", "gy", "gz"))
    return jax.shard_map(
        on_device, mesh=mesh, in_specs=in_specs, out_specs=out_specs, check_vma=False
    )
```

```python
import jax
import jax.numpy as jnp
from jax import lax
from jax.experimental import pallas as pl
from jax.experimental.pallas import tpu as pltpu
from jax.sharding import PartitionSpec as P

MESH = pl.DeviceIdType.MESH
AXES = ("gx", "gy", "gz")

leak_slope = 0.3
soft_scale = 10.0


def extended(cells, sides, width):
    for axis, dim in sides:
        count = lax.axis_size(axis)
        head = lax.slice_in_dim(cells, 0, width, axis=dim)
        tail = lax.slice_in_dim(cells, cells.shape[dim] - width, cells.shape[dim], axis=dim)
        cells = jnp.concatenate(
            [
                lax.ppermute(tail, axis, [(i, (i + 1) % count) for i in range(count)]),
                cells,
                lax.ppermute(head, axis, [((i + 1) % count, i) for i in range(count)]),
            ],
            axis=dim,
        )
    return cells


def extended_all(cells):
    names = AXES
    sizes = [lax.axis_size(a) for a in names]
    dims = (1, 2, 3)

    def part(piece, dim, d):
        n = piece.shape[dim]
        if d < 0:
            return lax.slice_in_dim(piece, n - 1, n, axis=dim)
        if d > 0:
            return lax.slice_in_dim(piece, 0, 1, axis=dim)
        return piece

    def linear(ix, iy, iz):
        return (ix * sizes[1] + iy) * sizes[2] + iz

    blocks = {}
    for dx in (-1, 0, 1):
        for dy in (-1, 0, 1):
            for dz in (-1, 0, 1):
                piece = part(part(part(cells, 1, dx), 2, dy), 3, dz)
                if (dx, dy, dz) != (0, 0, 0):
                    pairs = [
                        (
                            linear(ix, iy, iz),
                            linear((ix - dx) % sizes[0], (iy - dy) % sizes[1], (iz - dz) % sizes[2]),
                        )
                        for ix in range(sizes[0])
                        for iy in range(sizes[1])
                        for iz in range(sizes[2])
                    ]
                    piece = lax.ppermute(piece, names, pairs)
                blocks[dx, dy, dz] = piece
    return jnp.concatenate(
        [
            jnp.concatenate(
                [
                    jnp.concatenate([blocks[dx, dy, dz] for dz in (-1, 0, 1)], axis=3)
                    for dy in (-1, 0, 1)
                ],
                axis=2,
            )
            for dx in (-1, 0, 1)
        ],
        axis=1,
    )


def allreduce_kernel(sizes, x_ref, o_ref, slots_a, slots_b, acc_a, send_a, recv_a, send_b, recv_b):
    me = tuple(lax.axis_index(a) for a in AXES)
    groups = (
        [(k,) for k in range(sizes[0])],
        [(k, m) for k in range(sizes[1]) for m in range(sizes[2])],
    )
    places = ((0,), (1, 2))

    def device(phase, member):
        coords = list(me)
        for axis, value in zip(places[phase], member):
            coords[axis] = value
        return tuple(coords)

    def rank(phase):
        out = 0
        for axis in places[phase]:
            out = out * sizes[axis] + me[axis]
        return out

    def member_of(phase, index):
        out = []
        for axis in reversed(places[phase]):
            out.append(lax.rem(index, sizes[axis]))
            index = index // sizes[axis]
        return tuple(reversed(out))

    barrier = pltpu.get_barrier_semaphore()
    count = 0
    for phase in range(2):
        n = len(groups[phase])
        for d in range(1, n):
            target = member_of(phase, lax.rem(rank(phase) + d, n))
            pl.semaphore_signal(barrier, inc=1, device_id=device(phase, target), device_id_type=MESH)
            count += 1
    pl.semaphore_wait(barrier, count)

    slots = (slots_a, slots_b)
    sends = (send_a, send_b)
    recvs = (recv_a, recv_b)
    sources = (x_ref, acc_a)
    sinks = (acc_a, o_ref)
    for phase in range(2):
        n = len(groups[phase])
        src, held, sink = sources[phase], slots[phase], sinks[phase]
        mine = rank(phase)
        copies = []
        for d in range(1, n):
            target = member_of(phase, lax.rem(mine + d, n))
            copy = pltpu.make_async_remote_copy(
                src_ref=src,
                dst_ref=held.at[mine],
                send_sem=sends[phase].at[d],
                recv_sem=recvs[phase].at[mine],
                device_id=device(phase, target),
                device_id_type=MESH,
            )
            copy.start()
            copies.append(copy)
        held[mine] = src[...]
        for d in range(1, n):
            origin = lax.rem(mine + n - d, n)
            incoming = pltpu.make_async_remote_copy(
                src_ref=src,
                dst_ref=held.at[origin],
                send_sem=sends[phase].at[d],
                recv_sem=recvs[phase].at[origin],
                device_id=device(phase, member_of(phase, origin)),
                device_id_type=MESH,
            )
            incoming.wait_recv()
        for copy in copies:
            copy.wait_send()
        total = held[0]
        for k in range(1, n):
            total = total + held[k]
        sink[...] = total


def allreduce(x, sizes):
    shape = x.shape
    first, second = sizes[0], sizes[1] * sizes[2]
    return pl.pallas_call(
        lambda *refs: allreduce_kernel(sizes, *refs),
        out_shape=jax.ShapeDtypeStruct(shape, jnp.float32),
        in_specs=[pl.BlockSpec(memory_space=pltpu.VMEM)],
        out_specs=pl.BlockSpec(memory_space=pltpu.VMEM),
        scratch_shapes=[
            pltpu.VMEM((first,) + shape, jnp.float32),
            pltpu.VMEM((second,) + shape, jnp.float32),
            pltpu.VMEM(shape, jnp.float32),
            pltpu.SemaphoreType.DMA((first,)),
            pltpu.SemaphoreType.DMA((first,)),
            pltpu.SemaphoreType.DMA((second,)),
            pltpu.SemaphoreType.DMA((second,)),
        ],
        compiler_params=pltpu.CompilerParams(collective_id=0, has_side_effects=True),
    )(x)


def forward_kernel(rows, wide_y, w_ref, b_ref, q_ref, u_ref, wt_ref, p_ref, cot_ref,
                   pooled_ref, wg_ref, bg_ref, main_ref, edge_ref, wg_acc, bg_acc):
    step = pl.program_id(0)
    plane = p_ref.shape[0] // 2
    lines = plane // 4

    @pl.when(step == 0)
    def _():
        wg_acc[...] = jnp.zeros_like(wg_acc)
        bg_acc[...] = jnp.zeros_like(bg_acc)
        main_ref[...] = jnp.zeros_like(main_ref)
        edge_ref[...] = jnp.zeros_like(edge_ref)

    weight = w_ref[...]
    bias = b_ref[...]
    spread_w = wt_ref[...]
    slots = spread_w.shape[0] // 27
    lane = lax.broadcasted_iota(jnp.int32, (slots, rows), 1)
    first = lane == 0
    last = lane == rows - 1

    @pl.loop(0, lines)
    def _(j):
        cot = cot_ref[:, pl.ds(pl.multiple_of(j * rows, rows), rows)]
        ups = (
            jnp.dot(cot, u_ref[0], preferred_element_type=jnp.float32) * 0.125,
            jnp.dot(cot, u_ref[1], preferred_element_type=jnp.float32) * 0.125,
        )
        spread4 = jnp.concatenate([ups[0], ups[0], ups[1], ups[1]], axis=1)
        totals = [None, None]
        wg = None
        bg = None
        spreads = []
        for px, base in enumerate((0, plane)):
            patch = jnp.concatenate([p_ref[base + j * 4 + r] for r in range(4)], axis=1)
            preact = jnp.dot(weight, patch, preferred_element_type=jnp.float32) + bias
            scaled = soft_scale * preact
            e = jnp.exp(-jnp.abs(scaled))
            softplus = jnp.maximum(scaled, 0.0) + jnp.log1p(e)
            activated = leak_slope * preact + (1.0 - leak_slope) / soft_scale * softplus
            for half in range(2):
                pair = (
                    activated[:, 2 * half * rows : (2 * half + 1) * rows]
                    + activated[:, (2 * half + 1) * rows : (2 * half + 2) * rows]
                )
                totals[half] = pair if totals[half] is None else totals[half] + pair
            sigmoid = jnp.where(scaled >= 0.0, 1.0, e) / (1.0 + e)
            slope = leak_slope + (1.0 - leak_slope) * sigmoid
            delta = (slope * spread4).astype(jnp.bfloat16)
            term = lax.dot_general(
                delta, patch, (((1,), (1,)), ((), ())), preferred_element_type=jnp.float32
            )
            wg = term if wg is None else wg + term
            part = delta.astype(jnp.float32)
            bg = part if bg is None else bg + part
            spreads.append(jnp.dot(spread_w, delta, preferred_element_type=jnp.float32))
        acc_main = {}
        acc_edge = {}
        for px in range(2):
            for r in range(4):
                cols = slice(r * rows, (r + 1) * rows)
                for a in range(3):
                    for b in range(3):
                        at = (a * 3 + b) * 3 * slots
                        g = spreads[px]
                        v0 = pltpu.roll(g[at : at + slots, cols], rows - 1, 1)
                        v1 = g[at + slots : at + 2 * slots, cols]
                        v2 = pltpu.roll(g[at + 2 * slots : at + 3 * slots, cols], 1, 1)
                        inner = jnp.where(last, 0.0, v0) + v1 + jnp.where(first, 0.0, v2)
                        edge = jnp.where(last, v0, 0.0) + jnp.where(first, v2, 0.0)
                        key = (px + a, r + b)
                        if key in acc_main:
                            acc_main[key] = acc_main[key] + inner
                            acc_edge[key] = acc_edge[key] + edge
                        else:
                            acc_main[key] = inner
                            acc_edge[key] = edge
        for (dx, dy), value in acc_main.items():
            out = (step * 2 + dx) * wide_y + (j * 4 + dy)
            main_ref[out] += value[: main_ref.shape[1]]
            edge_ref[out] += acc_edge[dx, dy][: edge_ref.shape[1]]
        wg_acc[...] += wg
        bg_acc[...] += jnp.sum(bg, axis=1, keepdims=True)
        pooled = jnp.dot(
            totals[0], q_ref[0], preferred_element_type=jnp.float32, precision=lax.Precision.HIGHEST
        ) + jnp.dot(
            totals[1], q_ref[1], preferred_element_type=jnp.float32, precision=lax.Precision.HIGHEST
        )
        pooled_ref[:, pl.ds(pl.multiple_of(j * rows, rows), rows)] = (pooled * 0.125).astype(
            pooled_ref.dtype
        )

    @pl.when(step == pl.num_programs(0) - 1)
    def _():
        wg_ref[...] = wg_acc[...]
        bg_ref[...] = bg_acc[...]


def forward(weight, bias, patches, cot, pairs, wide_x, wide_y):
    lines, taps, rows = patches.shape
    chan_out, chan_in = weight.shape[:2]
    weight_mat = weight.reshape(chan_out, taps)
    slots = 8
    spread_w = jnp.transpose(weight, (2, 3, 4, 1, 0))
    spread_w = jnp.pad(spread_w, ((0, 0), (0, 0), (0, 0), (0, slots - chan_in), (0, 0)))
    spread_w = spread_w.reshape(27 * slots, chan_out)
    half = rows // 2
    z = jnp.arange(rows)
    k = jnp.arange(rows)
    pool = jnp.stack(
        [(k[None, :] == z[:, None] // 2), (k[None, :] == half + z[:, None] // 2)]
    ).astype(jnp.float32)
    spread = jnp.stack(
        [(z[None, :] // 2 == k[:, None]), (z[None, :] // 2 + half == k[:, None])]
    ).astype(jnp.bfloat16)
    full = lambda shape: pl.BlockSpec(shape, lambda p: (0,) * len(shape))
    block = lines // pairs
    acc_shape = (wide_x * wide_y, chan_in, rows)
    return pl.pallas_call(
        lambda *refs: forward_kernel(rows, wide_y, *refs),
        grid=(pairs,),
        out_shape=(
            jax.ShapeDtypeStruct(cot.shape, jnp.bfloat16),
            jax.ShapeDtypeStruct((chan_out, taps), jnp.float32),
            jax.ShapeDtypeStruct((chan_out, 1), jnp.float32),
            jax.ShapeDtypeStruct(acc_shape, jnp.float32),
            jax.ShapeDtypeStruct(acc_shape, jnp.float32),
        ),
        in_specs=[
            full((chan_out, taps)),
            full((chan_out, 1)),
            full((2, rows, rows)),
            full((2, rows, rows)),
            full((27 * slots, chan_out)),
            pl.BlockSpec((block, taps, rows), lambda p: (p, 0, 0)),
            pl.BlockSpec((chan_out, cot.shape[1] // pairs), lambda p: (0, p)),
        ],
        out_specs=(
            pl.BlockSpec((chan_out, cot.shape[1] // pairs), lambda p: (0, p)),
            full((chan_out, taps)),
            full((chan_out, 1)),
            full(acc_shape),
            full(acc_shape),
        ),
        scratch_shapes=[
            pltpu.VMEM((chan_out, taps), jnp.float32),
            pltpu.VMEM((chan_out, 1), jnp.float32),
        ],
    )(weight_mat, bias, pool, spread, spread_w, patches, cot)


def fold_halo(main, axis, dim, width):
    count = lax.axis_size(axis)
    size = main.shape[dim]
    head = lax.slice_in_dim(main, 0, width, axis=dim)
    tail = lax.slice_in_dim(main, size - width, size, axis=dim)
    from_left = lax.ppermute(tail, axis, [(i, (i + 1) % count) for i in range(count)])
    from_right = lax.ppermute(head, axis, [((i + 1) % count, i) for i in range(count)])
    inner = lax.slice_in_dim(main, width, size - width, axis=dim)
    inner_size = size - 2 * width
    start = [0] * main.ndim
    inner = lax.dynamic_update_slice(
        inner, lax.slice_in_dim(inner, 0, width, axis=dim) + from_left, start
    )
    start[dim] = inner_size - width
    inner = lax.dynamic_update_slice(
        inner, lax.slice_in_dim(inner, inner_size - width, inner_size, axis=dim) + from_right, start
    )
    return inner


def on_device(cells, weight, bias, cotangent):
    chan_in, cells_x, cells_y, cells_z = cells.shape
    chan_out = weight.shape[0]
    stencil = [
        (shift_a, shift_b, shift_e)
        for shift_a in range(3)
        for shift_b in range(3)
        for shift_e in range(3)
    ]
    widened = extended_all(cells)
    patches = jnp.stack(
        [
            jnp.transpose(
                widened[:, sa : sa + cells_x, sb : sb + cells_y, se : se + cells_z], (1, 2, 0, 3)
            )
            for sa, sb, se in stencil
        ],
        axis=3,
    )
    patches = patches.reshape(cells_x * cells_y, chan_in * 27, cells_z)
    cot = cotangent.reshape(chan_out, -1)
    wide_x, wide_y = cells_x + 2, cells_y + 2
    pooled, weight_local, bias_local, main, edge = forward(
        weight, bias.reshape(chan_out, 1), patches, cot, cells_x // 2, wide_x, wide_y
    )
    pooled = pooled.reshape(cotangent.shape)
    taps = chan_in * 27
    width = -(-(taps + 1) // 128) * 128
    partial = jnp.concatenate(
        [weight_local, bias_local, jnp.zeros((chan_out, width - taps - 1), jnp.float32)],
        axis=1,
    )
    sizes = tuple(lax.axis_size(a) for a in AXES)
    both = allreduce(partial, sizes)
    weight_grad = both[:, :taps].reshape(chan_out, chan_in, 3, 3, 3)
    bias_grad = both[:, taps]
    main = main.reshape(wide_x, wide_y, chan_in, cells_z)
    edge = edge.reshape(wide_x, wide_y, chan_in, cells_z)
    lo = edge[..., cells_z - 1 :]
    hi = edge[..., :1]
    count = lax.axis_size("gz")
    from_left = lax.ppermute(hi, "gz", [(i, (i + 1) % count) for i in range(count)])
    from_right = lax.ppermute(lo, "gz", [((i + 1) % count, i) for i in range(count)])
    main = jnp.concatenate(
        [
            main[..., :1] + from_left,
            main[..., 1 : cells_z - 1],
            main[..., cells_z - 1 :] + from_right,
        ],
        axis=3,
    )
    main = fold_halo(main, "gy", 1, 1)
    main = fold_halo(main, "gx", 0, 1)
    input_grad = jnp.transpose(main, (2, 0, 1, 3))
    return (pooled, weight_grad, bias_grad, input_grad)


def solution(mesh):
    in_specs = (P(None, "gx", "gy", "gz"), P(), P(), P(None, "gx", "gy", "gz"))
    out_specs = (P(None, "gx", "gy", "gz"), P(), P(), P(None, "gx", "gy", "gz"))
    return jax.shard_map(
        on_device, mesh=mesh, in_specs=in_specs, out_specs=out_specs, check_vma=False
    )
```

```python
import jax
import jax.numpy as jnp
from jax import lax
from jax.experimental import pallas as pl
from jax.experimental.pallas import tpu as pltpu
from jax.sharding import PartitionSpec as P

MESH = pl.DeviceIdType.MESH
AXES = ("gx", "gy", "gz")

leak_slope = 0.3
soft_scale = 10.0


def extended(cells, sides, width):
    for axis, dim in sides:
        count = lax.axis_size(axis)
        head = lax.slice_in_dim(cells, 0, width, axis=dim)
        tail = lax.slice_in_dim(cells, cells.shape[dim] - width, cells.shape[dim], axis=dim)
        cells = jnp.concatenate(
            [
                lax.ppermute(tail, axis, [(i, (i + 1) % count) for i in range(count)]),
                cells,
                lax.ppermute(head, axis, [((i + 1) % count, i) for i in range(count)]),
            ],
            axis=dim,
        )
    return cells


def allreduce_kernel(sizes, x_ref, o_ref, slots_a, slots_b, acc_a, send_a, recv_a, send_b, recv_b):
    me = tuple(lax.axis_index(a) for a in AXES)
    groups = (
        [(k,) for k in range(sizes[0])],
        [(k, m) for k in range(sizes[1]) for m in range(sizes[2])],
    )
    places = ((0,), (1, 2))

    def device(phase, member):
        coords = list(me)
        for axis, value in zip(places[phase], member):
            coords[axis] = value
        return tuple(coords)

    def rank(phase):
        out = 0
        for axis in places[phase]:
            out = out * sizes[axis] + me[axis]
        return out

    def member_of(phase, index):
        out = []
        for axis in reversed(places[phase]):
            out.append(lax.rem(index, sizes[axis]))
            index = index // sizes[axis]
        return tuple(reversed(out))

    barrier = pltpu.get_barrier_semaphore()
    count = 0
    for phase in range(2):
        n = len(groups[phase])
        for d in range(1, n):
            target = member_of(phase, lax.rem(rank(phase) + d, n))
            pl.semaphore_signal(barrier, inc=1, device_id=device(phase, target), device_id_type=MESH)
            count += 1
    pl.semaphore_wait(barrier, count)

    slots = (slots_a, slots_b)
    sends = (send_a, send_b)
    recvs = (recv_a, recv_b)
    sources = (x_ref, acc_a)
    sinks = (acc_a, o_ref)
    for phase in range(2):
        n = len(groups[phase])
        src, held, sink = sources[phase], slots[phase], sinks[phase]
        mine = rank(phase)
        copies = []
        for d in range(1, n):
            target = member_of(phase, lax.rem(mine + d, n))
            copy = pltpu.make_async_remote_copy(
                src_ref=src,
                dst_ref=held.at[mine],
                send_sem=sends[phase].at[d],
                recv_sem=recvs[phase].at[mine],
                device_id=device(phase, target),
                device_id_type=MESH,
            )
            copy.start()
            copies.append(copy)
        held[mine] = src[...]
        for d in range(1, n):
            origin = lax.rem(mine + n - d, n)
            incoming = pltpu.make_async_remote_copy(
                src_ref=src,
                dst_ref=held.at[origin],
                send_sem=sends[phase].at[d],
                recv_sem=recvs[phase].at[origin],
                device_id=device(phase, member_of(phase, origin)),
                device_id_type=MESH,
            )
            incoming.wait_recv()
        for copy in copies:
            copy.wait_send()
        total = held[0]
        for k in range(1, n):
            total = total + held[k]
        sink[...] = total


def allreduce(x, sizes):
    shape = x.shape
    first, second = sizes[0], sizes[1] * sizes[2]
    return pl.pallas_call(
        lambda *refs: allreduce_kernel(sizes, *refs),
        out_shape=jax.ShapeDtypeStruct(shape, jnp.float32),
        in_specs=[pl.BlockSpec(memory_space=pltpu.VMEM)],
        out_specs=pl.BlockSpec(memory_space=pltpu.VMEM),
        scratch_shapes=[
            pltpu.VMEM((first,) + shape, jnp.float32),
            pltpu.VMEM((second,) + shape, jnp.float32),
            pltpu.VMEM(shape, jnp.float32),
            pltpu.SemaphoreType.DMA((first,)),
            pltpu.SemaphoreType.DMA((first,)),
            pltpu.SemaphoreType.DMA((second,)),
            pltpu.SemaphoreType.DMA((second,)),
        ],
        compiler_params=pltpu.CompilerParams(collective_id=0, has_side_effects=True),
    )(x)


def forward_kernel(rows, wide_y, w_ref, b_ref, q_ref, u_ref, wt_ref, p_ref, cot_ref,
                   pooled_ref, wg_ref, bg_ref, main_ref, edge_ref, wg_acc, bg_acc):
    step = pl.program_id(0)
    plane = p_ref.shape[0] // 2
    lines = plane // 4

    @pl.when(step == 0)
    def _():
        wg_acc[...] = jnp.zeros_like(wg_acc)
        bg_acc[...] = jnp.zeros_like(bg_acc)
        main_ref[...] = jnp.zeros_like(main_ref)
        edge_ref[...] = jnp.zeros_like(edge_ref)

    weight = w_ref[...]
    bias = b_ref[...]
    spread_w = wt_ref[...]
    slots = spread_w.shape[0] // 27
    lane = lax.broadcasted_iota(jnp.int32, (slots, rows), 1)
    first = lane == 0
    last = lane == rows - 1

    group = 8
    pooled_rows = group // 2
    pieces = pooled_rows // 2

    @pl.loop(0, plane // group)
    def _(j):
        ups = []
        for m in range(pieces):
            cot = cot_ref[:, pl.ds(pl.multiple_of((j * pieces + m) * rows, rows), rows)]
            ups.append(jnp.dot(cot, u_ref[0], preferred_element_type=jnp.float32) * 0.125)
            ups.append(jnp.dot(cot, u_ref[1], preferred_element_type=jnp.float32) * 0.125)
        spread_all = jnp.concatenate([ups[r // 2] for r in range(group)], axis=1)
        totals = [None] * pooled_rows
        wg = None
        bg = None
        spreads = []
        for px, base in enumerate((0, plane)):
            patch = jnp.concatenate([p_ref[base + j * group + r] for r in range(group)], axis=1)
            preact = jnp.dot(weight, patch, preferred_element_type=jnp.float32) + bias
            scaled = soft_scale * preact
            e = jnp.exp(-jnp.abs(scaled))
            softplus = jnp.maximum(scaled, 0.0) + jnp.log1p(e)
            activated = leak_slope * preact + (1.0 - leak_slope) / soft_scale * softplus
            for h in range(pooled_rows):
                pair = (
                    activated[:, 2 * h * rows : (2 * h + 1) * rows]
                    + activated[:, (2 * h + 1) * rows : (2 * h + 2) * rows]
                )
                totals[h] = pair if totals[h] is None else totals[h] + pair
            sigmoid = jnp.where(scaled >= 0.0, 1.0, e) / (1.0 + e)
            slope = leak_slope + (1.0 - leak_slope) * sigmoid
            delta = (slope * spread_all).astype(jnp.bfloat16)
            term = lax.dot_general(
                delta, patch, (((1,), (1,)), ((), ())), preferred_element_type=jnp.float32
            )
            wg = term if wg is None else wg + term
            part = delta.astype(jnp.float32)
            bg = part if bg is None else bg + part
            spreads.append(jnp.dot(spread_w, delta, preferred_element_type=jnp.float32))
        acc_main = {}
        acc_edge = {}
        for px in range(2):
            for r in range(group):
                cols = slice(r * rows, (r + 1) * rows)
                for a in range(3):
                    for b in range(3):
                        at = (a * 3 + b) * 3 * slots
                        g = spreads[px]
                        v0 = pltpu.roll(g[at : at + slots, cols], rows - 1, 1)
                        v1 = g[at + slots : at + 2 * slots, cols]
                        v2 = pltpu.roll(g[at + 2 * slots : at + 3 * slots, cols], 1, 1)
                        inner = jnp.where(last, 0.0, v0) + v1 + jnp.where(first, 0.0, v2)
                        edge = jnp.where(last, v0, 0.0) + jnp.where(first, v2, 0.0)
                        key = (px + a, r + b)
                        if key in acc_main:
                            acc_main[key] = acc_main[key] + inner
                            acc_edge[key] = acc_edge[key] + edge
                        else:
                            acc_main[key] = inner
                            acc_edge[key] = edge
        for (dx, dy), value in acc_main.items():
            out = (step * 2 + dx) * wide_y + (j * group + dy)
            main_ref[out] += value[: main_ref.shape[1]]
            edge_ref[out] += acc_edge[dx, dy][: edge_ref.shape[1]]
        wg_acc[...] += wg
        bg_acc[...] += jnp.sum(bg, axis=1, keepdims=True)
        for m in range(pieces):
            pooled = jnp.dot(
                totals[2 * m], q_ref[0], preferred_element_type=jnp.float32,
                precision=lax.Precision.HIGHEST,
            ) + jnp.dot(
                totals[2 * m + 1], q_ref[1], preferred_element_type=jnp.float32,
                precision=lax.Precision.HIGHEST,
            )
            at = pl.multiple_of((j * pieces + m) * rows, rows)
            pooled_ref[:, pl.ds(at, rows)] = (pooled * 0.125).astype(pooled_ref.dtype)

    @pl.when(step == pl.num_programs(0) - 1)
    def _():
        wg_ref[...] = wg_acc[...]
        bg_ref[...] = bg_acc[...]


def forward(weight, bias, patches, cot, pairs, wide_x, wide_y):
    lines, taps, rows = patches.shape
    chan_out, chan_in = weight.shape[:2]
    weight_mat = weight.reshape(chan_out, taps)
    slots = 8
    spread_w = jnp.transpose(weight, (2, 3, 4, 1, 0))
    spread_w = jnp.pad(spread_w, ((0, 0), (0, 0), (0, 0), (0, slots - chan_in), (0, 0)))
    spread_w = spread_w.reshape(27 * slots, chan_out)
    half = rows // 2
    z = jnp.arange(rows)
    k = jnp.arange(rows)
    pool = jnp.stack(
        [(k[None, :] == z[:, None] // 2), (k[None, :] == half + z[:, None] // 2)]
    ).astype(jnp.float32)
    spread = jnp.stack(
        [(z[None, :] // 2 == k[:, None]), (z[None, :] // 2 + half == k[:, None])]
    ).astype(jnp.bfloat16)
    full = lambda shape: pl.BlockSpec(shape, lambda p: (0,) * len(shape))
    block = lines // pairs
    acc_shape = (wide_x * wide_y, chan_in, rows)
    return pl.pallas_call(
        lambda *refs: forward_kernel(rows, wide_y, *refs),
        grid=(pairs,),
        out_shape=(
            jax.ShapeDtypeStruct(cot.shape, jnp.bfloat16),
            jax.ShapeDtypeStruct((chan_out, taps), jnp.float32),
            jax.ShapeDtypeStruct((chan_out, 1), jnp.float32),
            jax.ShapeDtypeStruct(acc_shape, jnp.float32),
            jax.ShapeDtypeStruct(acc_shape, jnp.float32),
        ),
        in_specs=[
            full((chan_out, taps)),
            full((chan_out, 1)),
            full((2, rows, rows)),
            full((2, rows, rows)),
            full((27 * slots, chan_out)),
            pl.BlockSpec((block, taps, rows), lambda p: (p, 0, 0)),
            pl.BlockSpec((chan_out, cot.shape[1] // pairs), lambda p: (0, p)),
        ],
        out_specs=(
            pl.BlockSpec((chan_out, cot.shape[1] // pairs), lambda p: (0, p)),
            full((chan_out, taps)),
            full((chan_out, 1)),
            full(acc_shape),
            full(acc_shape),
        ),
        scratch_shapes=[
            pltpu.VMEM((chan_out, taps), jnp.float32),
            pltpu.VMEM((chan_out, 1), jnp.float32),
        ],
    )(weight_mat, bias, pool, spread, spread_w, patches, cot)


def fold_halo(main, axis, dim, width):
    count = lax.axis_size(axis)
    size = main.shape[dim]
    head = lax.slice_in_dim(main, 0, width, axis=dim)
    tail = lax.slice_in_dim(main, size - width, size, axis=dim)
    from_left = lax.ppermute(tail, axis, [(i, (i + 1) % count) for i in range(count)])
    from_right = lax.ppermute(head, axis, [((i + 1) % count, i) for i in range(count)])
    inner = lax.slice_in_dim(main, width, size - width, axis=dim)
    inner_size = size - 2 * width
    start = [0] * main.ndim
    inner = lax.dynamic_update_slice(
        inner, lax.slice_in_dim(inner, 0, width, axis=dim) + from_left, start
    )
    start[dim] = inner_size - width
    inner = lax.dynamic_update_slice(
        inner, lax.slice_in_dim(inner, inner_size - width, inner_size, axis=dim) + from_right, start
    )
    return inner


def on_device(cells, weight, bias, cotangent):
    chan_in, cells_x, cells_y, cells_z = cells.shape
    chan_out = weight.shape[0]
    stencil = [
        (shift_a, shift_b, shift_e)
        for shift_a in range(3)
        for shift_b in range(3)
        for shift_e in range(3)
    ]
    widened = extended(cells, (("gx", 1), ("gy", 2), ("gz", 3)), 1)
    patches = jnp.stack(
        [
            jnp.transpose(
                widened[:, sa : sa + cells_x, sb : sb + cells_y, se : se + cells_z], (1, 2, 0, 3)
            )
            for sa, sb, se in stencil
        ],
        axis=3,
    )
    patches = patches.reshape(cells_x * cells_y, chan_in * 27, cells_z)
    cot = cotangent.reshape(chan_out, -1)
    wide_x, wide_y = cells_x + 2, cells_y + 2
    pooled, weight_local, bias_local, main, edge = forward(
        weight, bias.reshape(chan_out, 1), patches, cot, cells_x // 2, wide_x, wide_y
    )
    pooled = pooled.reshape(cotangent.shape)
    taps = chan_in * 27
    width = -(-(taps + 1) // 128) * 128
    partial = jnp.concatenate(
        [weight_local, bias_local, jnp.zeros((chan_out, width - taps - 1), jnp.float32)],
        axis=1,
    )
    sizes = tuple(lax.axis_size(a) for a in AXES)
    both = allreduce(partial, sizes)
    weight_grad = both[:, :taps].reshape(chan_out, chan_in, 3, 3, 3)
    bias_grad = both[:, taps]
    main = main.reshape(wide_x, wide_y, chan_in, cells_z)
    edge = edge.reshape(wide_x, wide_y, chan_in, cells_z)
    lo = edge[..., cells_z - 1 :]
    hi = edge[..., :1]
    count = lax.axis_size("gz")
    from_left = lax.ppermute(hi, "gz", [(i, (i + 1) % count) for i in range(count)])
    from_right = lax.ppermute(lo, "gz", [((i + 1) % count, i) for i in range(count)])
    main = jnp.concatenate(
        [
            main[..., :1] + from_left,
            main[..., 1 : cells_z - 1],
            main[..., cells_z - 1 :] + from_right,
        ],
        axis=3,
    )
    main = fold_halo(main, "gy", 1, 1)
    main = fold_halo(main, "gx", 0, 1)
    input_grad = jnp.transpose(main, (2, 0, 1, 3))
    return (pooled, weight_grad, bias_grad, input_grad)


def solution(mesh):
    in_specs = (P(None, "gx", "gy", "gz"), P(), P(), P(None, "gx", "gy", "gz"))
    out_specs = (P(None, "gx", "gy", "gz"), P(), P(), P(None, "gx", "gy", "gz"))
    return jax.shard_map(
        on_device, mesh=mesh, in_specs=in_specs, out_specs=out_specs, check_vma=False
    )
```

```python
import jax
import jax.numpy as jnp
from jax import lax
from jax.experimental import pallas as pl
from jax.experimental.pallas import tpu as pltpu
from jax.sharding import PartitionSpec as P

MESH = pl.DeviceIdType.MESH
AXES = ("gx", "gy", "gz")

leak_slope = 0.3
soft_scale = 10.0


def extended(cells, sides, width):
    for axis, dim in sides:
        count = lax.axis_size(axis)
        head = lax.slice_in_dim(cells, 0, width, axis=dim)
        tail = lax.slice_in_dim(cells, cells.shape[dim] - width, cells.shape[dim], axis=dim)
        cells = jnp.concatenate(
            [
                lax.ppermute(tail, axis, [(i, (i + 1) % count) for i in range(count)]),
                cells,
                lax.ppermute(head, axis, [((i + 1) % count, i) for i in range(count)]),
            ],
            axis=dim,
        )
    return cells


def allreduce_kernel(sizes, x_ref, o_ref, slots_a, slots_b, acc_a, send_a, recv_a, send_b, recv_b):
    me = tuple(lax.axis_index(a) for a in AXES)
    groups = (
        [(k,) for k in range(sizes[0])],
        [(k, m) for k in range(sizes[1]) for m in range(sizes[2])],
    )
    places = ((0,), (1, 2))

    def device(phase, member):
        coords = list(me)
        for axis, value in zip(places[phase], member):
            coords[axis] = value
        return tuple(coords)

    def rank(phase):
        out = 0
        for axis in places[phase]:
            out = out * sizes[axis] + me[axis]
        return out

    def member_of(phase, index):
        out = []
        for axis in reversed(places[phase]):
            out.append(lax.rem(index, sizes[axis]))
            index = index // sizes[axis]
        return tuple(reversed(out))

    barrier = pltpu.get_barrier_semaphore()
    count = 0
    for phase in range(2):
        n = len(groups[phase])
        for d in range(1, n):
            target = member_of(phase, lax.rem(rank(phase) + d, n))
            pl.semaphore_signal(barrier, inc=1, device_id=device(phase, target), device_id_type=MESH)
            count += 1
    pl.semaphore_wait(barrier, count)

    slots = (slots_a, slots_b)
    sends = (send_a, send_b)
    recvs = (recv_a, recv_b)
    sources = (x_ref, acc_a)
    sinks = (acc_a, o_ref)
    for phase in range(2):
        n = len(groups[phase])
        src, held, sink = sources[phase], slots[phase], sinks[phase]
        mine = rank(phase)
        copies = []
        for d in range(1, n):
            target = member_of(phase, lax.rem(mine + d, n))
            copy = pltpu.make_async_remote_copy(
                src_ref=src,
                dst_ref=held.at[mine],
                send_sem=sends[phase].at[d],
                recv_sem=recvs[phase].at[mine],
                device_id=device(phase, target),
                device_id_type=MESH,
            )
            copy.start()
            copies.append(copy)
        held[mine] = src[...]
        for d in range(1, n):
            origin = lax.rem(mine + n - d, n)
            incoming = pltpu.make_async_remote_copy(
                src_ref=src,
                dst_ref=held.at[origin],
                send_sem=sends[phase].at[d],
                recv_sem=recvs[phase].at[origin],
                device_id=device(phase, member_of(phase, origin)),
                device_id_type=MESH,
            )
            incoming.wait_recv()
        for copy in copies:
            copy.wait_send()
        total = held[0]
        for k in range(1, n):
            total = total + held[k]
        sink[...] = total


def allreduce(x, sizes):
    shape = x.shape
    first, second = sizes[0], sizes[1] * sizes[2]
    return pl.pallas_call(
        lambda *refs: allreduce_kernel(sizes, *refs),
        out_shape=jax.ShapeDtypeStruct(shape, jnp.float32),
        in_specs=[pl.BlockSpec(memory_space=pltpu.VMEM)],
        out_specs=pl.BlockSpec(memory_space=pltpu.VMEM),
        scratch_shapes=[
            pltpu.VMEM((first,) + shape, jnp.float32),
            pltpu.VMEM((second,) + shape, jnp.float32),
            pltpu.VMEM(shape, jnp.float32),
            pltpu.SemaphoreType.DMA((first,)),
            pltpu.SemaphoreType.DMA((first,)),
            pltpu.SemaphoreType.DMA((second,)),
            pltpu.SemaphoreType.DMA((second,)),
        ],
        compiler_params=pltpu.CompilerParams(collective_id=0, has_side_effects=True),
    )(x)


def forward_kernel(rows, wide_y, w_ref, b_ref, q_ref, u_ref, wt_ref, p_ref, cot_ref,
                   pooled_ref, wg_ref, bg_ref, main_ref, edge_ref, wg_acc, bg_acc):
    step = pl.program_id(0)
    plane = p_ref.shape[0] // 2
    lines = plane // 4

    @pl.when(step == 0)
    def _():
        wg_acc[...] = jnp.zeros_like(wg_acc)
        bg_acc[...] = jnp.zeros_like(bg_acc)
        main_ref[...] = jnp.zeros_like(main_ref)
        edge_ref[...] = jnp.zeros_like(edge_ref)

    weight = w_ref[...]
    bias = b_ref[...]
    spread_w = wt_ref[...]
    slots = spread_w.shape[0] // 27
    lane = lax.broadcasted_iota(jnp.int32, (slots, rows), 1)
    first = lane == 0
    last = lane == rows - 1

    group = 16
    pooled_rows = group // 2
    pieces = pooled_rows // 2

    @pl.loop(0, plane // group)
    def _(j):
        ups = []
        for m in range(pieces):
            cot = cot_ref[:, pl.ds(pl.multiple_of((j * pieces + m) * rows, rows), rows)]
            ups.append(jnp.dot(cot, u_ref[0], preferred_element_type=jnp.float32) * 0.125)
            ups.append(jnp.dot(cot, u_ref[1], preferred_element_type=jnp.float32) * 0.125)
        spread_all = jnp.concatenate([ups[r // 2] for r in range(group)], axis=1)
        totals = [None] * pooled_rows
        wg = None
        bg = None
        spreads = []
        for px, base in enumerate((0, plane)):
            patch = jnp.concatenate([p_ref[base + j * group + r] for r in range(group)], axis=1)
            preact = jnp.dot(weight, patch, preferred_element_type=jnp.float32) + bias
            scaled = soft_scale * preact
            e = jnp.exp(-jnp.abs(scaled))
            softplus = jnp.maximum(scaled, 0.0) + jnp.log1p(e)
            activated = leak_slope * preact + (1.0 - leak_slope) / soft_scale * softplus
            for h in range(pooled_rows):
                pair = (
                    activated[:, 2 * h * rows : (2 * h + 1) * rows]
                    + activated[:, (2 * h + 1) * rows : (2 * h + 2) * rows]
                )
                totals[h] = pair if totals[h] is None else totals[h] + pair
            sigmoid = jnp.where(scaled >= 0.0, 1.0, e) / (1.0 + e)
            slope = leak_slope + (1.0 - leak_slope) * sigmoid
            delta = (slope * spread_all).astype(jnp.bfloat16)
            term = lax.dot_general(
                delta, patch, (((1,), (1,)), ((), ())), preferred_element_type=jnp.float32
            )
            wg = term if wg is None else wg + term
            part = delta.astype(jnp.float32)
            bg = part if bg is None else bg + part
            spreads.append(jnp.dot(spread_w, delta, preferred_element_type=jnp.float32))
        acc_main = {}
        acc_edge = {}
        for px in range(2):
            for r in range(group):
                cols = slice(r * rows, (r + 1) * rows)
                for a in range(3):
                    for b in range(3):
                        at = (a * 3 + b) * 3 * slots
                        g = spreads[px]
                        v0 = pltpu.roll(g[at : at + slots, cols], rows - 1, 1)
                        v1 = g[at + slots : at + 2 * slots, cols]
                        v2 = pltpu.roll(g[at + 2 * slots : at + 3 * slots, cols], 1, 1)
                        inner = jnp.where(last, 0.0, v0) + v1 + jnp.where(first, 0.0, v2)
                        edge = jnp.where(last, v0, 0.0) + jnp.where(first, v2, 0.0)
                        key = (px + a, r + b)
                        if key in acc_main:
                            acc_main[key] = acc_main[key] + inner
                            acc_edge[key] = acc_edge[key] + edge
                        else:
                            acc_main[key] = inner
                            acc_edge[key] = edge
        for (dx, dy), value in acc_main.items():
            out = (step * 2 + dx) * wide_y + (j * group + dy)
            main_ref[out] += value[: main_ref.shape[1]]
            edge_ref[out] += acc_edge[dx, dy][: edge_ref.shape[1]]
        wg_acc[...] += wg
        bg_acc[...] += jnp.sum(bg, axis=1, keepdims=True)
        for m in range(pieces):
            pooled = jnp.dot(
                totals[2 * m], q_ref[0], preferred_element_type=jnp.float32,
                precision=lax.Precision.HIGHEST,
            ) + jnp.dot(
                totals[2 * m + 1], q_ref[1], preferred_element_type=jnp.float32,
                precision=lax.Precision.HIGHEST,
            )
            at = pl.multiple_of((j * pieces + m) * rows, rows)
            pooled_ref[:, pl.ds(at, rows)] = (pooled * 0.125).astype(pooled_ref.dtype)

    @pl.when(step == pl.num_programs(0) - 1)
    def _():
        wg_ref[...] = wg_acc[...]
        bg_ref[...] = bg_acc[...]


def forward(weight, bias, patches, cot, pairs, wide_x, wide_y):
    lines, taps, rows = patches.shape
    chan_out, chan_in = weight.shape[:2]
    weight_mat = weight.reshape(chan_out, taps)
    slots = 8
    spread_w = jnp.transpose(weight, (2, 3, 4, 1, 0))
    spread_w = jnp.pad(spread_w, ((0, 0), (0, 0), (0, 0), (0, slots - chan_in), (0, 0)))
    spread_w = spread_w.reshape(27 * slots, chan_out)
    half = rows // 2
    z = jnp.arange(rows)
    k = jnp.arange(rows)
    pool = jnp.stack(
        [(k[None, :] == z[:, None] // 2), (k[None, :] == half + z[:, None] // 2)]
    ).astype(jnp.float32)
    spread = jnp.stack(
        [(z[None, :] // 2 == k[:, None]), (z[None, :] // 2 + half == k[:, None])]
    ).astype(jnp.bfloat16)
    full = lambda shape: pl.BlockSpec(shape, lambda p: (0,) * len(shape))
    block = lines // pairs
    acc_shape = (wide_x * wide_y, chan_in, rows)
    return pl.pallas_call(
        lambda *refs: forward_kernel(rows, wide_y, *refs),
        grid=(pairs,),
        out_shape=(
            jax.ShapeDtypeStruct(cot.shape, jnp.bfloat16),
            jax.ShapeDtypeStruct((chan_out, taps), jnp.float32),
            jax.ShapeDtypeStruct((chan_out, 1), jnp.float32),
            jax.ShapeDtypeStruct(acc_shape, jnp.float32),
            jax.ShapeDtypeStruct(acc_shape, jnp.float32),
        ),
        in_specs=[
            full((chan_out, taps)),
            full((chan_out, 1)),
            full((2, rows, rows)),
            full((2, rows, rows)),
            full((27 * slots, chan_out)),
            pl.BlockSpec((block, taps, rows), lambda p: (p, 0, 0)),
            pl.BlockSpec((chan_out, cot.shape[1] // pairs), lambda p: (0, p)),
        ],
        out_specs=(
            pl.BlockSpec((chan_out, cot.shape[1] // pairs), lambda p: (0, p)),
            full((chan_out, taps)),
            full((chan_out, 1)),
            full(acc_shape),
            full(acc_shape),
        ),
        scratch_shapes=[
            pltpu.VMEM((chan_out, taps), jnp.float32),
            pltpu.VMEM((chan_out, 1), jnp.float32),
        ],
    )(weight_mat, bias, pool, spread, spread_w, patches, cot)


def fold_halo(main, axis, dim, width):
    count = lax.axis_size(axis)
    size = main.shape[dim]
    head = lax.slice_in_dim(main, 0, width, axis=dim)
    tail = lax.slice_in_dim(main, size - width, size, axis=dim)
    from_left = lax.ppermute(tail, axis, [(i, (i + 1) % count) for i in range(count)])
    from_right = lax.ppermute(head, axis, [((i + 1) % count, i) for i in range(count)])
    inner = lax.slice_in_dim(main, width, size - width, axis=dim)
    inner_size = size - 2 * width
    start = [0] * main.ndim
    inner = lax.dynamic_update_slice(
        inner, lax.slice_in_dim(inner, 0, width, axis=dim) + from_left, start
    )
    start[dim] = inner_size - width
    inner = lax.dynamic_update_slice(
        inner, lax.slice_in_dim(inner, inner_size - width, inner_size, axis=dim) + from_right, start
    )
    return inner


def on_device(cells, weight, bias, cotangent):
    chan_in, cells_x, cells_y, cells_z = cells.shape
    chan_out = weight.shape[0]
    stencil = [
        (shift_a, shift_b, shift_e)
        for shift_a in range(3)
        for shift_b in range(3)
        for shift_e in range(3)
    ]
    widened = extended(cells, (("gx", 1), ("gy", 2), ("gz", 3)), 1)
    patches = jnp.stack(
        [
            jnp.transpose(
                widened[:, sa : sa + cells_x, sb : sb + cells_y, se : se + cells_z], (1, 2, 0, 3)
            )
            for sa, sb, se in stencil
        ],
        axis=3,
    )
    patches = patches.reshape(cells_x * cells_y, chan_in * 27, cells_z)
    cot = cotangent.reshape(chan_out, -1)
    wide_x, wide_y = cells_x + 2, cells_y + 2
    pooled, weight_local, bias_local, main, edge = forward(
        weight, bias.reshape(chan_out, 1), patches, cot, cells_x // 2, wide_x, wide_y
    )
    pooled = pooled.reshape(cotangent.shape)
    taps = chan_in * 27
    width = -(-(taps + 1) // 128) * 128
    partial = jnp.concatenate(
        [weight_local, bias_local, jnp.zeros((chan_out, width - taps - 1), jnp.float32)],
        axis=1,
    )
    sizes = tuple(lax.axis_size(a) for a in AXES)
    both = allreduce(partial, sizes)
    weight_grad = both[:, :taps].reshape(chan_out, chan_in, 3, 3, 3)
    bias_grad = both[:, taps]
    main = main.reshape(wide_x, wide_y, chan_in, cells_z)
    edge = edge.reshape(wide_x, wide_y, chan_in, cells_z)
    lo = edge[..., cells_z - 1 :]
    hi = edge[..., :1]
    count = lax.axis_size("gz")
    from_left = lax.ppermute(hi, "gz", [(i, (i + 1) % count) for i in range(count)])
    from_right = lax.ppermute(lo, "gz", [((i + 1) % count, i) for i in range(count)])
    main = jnp.concatenate(
        [
            main[..., :1] + from_left,
            main[..., 1 : cells_z - 1],
            main[..., cells_z - 1 :] + from_right,
        ],
        axis=3,
    )
    main = fold_halo(main, "gy", 1, 1)
    main = fold_halo(main, "gx", 0, 1)
    input_grad = jnp.transpose(main, (2, 0, 1, 3))
    return (pooled, weight_grad, bias_grad, input_grad)


def solution(mesh):
    in_specs = (P(None, "gx", "gy", "gz"), P(), P(), P(None, "gx", "gy", "gz"))
    out_specs = (P(None, "gx", "gy", "gz"), P(), P(), P(None, "gx", "gy", "gz"))
    return jax.shard_map(
        on_device, mesh=mesh, in_specs=in_specs, out_specs=out_specs, check_vma=False
    )
```

```python
import jax
import jax.numpy as jnp
from jax import lax
from jax.experimental import pallas as pl
from jax.experimental.pallas import tpu as pltpu
from jax.sharding import PartitionSpec as P

MESH = pl.DeviceIdType.MESH
AXES = ("gx", "gy", "gz")

leak_slope = 0.3
soft_scale = 10.0


def extended(cells, sides, width):
    for axis, dim in sides:
        count = lax.axis_size(axis)
        head = lax.slice_in_dim(cells, 0, width, axis=dim)
        tail = lax.slice_in_dim(cells, cells.shape[dim] - width, cells.shape[dim], axis=dim)
        cells = jnp.concatenate(
            [
                lax.ppermute(tail, axis, [(i, (i + 1) % count) for i in range(count)]),
                cells,
                lax.ppermute(head, axis, [((i + 1) % count, i) for i in range(count)]),
            ],
            axis=dim,
        )
    return cells


def allreduce_kernel(sizes, x_ref, o_ref, slots_a, slots_b, acc_a, send_a, recv_a, send_b, recv_b):
    me = tuple(lax.axis_index(a) for a in AXES)
    groups = (
        [(k,) for k in range(sizes[0])],
        [(k, m) for k in range(sizes[1]) for m in range(sizes[2])],
    )
    places = ((0,), (1, 2))

    def device(phase, member):
        coords = list(me)
        for axis, value in zip(places[phase], member):
            coords[axis] = value
        return tuple(coords)

    def rank(phase):
        out = 0
        for axis in places[phase]:
            out = out * sizes[axis] + me[axis]
        return out

    def member_of(phase, index):
        out = []
        for axis in reversed(places[phase]):
            out.append(lax.rem(index, sizes[axis]))
            index = index // sizes[axis]
        return tuple(reversed(out))

    barrier = pltpu.get_barrier_semaphore()
    count = 0
    for phase in range(2):
        n = len(groups[phase])
        for d in range(1, n):
            target = member_of(phase, lax.rem(rank(phase) + d, n))
            pl.semaphore_signal(barrier, inc=1, device_id=device(phase, target), device_id_type=MESH)
            count += 1
    pl.semaphore_wait(barrier, count)

    slots = (slots_a, slots_b)
    sends = (send_a, send_b)
    recvs = (recv_a, recv_b)
    sources = (x_ref, acc_a)
    sinks = (acc_a, o_ref)
    for phase in range(2):
        n = len(groups[phase])
        src, held, sink = sources[phase], slots[phase], sinks[phase]
        mine = rank(phase)
        copies = []
        for d in range(1, n):
            target = member_of(phase, lax.rem(mine + d, n))
            copy = pltpu.make_async_remote_copy(
                src_ref=src,
                dst_ref=held.at[mine],
                send_sem=sends[phase].at[d],
                recv_sem=recvs[phase].at[mine],
                device_id=device(phase, target),
                device_id_type=MESH,
            )
            copy.start()
            copies.append(copy)
        held[mine] = src[...]
        for d in range(1, n):
            origin = lax.rem(mine + n - d, n)
            incoming = pltpu.make_async_remote_copy(
                src_ref=src,
                dst_ref=held.at[origin],
                send_sem=sends[phase].at[d],
                recv_sem=recvs[phase].at[origin],
                device_id=device(phase, member_of(phase, origin)),
                device_id_type=MESH,
            )
            incoming.wait_recv()
        for copy in copies:
            copy.wait_send()
        total = held[0]
        for k in range(1, n):
            total = total + held[k]
        sink[...] = total


def allreduce(x, sizes):
    shape = x.shape
    first, second = sizes[0], sizes[1] * sizes[2]
    return pl.pallas_call(
        lambda *refs: allreduce_kernel(sizes, *refs),
        out_shape=jax.ShapeDtypeStruct(shape, jnp.float32),
        in_specs=[pl.BlockSpec(memory_space=pltpu.VMEM)],
        out_specs=pl.BlockSpec(memory_space=pltpu.VMEM),
        scratch_shapes=[
            pltpu.VMEM((first,) + shape, jnp.float32),
            pltpu.VMEM((second,) + shape, jnp.float32),
            pltpu.VMEM(shape, jnp.float32),
            pltpu.SemaphoreType.DMA((first,)),
            pltpu.SemaphoreType.DMA((first,)),
            pltpu.SemaphoreType.DMA((second,)),
            pltpu.SemaphoreType.DMA((second,)),
        ],
        compiler_params=pltpu.CompilerParams(collective_id=0, has_side_effects=True),
    )(x)


def forward_kernel(rows, wide_y, w_ref, b_ref, q_ref, u_ref, wt_ref, p_ref, cot_ref,
                   pooled_ref, wg_ref, bg_ref, main_ref, edge_ref, wg_acc, bg_acc):
    step = pl.program_id(0)
    plane = p_ref.shape[0] // 2
    lines = plane // 4

    @pl.when(step == 0)
    def _():
        wg_acc[...] = jnp.zeros_like(wg_acc)
        bg_acc[...] = jnp.zeros_like(bg_acc)
        main_ref[...] = jnp.zeros_like(main_ref)
        edge_ref[...] = jnp.zeros_like(edge_ref)

    weight = w_ref[...]
    bias = b_ref[...]
    spread_w = wt_ref[...]
    slots = spread_w.shape[0] // 27
    lane = lax.broadcasted_iota(jnp.int32, (slots, rows), 1)
    first = lane == 0
    last = lane == rows - 1

    group = 32
    pooled_rows = group // 2
    pieces = pooled_rows // 2

    @pl.loop(0, plane // group)
    def _(j):
        ups = []
        for m in range(pieces):
            cot = cot_ref[:, pl.ds(pl.multiple_of((j * pieces + m) * rows, rows), rows)]
            ups.append(jnp.dot(cot, u_ref[0], preferred_element_type=jnp.float32) * 0.125)
            ups.append(jnp.dot(cot, u_ref[1], preferred_element_type=jnp.float32) * 0.125)
        spread_all = jnp.concatenate([ups[r // 2] for r in range(group)], axis=1)
        totals = [None] * pooled_rows
        wg = None
        bg = None
        spreads = []
        for px, base in enumerate((0, plane)):
            patch = jnp.concatenate([p_ref[base + j * group + r] for r in range(group)], axis=1)
            preact = jnp.dot(weight, patch, preferred_element_type=jnp.float32) + bias
            scaled = soft_scale * preact
            e = jnp.exp(-jnp.abs(scaled))
            softplus = jnp.maximum(scaled, 0.0) + jnp.log1p(e)
            activated = leak_slope * preact + (1.0 - leak_slope) / soft_scale * softplus
            for h in range(pooled_rows):
                pair = (
                    activated[:, 2 * h * rows : (2 * h + 1) * rows]
                    + activated[:, (2 * h + 1) * rows : (2 * h + 2) * rows]
                )
                totals[h] = pair if totals[h] is None else totals[h] + pair
            sigmoid = jnp.where(scaled >= 0.0, 1.0, e) / (1.0 + e)
            slope = leak_slope + (1.0 - leak_slope) * sigmoid
            delta = (slope * spread_all).astype(jnp.bfloat16)
            term = lax.dot_general(
                delta, patch, (((1,), (1,)), ((), ())), preferred_element_type=jnp.float32
            )
            wg = term if wg is None else wg + term
            part = delta.astype(jnp.float32)
            bg = part if bg is None else bg + part
            spreads.append(jnp.dot(spread_w, delta, preferred_element_type=jnp.float32))
        acc_main = {}
        acc_edge = {}
        for px in range(2):
            for r in range(group):
                cols = slice(r * rows, (r + 1) * rows)
                for a in range(3):
                    for b in range(3):
                        at = (a * 3 + b) * 3 * slots
                        g = spreads[px]
                        v0 = pltpu.roll(g[at : at + slots, cols], rows - 1, 1)
                        v1 = g[at + slots : at + 2 * slots, cols]
                        v2 = pltpu.roll(g[at + 2 * slots : at + 3 * slots, cols], 1, 1)
                        inner = jnp.where(last, 0.0, v0) + v1 + jnp.where(first, 0.0, v2)
                        edge = jnp.where(last, v0, 0.0) + jnp.where(first, v2, 0.0)
                        key = (px + a, r + b)
                        if key in acc_main:
                            acc_main[key] = acc_main[key] + inner
                            acc_edge[key] = acc_edge[key] + edge
                        else:
                            acc_main[key] = inner
                            acc_edge[key] = edge
        for (dx, dy), value in acc_main.items():
            out = (step * 2 + dx) * wide_y + (j * group + dy)
            main_ref[out] += value[: main_ref.shape[1]]
            edge_ref[out] += acc_edge[dx, dy][: edge_ref.shape[1]]
        wg_acc[...] += wg
        bg_acc[...] += jnp.sum(bg, axis=1, keepdims=True)
        for m in range(pieces):
            pooled = jnp.dot(
                totals[2 * m], q_ref[0], preferred_element_type=jnp.float32,
                precision=lax.Precision.HIGHEST,
            ) + jnp.dot(
                totals[2 * m + 1], q_ref[1], preferred_element_type=jnp.float32,
                precision=lax.Precision.HIGHEST,
            )
            at = pl.multiple_of((j * pieces + m) * rows, rows)
            pooled_ref[:, pl.ds(at, rows)] = (pooled * 0.125).astype(pooled_ref.dtype)

    @pl.when(step == pl.num_programs(0) - 1)
    def _():
        wg_ref[...] = wg_acc[...]
        bg_ref[...] = bg_acc[...]


def forward(weight, bias, patches, cot, pairs, wide_x, wide_y):
    lines, taps, rows = patches.shape
    chan_out, chan_in = weight.shape[:2]
    weight_mat = weight.reshape(chan_out, taps)
    slots = 8
    spread_w = jnp.transpose(weight, (2, 3, 4, 1, 0))
    spread_w = jnp.pad(spread_w, ((0, 0), (0, 0), (0, 0), (0, slots - chan_in), (0, 0)))
    spread_w = spread_w.reshape(27 * slots, chan_out)
    half = rows // 2
    z = jnp.arange(rows)
    k = jnp.arange(rows)
    pool = jnp.stack(
        [(k[None, :] == z[:, None] // 2), (k[None, :] == half + z[:, None] // 2)]
    ).astype(jnp.float32)
    spread = jnp.stack(
        [(z[None, :] // 2 == k[:, None]), (z[None, :] // 2 + half == k[:, None])]
    ).astype(jnp.bfloat16)
    full = lambda shape: pl.BlockSpec(shape, lambda p: (0,) * len(shape))
    block = lines // pairs
    acc_shape = (wide_x * wide_y, chan_in, rows)
    return pl.pallas_call(
        lambda *refs: forward_kernel(rows, wide_y, *refs),
        grid=(pairs,),
        out_shape=(
            jax.ShapeDtypeStruct(cot.shape, jnp.bfloat16),
            jax.ShapeDtypeStruct((chan_out, taps), jnp.float32),
            jax.ShapeDtypeStruct((chan_out, 1), jnp.float32),
            jax.ShapeDtypeStruct(acc_shape, jnp.float32),
            jax.ShapeDtypeStruct(acc_shape, jnp.float32),
        ),
        in_specs=[
            full((chan_out, taps)),
            full((chan_out, 1)),
            full((2, rows, rows)),
            full((2, rows, rows)),
            full((27 * slots, chan_out)),
            pl.BlockSpec((block, taps, rows), lambda p: (p, 0, 0)),
            pl.BlockSpec((chan_out, cot.shape[1] // pairs), lambda p: (0, p)),
        ],
        out_specs=(
            pl.BlockSpec((chan_out, cot.shape[1] // pairs), lambda p: (0, p)),
            full((chan_out, taps)),
            full((chan_out, 1)),
            full(acc_shape),
            full(acc_shape),
        ),
        scratch_shapes=[
            pltpu.VMEM((chan_out, taps), jnp.float32),
            pltpu.VMEM((chan_out, 1), jnp.float32),
        ],
    )(weight_mat, bias, pool, spread, spread_w, patches, cot)


def fold_halo(main, axis, dim, width):
    count = lax.axis_size(axis)
    size = main.shape[dim]
    head = lax.slice_in_dim(main, 0, width, axis=dim)
    tail = lax.slice_in_dim(main, size - width, size, axis=dim)
    from_left = lax.ppermute(tail, axis, [(i, (i + 1) % count) for i in range(count)])
    from_right = lax.ppermute(head, axis, [((i + 1) % count, i) for i in range(count)])
    inner = lax.slice_in_dim(main, width, size - width, axis=dim)
    inner_size = size - 2 * width
    start = [0] * main.ndim
    inner = lax.dynamic_update_slice(
        inner, lax.slice_in_dim(inner, 0, width, axis=dim) + from_left, start
    )
    start[dim] = inner_size - width
    inner = lax.dynamic_update_slice(
        inner, lax.slice_in_dim(inner, inner_size - width, inner_size, axis=dim) + from_right, start
    )
    return inner


def on_device(cells, weight, bias, cotangent):
    chan_in, cells_x, cells_y, cells_z = cells.shape
    chan_out = weight.shape[0]
    stencil = [
        (shift_a, shift_b, shift_e)
        for shift_a in range(3)
        for shift_b in range(3)
        for shift_e in range(3)
    ]
    widened = extended(cells, (("gx", 1), ("gy", 2), ("gz", 3)), 1)
    patches = jnp.stack(
        [
            jnp.transpose(
                widened[:, sa : sa + cells_x, sb : sb + cells_y, se : se + cells_z], (1, 2, 0, 3)
            )
            for sa, sb, se in stencil
        ],
        axis=3,
    )
    patches = patches.reshape(cells_x * cells_y, chan_in * 27, cells_z)
    cot = cotangent.reshape(chan_out, -1)
    wide_x, wide_y = cells_x + 2, cells_y + 2
    pooled, weight_local, bias_local, main, edge = forward(
        weight, bias.reshape(chan_out, 1), patches, cot, cells_x // 2, wide_x, wide_y
    )
    pooled = pooled.reshape(cotangent.shape)
    taps = chan_in * 27
    width = -(-(taps + 1) // 128) * 128
    partial = jnp.concatenate(
        [weight_local, bias_local, jnp.zeros((chan_out, width - taps - 1), jnp.float32)],
        axis=1,
    )
    sizes = tuple(lax.axis_size(a) for a in AXES)
    both = allreduce(partial, sizes)
    weight_grad = both[:, :taps].reshape(chan_out, chan_in, 3, 3, 3)
    bias_grad = both[:, taps]
    main = main.reshape(wide_x, wide_y, chan_in, cells_z)
    edge = edge.reshape(wide_x, wide_y, chan_in, cells_z)
    lo = edge[..., cells_z - 1 :]
    hi = edge[..., :1]
    count = lax.axis_size("gz")
    from_left = lax.ppermute(hi, "gz", [(i, (i + 1) % count) for i in range(count)])
    from_right = lax.ppermute(lo, "gz", [((i + 1) % count, i) for i in range(count)])
    main = jnp.concatenate(
        [
            main[..., :1] + from_left,
            main[..., 1 : cells_z - 1],
            main[..., cells_z - 1 :] + from_right,
        ],
        axis=3,
    )
    main = fold_halo(main, "gy", 1, 1)
    main = fold_halo(main, "gx", 0, 1)
    input_grad = jnp.transpose(main, (2, 0, 1, 3))
    return (pooled, weight_grad, bias_grad, input_grad)


def solution(mesh):
    in_specs = (P(None, "gx", "gy", "gz"), P(), P(), P(None, "gx", "gy", "gz"))
    out_specs = (P(None, "gx", "gy", "gz"), P(), P(), P(None, "gx", "gy", "gz"))
    return jax.shard_map(
        on_device, mesh=mesh, in_specs=in_specs, out_specs=out_specs, check_vma=False
    )
```

```python
import jax
import jax.numpy as jnp
from jax import lax
from jax.experimental import pallas as pl
from jax.experimental.pallas import tpu as pltpu
from jax.sharding import PartitionSpec as P

MESH = pl.DeviceIdType.MESH
AXES = ("gx", "gy", "gz")

leak_slope = 0.3
soft_scale = 10.0


def extended(cells, sides, width):
    for axis, dim in sides:
        count = lax.axis_size(axis)
        head = lax.slice_in_dim(cells, 0, width, axis=dim)
        tail = lax.slice_in_dim(cells, cells.shape[dim] - width, cells.shape[dim], axis=dim)
        cells = jnp.concatenate(
            [
                lax.ppermute(tail, axis, [(i, (i + 1) % count) for i in range(count)]),
                cells,
                lax.ppermute(head, axis, [((i + 1) % count, i) for i in range(count)]),
            ],
            axis=dim,
        )
    return cells


def allreduce_kernel(sizes, x_ref, o_ref, slots_a, slots_b, acc_a, send_a, recv_a, send_b, recv_b):
    me = tuple(lax.axis_index(a) for a in AXES)
    groups = (
        [(k,) for k in range(sizes[0])],
        [(k, m) for k in range(sizes[1]) for m in range(sizes[2])],
    )
    places = ((0,), (1, 2))

    def device(phase, member):
        coords = list(me)
        for axis, value in zip(places[phase], member):
            coords[axis] = value
        return tuple(coords)

    def rank(phase):
        out = 0
        for axis in places[phase]:
            out = out * sizes[axis] + me[axis]
        return out

    def member_of(phase, index):
        out = []
        for axis in reversed(places[phase]):
            out.append(lax.rem(index, sizes[axis]))
            index = index // sizes[axis]
        return tuple(reversed(out))

    barrier = pltpu.get_barrier_semaphore()
    count = 0
    for phase in range(2):
        n = len(groups[phase])
        for d in range(1, n):
            target = member_of(phase, lax.rem(rank(phase) + d, n))
            pl.semaphore_signal(barrier, inc=1, device_id=device(phase, target), device_id_type=MESH)
            count += 1
    pl.semaphore_wait(barrier, count)

    slots = (slots_a, slots_b)
    sends = (send_a, send_b)
    recvs = (recv_a, recv_b)
    sources = (x_ref, acc_a)
    sinks = (acc_a, o_ref)
    for phase in range(2):
        n = len(groups[phase])
        src, held, sink = sources[phase], slots[phase], sinks[phase]
        mine = rank(phase)
        copies = []
        for d in range(1, n):
            target = member_of(phase, lax.rem(mine + d, n))
            copy = pltpu.make_async_remote_copy(
                src_ref=src,
                dst_ref=held.at[mine],
                send_sem=sends[phase].at[d],
                recv_sem=recvs[phase].at[mine],
                device_id=device(phase, target),
                device_id_type=MESH,
            )
            copy.start()
            copies.append(copy)
        held[mine] = src[...]
        for d in range(1, n):
            origin = lax.rem(mine + n - d, n)
            incoming = pltpu.make_async_remote_copy(
                src_ref=src,
                dst_ref=held.at[origin],
                send_sem=sends[phase].at[d],
                recv_sem=recvs[phase].at[origin],
                device_id=device(phase, member_of(phase, origin)),
                device_id_type=MESH,
            )
            incoming.wait_recv()
        for copy in copies:
            copy.wait_send()
        total = held[0]
        for k in range(1, n):
            total = total + held[k]
        sink[...] = total


def allreduce(x, sizes):
    shape = x.shape
    first, second = sizes[0], sizes[1] * sizes[2]
    return pl.pallas_call(
        lambda *refs: allreduce_kernel(sizes, *refs),
        out_shape=jax.ShapeDtypeStruct(shape, jnp.float32),
        in_specs=[pl.BlockSpec(memory_space=pltpu.VMEM)],
        out_specs=pl.BlockSpec(memory_space=pltpu.VMEM),
        scratch_shapes=[
            pltpu.VMEM((first,) + shape, jnp.float32),
            pltpu.VMEM((second,) + shape, jnp.float32),
            pltpu.VMEM(shape, jnp.float32),
            pltpu.SemaphoreType.DMA((first,)),
            pltpu.SemaphoreType.DMA((first,)),
            pltpu.SemaphoreType.DMA((second,)),
            pltpu.SemaphoreType.DMA((second,)),
        ],
        compiler_params=pltpu.CompilerParams(collective_id=0, has_side_effects=True),
    )(x)


def forward_kernel(rows, wide_y, w_ref, b_ref, q_ref, u_ref, wt_ref, p_ref, cot_ref,
                   pooled_ref, wg_ref, bg_ref, main_ref, edge_ref, wg_acc, bg_acc):
    step = pl.program_id(0)
    plane = p_ref.shape[0] // 2
    lines = plane // 4

    @pl.when(step == 0)
    def _():
        wg_acc[...] = jnp.zeros_like(wg_acc)
        bg_acc[...] = jnp.zeros_like(bg_acc)
        main_ref[...] = jnp.zeros_like(main_ref)
        edge_ref[...] = jnp.zeros_like(edge_ref)

    weight = w_ref[...]
    bias = b_ref[...]
    spread_w = wt_ref[...]
    slots = spread_w.shape[0] // 27
    lane = lax.broadcasted_iota(jnp.int32, (slots, rows), 1)
    first = lane == 0
    last = lane == rows - 1

    group = 32
    pooled_rows = group // 2
    pieces = pooled_rows // 2

    @pl.loop(0, plane // group)
    def _(j):
        ups = []
        for m in range(pieces):
            cot = cot_ref[:, pl.ds(pl.multiple_of((j * pieces + m) * rows, rows), rows)]
            ups.append(jnp.dot(cot, u_ref[0], preferred_element_type=jnp.float32) * 0.125)
            ups.append(jnp.dot(cot, u_ref[1], preferred_element_type=jnp.float32) * 0.125)
        spread_all = jnp.concatenate([ups[r // 2] for r in range(group)], axis=1)
        totals = [None] * pooled_rows
        wg = None
        bg = None
        spreads = []
        for px, base in enumerate((0, plane)):
            patch = jnp.concatenate([p_ref[base + j * group + r] for r in range(group)], axis=1)
            preact = jnp.dot(weight, patch, preferred_element_type=jnp.float32) + bias
            scaled = soft_scale * preact
            e = jnp.exp(-jnp.abs(scaled))
            softplus = jnp.maximum(scaled, 0.0) + jnp.log1p(e)
            activated = leak_slope * preact + (1.0 - leak_slope) / soft_scale * softplus
            for h in range(pooled_rows):
                pair = (
                    activated[:, 2 * h * rows : (2 * h + 1) * rows]
                    + activated[:, (2 * h + 1) * rows : (2 * h + 2) * rows]
                )
                totals[h] = pair if totals[h] is None else totals[h] + pair
            sigmoid = jnp.where(scaled >= 0.0, 1.0, e) / (1.0 + e)
            slope = leak_slope + (1.0 - leak_slope) * sigmoid
            delta = (slope * spread_all).astype(jnp.bfloat16)
            term = lax.dot_general(
                delta, patch, (((1,), (1,)), ((), ())), preferred_element_type=jnp.float32
            )
            wg = term if wg is None else wg + term
            part = delta.astype(jnp.float32)
            bg = part if bg is None else bg + part
            spreads.append(jnp.dot(spread_w, delta, preferred_element_type=jnp.float32))
        acc_main = {}
        acc_edge = {}
        for px in range(2):
            for r in range(group):
                cols = slice(r * rows, (r + 1) * rows)
                for a in range(3):
                    for b in range(3):
                        at = (a * 3 + b) * 3 * slots
                        g = spreads[px]
                        v0 = pltpu.roll(g[at : at + slots, cols], rows - 1, 1)
                        v1 = g[at + slots : at + 2 * slots, cols]
                        v2 = pltpu.roll(g[at + 2 * slots : at + 3 * slots, cols], 1, 1)
                        inner = jnp.where(last, 0.0, v0) + v1 + jnp.where(first, 0.0, v2)
                        edge = jnp.where(last, v0, 0.0) + jnp.where(first, v2, 0.0)
                        key = (px + a, r + b)
                        if key in acc_main:
                            acc_main[key] = acc_main[key] + inner
                            acc_edge[key] = acc_edge[key] + edge
                        else:
                            acc_main[key] = inner
                            acc_edge[key] = edge
        for (dx, dy), value in acc_main.items():
            out = (step * 2 + dx) * wide_y + (j * group + dy)
            main_ref[out] += value[: main_ref.shape[1]]
            edge_ref[out] += acc_edge[dx, dy][: edge_ref.shape[1]]
        wg_acc[...] += wg
        bg_acc[...] += jnp.sum(bg, axis=1, keepdims=True)
        for m in range(pieces):
            pooled = jnp.dot(
                totals[2 * m], q_ref[0], preferred_element_type=jnp.float32,
                precision=lax.Precision.HIGHEST,
            ) + jnp.dot(
                totals[2 * m + 1], q_ref[1], preferred_element_type=jnp.float32,
                precision=lax.Precision.HIGHEST,
            )
            at = pl.multiple_of((j * pieces + m) * rows, rows)
            pooled_ref[:, pl.ds(at, rows)] = (pooled * 0.125).astype(pooled_ref.dtype)

    @pl.when(step == pl.num_programs(0) - 1)
    def _():
        wg_ref[...] = wg_acc[...]
        bg_ref[...] = bg_acc[...]


def forward(weight, bias, patches, cot, pairs, wide_x, wide_y):
    lines, taps, rows = patches.shape
    chan_out, chan_in = weight.shape[:2]
    weight_mat = jnp.transpose(weight.reshape(chan_out, chan_in, 27), (0, 2, 1))
    weight_mat = weight_mat.reshape(chan_out, taps)
    slots = 8
    spread_w = jnp.transpose(weight, (2, 3, 4, 1, 0))
    spread_w = jnp.pad(spread_w, ((0, 0), (0, 0), (0, 0), (0, slots - chan_in), (0, 0)))
    spread_w = spread_w.reshape(27 * slots, chan_out)
    half = rows // 2
    z = jnp.arange(rows)
    k = jnp.arange(rows)
    pool = jnp.stack(
        [(k[None, :] == z[:, None] // 2), (k[None, :] == half + z[:, None] // 2)]
    ).astype(jnp.float32)
    spread = jnp.stack(
        [(z[None, :] // 2 == k[:, None]), (z[None, :] // 2 + half == k[:, None])]
    ).astype(jnp.bfloat16)
    full = lambda shape: pl.BlockSpec(shape, lambda p: (0,) * len(shape))
    block = lines // pairs
    acc_shape = (wide_x * wide_y, chan_in, rows)
    return pl.pallas_call(
        lambda *refs: forward_kernel(rows, wide_y, *refs),
        grid=(pairs,),
        out_shape=(
            jax.ShapeDtypeStruct(cot.shape, jnp.bfloat16),
            jax.ShapeDtypeStruct((chan_out, taps), jnp.float32),
            jax.ShapeDtypeStruct((chan_out, 1), jnp.float32),
            jax.ShapeDtypeStruct(acc_shape, jnp.float32),
            jax.ShapeDtypeStruct(acc_shape, jnp.float32),
        ),
        in_specs=[
            full((chan_out, taps)),
            full((chan_out, 1)),
            full((2, rows, rows)),
            full((2, rows, rows)),
            full((27 * slots, chan_out)),
            pl.BlockSpec((block, taps, rows), lambda p: (p, 0, 0)),
            pl.BlockSpec((chan_out, cot.shape[1] // pairs), lambda p: (0, p)),
        ],
        out_specs=(
            pl.BlockSpec((chan_out, cot.shape[1] // pairs), lambda p: (0, p)),
            full((chan_out, taps)),
            full((chan_out, 1)),
            full(acc_shape),
            full(acc_shape),
        ),
        scratch_shapes=[
            pltpu.VMEM((chan_out, taps), jnp.float32),
            pltpu.VMEM((chan_out, 1), jnp.float32),
        ],
    )(weight_mat, bias, pool, spread, spread_w, patches, cot)


def fold_halo(main, axis, dim, width):
    count = lax.axis_size(axis)
    size = main.shape[dim]
    head = lax.slice_in_dim(main, 0, width, axis=dim)
    tail = lax.slice_in_dim(main, size - width, size, axis=dim)
    from_left = lax.ppermute(tail, axis, [(i, (i + 1) % count) for i in range(count)])
    from_right = lax.ppermute(head, axis, [((i + 1) % count, i) for i in range(count)])
    inner = lax.slice_in_dim(main, width, size - width, axis=dim)
    inner_size = size - 2 * width
    start = [0] * main.ndim
    inner = lax.dynamic_update_slice(
        inner, lax.slice_in_dim(inner, 0, width, axis=dim) + from_left, start
    )
    start[dim] = inner_size - width
    inner = lax.dynamic_update_slice(
        inner, lax.slice_in_dim(inner, inner_size - width, inner_size, axis=dim) + from_right, start
    )
    return inner


def on_device(cells, weight, bias, cotangent):
    chan_in, cells_x, cells_y, cells_z = cells.shape
    chan_out = weight.shape[0]
    stencil = [
        (shift_a, shift_b, shift_e)
        for shift_a in range(3)
        for shift_b in range(3)
        for shift_e in range(3)
    ]
    widened = extended(cells, (("gx", 1), ("gy", 2), ("gz", 3)), 1)
    patches = jnp.concatenate(
        [
            jnp.transpose(
                widened[:, sa : sa + cells_x, sb : sb + cells_y, se : se + cells_z], (1, 2, 0, 3)
            )
            for sa, sb, se in stencil
        ],
        axis=2,
    )
    patches = patches.reshape(cells_x * cells_y, 27 * chan_in, cells_z)
    cot = cotangent.reshape(chan_out, -1)
    wide_x, wide_y = cells_x + 2, cells_y + 2
    pooled, weight_local, bias_local, main, edge = forward(
        weight, bias.reshape(chan_out, 1), patches, cot, cells_x // 2, wide_x, wide_y
    )
    pooled = pooled.reshape(cotangent.shape)
    weight_local = jnp.transpose(weight_local.reshape(chan_out, 27, chan_in), (0, 2, 1))
    weight_local = weight_local.reshape(chan_out, -1)
    taps = chan_in * 27
    width = -(-(taps + 1) // 128) * 128
    partial = jnp.concatenate(
        [weight_local, bias_local, jnp.zeros((chan_out, width - taps - 1), jnp.float32)],
        axis=1,
    )
    sizes = tuple(lax.axis_size(a) for a in AXES)
    both = allreduce(partial, sizes)
    weight_grad = both[:, :taps].reshape(chan_out, chan_in, 3, 3, 3)
    bias_grad = both[:, taps]
    main = main.reshape(wide_x, wide_y, chan_in, cells_z)
    edge = edge.reshape(wide_x, wide_y, chan_in, cells_z)
    lo = edge[..., cells_z - 1 :]
    hi = edge[..., :1]
    count = lax.axis_size("gz")
    from_left = lax.ppermute(hi, "gz", [(i, (i + 1) % count) for i in range(count)])
    from_right = lax.ppermute(lo, "gz", [((i + 1) % count, i) for i in range(count)])
    main = jnp.concatenate(
        [
            main[..., :1] + from_left,
            main[..., 1 : cells_z - 1],
            main[..., cells_z - 1 :] + from_right,
        ],
        axis=3,
    )
    main = fold_halo(main, "gy", 1, 1)
    main = fold_halo(main, "gx", 0, 1)
    input_grad = jnp.transpose(main, (2, 0, 1, 3))
    return (pooled, weight_grad, bias_grad, input_grad)


def solution(mesh):
    in_specs = (P(None, "gx", "gy", "gz"), P(), P(), P(None, "gx", "gy", "gz"))
    out_specs = (P(None, "gx", "gy", "gz"), P(), P(), P(None, "gx", "gy", "gz"))
    return jax.shard_map(
        on_device, mesh=mesh, in_specs=in_specs, out_specs=out_specs, check_vma=False
    )
```

```python
import jax
import jax.numpy as jnp
from jax import lax
from jax.experimental import pallas as pl
from jax.experimental.pallas import tpu as pltpu
from jax.sharding import PartitionSpec as P

MESH = pl.DeviceIdType.MESH
AXES = ("gx", "gy", "gz")

leak_slope = 0.3
soft_scale = 10.0


def extended(cells, sides, width):
    for axis, dim in sides:
        count = lax.axis_size(axis)
        head = lax.slice_in_dim(cells, 0, width, axis=dim)
        tail = lax.slice_in_dim(cells, cells.shape[dim] - width, cells.shape[dim], axis=dim)
        cells = jnp.concatenate(
            [
                lax.ppermute(tail, axis, [(i, (i + 1) % count) for i in range(count)]),
                cells,
                lax.ppermute(head, axis, [((i + 1) % count, i) for i in range(count)]),
            ],
            axis=dim,
        )
    return cells


def allreduce_kernel(sizes, x_ref, o_ref, slots_a, slots_b, acc_a, send_a, recv_a, send_b, recv_b):
    me = tuple(lax.axis_index(a) for a in AXES)
    groups = (
        [(k,) for k in range(sizes[0])],
        [(k, m) for k in range(sizes[1]) for m in range(sizes[2])],
    )
    places = ((0,), (1, 2))

    def device(phase, member):
        coords = list(me)
        for axis, value in zip(places[phase], member):
            coords[axis] = value
        return tuple(coords)

    def rank(phase):
        out = 0
        for axis in places[phase]:
            out = out * sizes[axis] + me[axis]
        return out

    def member_of(phase, index):
        out = []
        for axis in reversed(places[phase]):
            out.append(lax.rem(index, sizes[axis]))
            index = index // sizes[axis]
        return tuple(reversed(out))

    barrier = pltpu.get_barrier_semaphore()
    count = 0
    for phase in range(2):
        n = len(groups[phase])
        for d in range(1, n):
            target = member_of(phase, lax.rem(rank(phase) + d, n))
            pl.semaphore_signal(barrier, inc=1, device_id=device(phase, target), device_id_type=MESH)
            count += 1
    pl.semaphore_wait(barrier, count)

    slots = (slots_a, slots_b)
    sends = (send_a, send_b)
    recvs = (recv_a, recv_b)
    sources = (x_ref, acc_a)
    sinks = (acc_a, o_ref)
    for phase in range(2):
        n = len(groups[phase])
        src, held, sink = sources[phase], slots[phase], sinks[phase]
        mine = rank(phase)
        copies = []
        for d in range(1, n):
            target = member_of(phase, lax.rem(mine + d, n))
            copy = pltpu.make_async_remote_copy(
                src_ref=src,
                dst_ref=held.at[mine],
                send_sem=sends[phase].at[d],
                recv_sem=recvs[phase].at[mine],
                device_id=device(phase, target),
                device_id_type=MESH,
            )
            copy.start()
            copies.append(copy)
        held[mine] = src[...]
        for d in range(1, n):
            origin = lax.rem(mine + n - d, n)
            incoming = pltpu.make_async_remote_copy(
                src_ref=src,
                dst_ref=held.at[origin],
                send_sem=sends[phase].at[d],
                recv_sem=recvs[phase].at[origin],
                device_id=device(phase, member_of(phase, origin)),
                device_id_type=MESH,
            )
            incoming.wait_recv()
        for copy in copies:
            copy.wait_send()
        total = held[0]
        for k in range(1, n):
            total = total + held[k]
        sink[...] = total


def allreduce(x, sizes):
    shape = x.shape
    first, second = sizes[0], sizes[1] * sizes[2]
    return pl.pallas_call(
        lambda *refs: allreduce_kernel(sizes, *refs),
        out_shape=jax.ShapeDtypeStruct(shape, jnp.float32),
        in_specs=[pl.BlockSpec(memory_space=pltpu.VMEM)],
        out_specs=pl.BlockSpec(memory_space=pltpu.VMEM),
        scratch_shapes=[
            pltpu.VMEM((first,) + shape, jnp.float32),
            pltpu.VMEM((second,) + shape, jnp.float32),
            pltpu.VMEM(shape, jnp.float32),
            pltpu.SemaphoreType.DMA((first,)),
            pltpu.SemaphoreType.DMA((first,)),
            pltpu.SemaphoreType.DMA((second,)),
            pltpu.SemaphoreType.DMA((second,)),
        ],
        compiler_params=pltpu.CompilerParams(collective_id=0, has_side_effects=True),
    )(x)


def forward_kernel(rows, wide_y, w_ref, b_ref, q_ref, u_ref, wt_ref, p_ref, cot_ref,
                   pooled_ref, wg_ref, bg_ref, main_ref, edge_ref, wg_acc, bg_acc):
    step = pl.program_id(0)
    plane = p_ref.shape[0] // 2
    lines = plane // 4

    @pl.when(step == 0)
    def _():
        wg_acc[...] = jnp.zeros_like(wg_acc)
        bg_acc[...] = jnp.zeros_like(bg_acc)
        main_ref[...] = jnp.zeros_like(main_ref)
        edge_ref[...] = jnp.zeros_like(edge_ref)

    weight = w_ref[...]
    bias = b_ref[...]
    spread_w = wt_ref[...]
    slots = spread_w.shape[0] // 27
    lane = lax.broadcasted_iota(jnp.int32, (slots, rows), 1)
    first = lane == 0
    last = lane == rows - 1

    group = 64
    pooled_rows = group // 2
    pieces = pooled_rows // 2

    @pl.loop(0, plane // group)
    def _(j):
        ups = []
        for m in range(pieces):
            cot = cot_ref[:, pl.ds(pl.multiple_of((j * pieces + m) * rows, rows), rows)]
            ups.append(jnp.dot(cot, u_ref[0], preferred_element_type=jnp.float32) * 0.125)
            ups.append(jnp.dot(cot, u_ref[1], preferred_element_type=jnp.float32) * 0.125)
        spread_all = jnp.concatenate([ups[r // 2] for r in range(group)], axis=1)
        totals = [None] * pooled_rows
        wg = None
        bg = None
        spreads = []
        for px, base in enumerate((0, plane)):
            patch = jnp.concatenate([p_ref[base + j * group + r] for r in range(group)], axis=1)
            preact = jnp.dot(weight, patch, preferred_element_type=jnp.float32) + bias
            scaled = soft_scale * preact
            e = jnp.exp(-jnp.abs(scaled))
            softplus = jnp.maximum(scaled, 0.0) + jnp.log1p(e)
            activated = leak_slope * preact + (1.0 - leak_slope) / soft_scale * softplus
            for h in range(pooled_rows):
                pair = (
                    activated[:, 2 * h * rows : (2 * h + 1) * rows]
                    + activated[:, (2 * h + 1) * rows : (2 * h + 2) * rows]
                )
                totals[h] = pair if totals[h] is None else totals[h] + pair
            sigmoid = jnp.where(scaled >= 0.0, 1.0, e) / (1.0 + e)
            slope = leak_slope + (1.0 - leak_slope) * sigmoid
            delta = (slope * spread_all).astype(jnp.bfloat16)
            term = lax.dot_general(
                delta, patch, (((1,), (1,)), ((), ())), preferred_element_type=jnp.float32
            )
            wg = term if wg is None else wg + term
            part = delta.astype(jnp.float32)
            bg = part if bg is None else bg + part
            spreads.append(jnp.dot(spread_w, delta, preferred_element_type=jnp.float32))
        acc_main = {}
        acc_edge = {}
        for px in range(2):
            for r in range(group):
                cols = slice(r * rows, (r + 1) * rows)
                for a in range(3):
                    for b in range(3):
                        at = (a * 3 + b) * 3 * slots
                        g = spreads[px]
                        v0 = pltpu.roll(g[at : at + slots, cols], rows - 1, 1)
                        v1 = g[at + slots : at + 2 * slots, cols]
                        v2 = pltpu.roll(g[at + 2 * slots : at + 3 * slots, cols], 1, 1)
                        inner = jnp.where(last, 0.0, v0) + v1 + jnp.where(first, 0.0, v2)
                        edge = jnp.where(last, v0, 0.0) + jnp.where(first, v2, 0.0)
                        key = (px + a, r + b)
                        if key in acc_main:
                            acc_main[key] = acc_main[key] + inner
                            acc_edge[key] = acc_edge[key] + edge
                        else:
                            acc_main[key] = inner
                            acc_edge[key] = edge
        for (dx, dy), value in acc_main.items():
            out = (step * 2 + dx) * wide_y + (j * group + dy)
            main_ref[out] += value[: main_ref.shape[1]]
            edge_ref[out] += acc_edge[dx, dy][: edge_ref.shape[1]]
        wg_acc[...] += wg
        bg_acc[...] += jnp.sum(bg, axis=1, keepdims=True)
        for m in range(pieces):
            pooled = jnp.dot(
                totals[2 * m], q_ref[0], preferred_element_type=jnp.float32,
                precision=lax.Precision.HIGHEST,
            ) + jnp.dot(
                totals[2 * m + 1], q_ref[1], preferred_element_type=jnp.float32,
                precision=lax.Precision.HIGHEST,
            )
            at = pl.multiple_of((j * pieces + m) * rows, rows)
            pooled_ref[:, pl.ds(at, rows)] = (pooled * 0.125).astype(pooled_ref.dtype)

    @pl.when(step == pl.num_programs(0) - 1)
    def _():
        wg_ref[...] = wg_acc[...]
        bg_ref[...] = bg_acc[...]


def forward(weight, bias, patches, cot, pairs, wide_x, wide_y):
    lines, taps, rows = patches.shape
    chan_out, chan_in = weight.shape[:2]
    weight_mat = weight.reshape(chan_out, taps)
    slots = 8
    spread_w = jnp.transpose(weight, (2, 3, 4, 1, 0))
    spread_w = jnp.pad(spread_w, ((0, 0), (0, 0), (0, 0), (0, slots - chan_in), (0, 0)))
    spread_w = spread_w.reshape(27 * slots, chan_out)
    half = rows // 2
    z = jnp.arange(rows)
    k = jnp.arange(rows)
    pool = jnp.stack(
        [(k[None, :] == z[:, None] // 2), (k[None, :] == half + z[:, None] // 2)]
    ).astype(jnp.float32)
    spread = jnp.stack(
        [(z[None, :] // 2 == k[:, None]), (z[None, :] // 2 + half == k[:, None])]
    ).astype(jnp.bfloat16)
    full = lambda shape: pl.BlockSpec(shape, lambda p: (0,) * len(shape))
    block = lines // pairs
    acc_shape = (wide_x * wide_y, chan_in, rows)
    return pl.pallas_call(
        lambda *refs: forward_kernel(rows, wide_y, *refs),
        grid=(pairs,),
        out_shape=(
            jax.ShapeDtypeStruct(cot.shape, jnp.bfloat16),
            jax.ShapeDtypeStruct((chan_out, taps), jnp.float32),
            jax.ShapeDtypeStruct((chan_out, 1), jnp.float32),
            jax.ShapeDtypeStruct(acc_shape, jnp.float32),
            jax.ShapeDtypeStruct(acc_shape, jnp.float32),
        ),
        in_specs=[
            full((chan_out, taps)),
            full((chan_out, 1)),
            full((2, rows, rows)),
            full((2, rows, rows)),
            full((27 * slots, chan_out)),
            pl.BlockSpec((block, taps, rows), lambda p: (p, 0, 0)),
            pl.BlockSpec((chan_out, cot.shape[1] // pairs), lambda p: (0, p)),
        ],
        out_specs=(
            pl.BlockSpec((chan_out, cot.shape[1] // pairs), lambda p: (0, p)),
            full((chan_out, taps)),
            full((chan_out, 1)),
            full(acc_shape),
            full(acc_shape),
        ),
        scratch_shapes=[
            pltpu.VMEM((chan_out, taps), jnp.float32),
            pltpu.VMEM((chan_out, 1), jnp.float32),
        ],
    )(weight_mat, bias, pool, spread, spread_w, patches, cot)


def fold_halo(main, axis, dim, width):
    count = lax.axis_size(axis)
    size = main.shape[dim]
    head = lax.slice_in_dim(main, 0, width, axis=dim)
    tail = lax.slice_in_dim(main, size - width, size, axis=dim)
    from_left = lax.ppermute(tail, axis, [(i, (i + 1) % count) for i in range(count)])
    from_right = lax.ppermute(head, axis, [((i + 1) % count, i) for i in range(count)])
    inner = lax.slice_in_dim(main, width, size - width, axis=dim)
    inner_size = size - 2 * width
    start = [0] * main.ndim
    inner = lax.dynamic_update_slice(
        inner, lax.slice_in_dim(inner, 0, width, axis=dim) + from_left, start
    )
    start[dim] = inner_size - width
    inner = lax.dynamic_update_slice(
        inner, lax.slice_in_dim(inner, inner_size - width, inner_size, axis=dim) + from_right, start
    )
    return inner


def on_device(cells, weight, bias, cotangent):
    chan_in, cells_x, cells_y, cells_z = cells.shape
    chan_out = weight.shape[0]
    stencil = [
        (shift_a, shift_b, shift_e)
        for shift_a in range(3)
        for shift_b in range(3)
        for shift_e in range(3)
    ]
    widened = extended(cells, (("gx", 1), ("gy", 2), ("gz", 3)), 1)
    patches = jnp.stack(
        [
            jnp.transpose(
                widened[:, sa : sa + cells_x, sb : sb + cells_y, se : se + cells_z], (1, 2, 0, 3)
            )
            for sa, sb, se in stencil
        ],
        axis=3,
    )
    patches = patches.reshape(cells_x * cells_y, chan_in * 27, cells_z)
    cot = cotangent.reshape(chan_out, -1)
    wide_x, wide_y = cells_x + 2, cells_y + 2
    pooled, weight_local, bias_local, main, edge = forward(
        weight, bias.reshape(chan_out, 1), patches, cot, cells_x // 2, wide_x, wide_y
    )
    pooled = pooled.reshape(cotangent.shape)
    taps = chan_in * 27
    width = -(-(taps + 1) // 128) * 128
    partial = jnp.concatenate(
        [weight_local, bias_local, jnp.zeros((chan_out, width - taps - 1), jnp.float32)],
        axis=1,
    )
    sizes = tuple(lax.axis_size(a) for a in AXES)
    both = allreduce(partial, sizes)
    weight_grad = both[:, :taps].reshape(chan_out, chan_in, 3, 3, 3)
    bias_grad = both[:, taps]
    main = main.reshape(wide_x, wide_y, chan_in, cells_z)
    edge = edge.reshape(wide_x, wide_y, chan_in, cells_z)
    lo = edge[..., cells_z - 1 :]
    hi = edge[..., :1]
    count = lax.axis_size("gz")
    from_left = lax.ppermute(hi, "gz", [(i, (i + 1) % count) for i in range(count)])
    from_right = lax.ppermute(lo, "gz", [((i + 1) % count, i) for i in range(count)])
    main = jnp.concatenate(
        [
            main[..., :1] + from_left,
            main[..., 1 : cells_z - 1],
            main[..., cells_z - 1 :] + from_right,
        ],
        axis=3,
    )
    main = fold_halo(main, "gy", 1, 1)
    main = fold_halo(main, "gx", 0, 1)
    input_grad = jnp.transpose(main, (2, 0, 1, 3))
    return (pooled, weight_grad, bias_grad, input_grad)


def solution(mesh):
    in_specs = (P(None, "gx", "gy", "gz"), P(), P(), P(None, "gx", "gy", "gz"))
    out_specs = (P(None, "gx", "gy", "gz"), P(), P(), P(None, "gx", "gy", "gz"))
    return jax.shard_map(
        on_device, mesh=mesh, in_specs=in_specs, out_specs=out_specs, check_vma=False
    )
```

```python
import jax
import jax.numpy as jnp
from jax import lax
from jax.experimental import pallas as pl
from jax.experimental.pallas import tpu as pltpu
from jax.sharding import PartitionSpec as P

MESH = pl.DeviceIdType.MESH
AXES = ("gx", "gy", "gz")

leak_slope = 0.3
soft_scale = 10.0


def extended(cells, sides, width):
    for axis, dim in sides:
        count = lax.axis_size(axis)
        head = lax.slice_in_dim(cells, 0, width, axis=dim)
        tail = lax.slice_in_dim(cells, cells.shape[dim] - width, cells.shape[dim], axis=dim)
        cells = jnp.concatenate(
            [
                lax.ppermute(tail, axis, [(i, (i + 1) % count) for i in range(count)]),
                cells,
                lax.ppermute(head, axis, [((i + 1) % count, i) for i in range(count)]),
            ],
            axis=dim,
        )
    return cells


def allreduce_kernel(sizes, x_ref, o_ref, slots_a, slots_b, acc_a, send_a, recv_a, send_b, recv_b):
    me = tuple(lax.axis_index(a) for a in AXES)
    groups = (
        [(k,) for k in range(sizes[0])],
        [(k, m) for k in range(sizes[1]) for m in range(sizes[2])],
    )
    places = ((0,), (1, 2))

    def device(phase, member):
        coords = list(me)
        for axis, value in zip(places[phase], member):
            coords[axis] = value
        return tuple(coords)

    def rank(phase):
        out = 0
        for axis in places[phase]:
            out = out * sizes[axis] + me[axis]
        return out

    def member_of(phase, index):
        out = []
        for axis in reversed(places[phase]):
            out.append(lax.rem(index, sizes[axis]))
            index = index // sizes[axis]
        return tuple(reversed(out))

    barrier = pltpu.get_barrier_semaphore()
    count = 0
    for phase in range(2):
        n = len(groups[phase])
        for d in range(1, n):
            target = member_of(phase, lax.rem(rank(phase) + d, n))
            pl.semaphore_signal(barrier, inc=1, device_id=device(phase, target), device_id_type=MESH)
            count += 1
    pl.semaphore_wait(barrier, count)

    slots = (slots_a, slots_b)
    sends = (send_a, send_b)
    recvs = (recv_a, recv_b)
    sources = (x_ref, acc_a)
    sinks = (acc_a, o_ref)
    for phase in range(2):
        n = len(groups[phase])
        src, held, sink = sources[phase], slots[phase], sinks[phase]
        mine = rank(phase)
        copies = []
        for d in range(1, n):
            target = member_of(phase, lax.rem(mine + d, n))
            copy = pltpu.make_async_remote_copy(
                src_ref=src,
                dst_ref=held.at[mine],
                send_sem=sends[phase].at[d],
                recv_sem=recvs[phase].at[mine],
                device_id=device(phase, target),
                device_id_type=MESH,
            )
            copy.start()
            copies.append(copy)
        held[mine] = src[...]
        for d in range(1, n):
            origin = lax.rem(mine + n - d, n)
            incoming = pltpu.make_async_remote_copy(
                src_ref=src,
                dst_ref=held.at[origin],
                send_sem=sends[phase].at[d],
                recv_sem=recvs[phase].at[origin],
                device_id=device(phase, member_of(phase, origin)),
                device_id_type=MESH,
            )
            incoming.wait_recv()
        for copy in copies:
            copy.wait_send()
        total = held[0]
        for k in range(1, n):
            total = total + held[k]
        sink[...] = total


def allreduce(x, sizes):
    shape = x.shape
    first, second = sizes[0], sizes[1] * sizes[2]
    return pl.pallas_call(
        lambda *refs: allreduce_kernel(sizes, *refs),
        out_shape=jax.ShapeDtypeStruct(shape, jnp.float32),
        in_specs=[pl.BlockSpec(memory_space=pltpu.VMEM)],
        out_specs=pl.BlockSpec(memory_space=pltpu.VMEM),
        scratch_shapes=[
            pltpu.VMEM((first,) + shape, jnp.float32),
            pltpu.VMEM((second,) + shape, jnp.float32),
            pltpu.VMEM(shape, jnp.float32),
            pltpu.SemaphoreType.DMA((first,)),
            pltpu.SemaphoreType.DMA((first,)),
            pltpu.SemaphoreType.DMA((second,)),
            pltpu.SemaphoreType.DMA((second,)),
        ],
        compiler_params=pltpu.CompilerParams(collective_id=0, has_side_effects=True),
    )(x)


def forward_kernel(rows, wide_y, w_ref, b_ref, q_ref, u_ref, wt_ref, p_ref, cot_ref,
                   pooled_ref, wg_ref, bg_ref, main_ref, edge_ref, wg_acc, bg_acc):
    step = pl.program_id(0)
    plane = p_ref.shape[0] // 2
    lines = plane // 4

    @pl.when(step == 0)
    def _():
        wg_acc[...] = jnp.zeros_like(wg_acc)
        bg_acc[...] = jnp.zeros_like(bg_acc)
        main_ref[...] = jnp.zeros_like(main_ref)
        edge_ref[...] = jnp.zeros_like(edge_ref)

    weight = w_ref[...]
    bias = b_ref[...]
    spread_w = wt_ref[...]
    slots = spread_w.shape[0] // 27
    lane = lax.broadcasted_iota(jnp.int32, (slots, rows), 1)
    first = lane == 0
    last = lane == rows - 1

    group = 32
    pooled_rows = group // 2
    pieces = pooled_rows // 2

    @pl.loop(0, plane // group)
    def _(j):
        ups = []
        for m in range(pieces):
            cot = cot_ref[:, pl.ds(pl.multiple_of((j * pieces + m) * rows, rows), rows)]
            ups.append(jnp.dot(cot, u_ref[0], preferred_element_type=jnp.float32) * 0.125)
            ups.append(jnp.dot(cot, u_ref[1], preferred_element_type=jnp.float32) * 0.125)
        spread_all = jnp.concatenate([ups[r // 2] for r in range(group)], axis=1)
        totals = [None] * pooled_rows
        wg = None
        bg = None
        spreads = []
        for px, base in enumerate((0, plane)):
            patch = jnp.concatenate([p_ref[base + j * group + r] for r in range(group)], axis=1)
            preact = jnp.dot(weight, patch, preferred_element_type=jnp.float32) + bias
            scaled = soft_scale * preact
            e = jnp.exp(-jnp.abs(scaled))
            softplus = jnp.maximum(scaled, 0.0) + jnp.log1p(e)
            activated = leak_slope * preact + (1.0 - leak_slope) / soft_scale * softplus
            for h in range(pooled_rows):
                pair = (
                    activated[:, 2 * h * rows : (2 * h + 1) * rows]
                    + activated[:, (2 * h + 1) * rows : (2 * h + 2) * rows]
                )
                totals[h] = pair if totals[h] is None else totals[h] + pair
            sigmoid = jnp.where(scaled >= 0.0, 1.0, e) / (1.0 + e)
            slope = leak_slope + (1.0 - leak_slope) * sigmoid
            delta = (slope * spread_all).astype(jnp.bfloat16)
            term = lax.dot_general(
                delta, patch, (((1,), (1,)), ((), ())), preferred_element_type=jnp.float32
            )
            wg = term if wg is None else wg + term
            part = delta.astype(jnp.float32)
            bg = part if bg is None else bg + part
            spreads.append(jnp.dot(spread_w, delta, preferred_element_type=jnp.float32))
        acc_main = {}
        acc_edge = {}
        for px in range(2):
            for r in range(group):
                cols = slice(r * rows, (r + 1) * rows)
                for a in range(3):
                    for b in range(3):
                        at = (a * 3 + b) * 3 * slots
                        g = spreads[px]
                        v0 = pltpu.roll(g[at : at + slots, cols], rows - 1, 1)
                        v1 = g[at + slots : at + 2 * slots, cols]
                        v2 = pltpu.roll(g[at + 2 * slots : at + 3 * slots, cols], 1, 1)
                        inner = jnp.where(last, 0.0, v0) + v1 + jnp.where(first, 0.0, v2)
                        edge = jnp.where(last, v0, 0.0) + jnp.where(first, v2, 0.0)
                        key = (px + a, r + b)
                        if key in acc_main:
                            acc_main[key] = acc_main[key] + inner
                            acc_edge[key] = acc_edge[key] + edge
                        else:
                            acc_main[key] = inner
                            acc_edge[key] = edge
        for (dx, dy), value in acc_main.items():
            out = (step * 2 + dx) * wide_y + (j * group + dy)
            main_ref[out] += value[: main_ref.shape[1]]
            edge_ref[out] += acc_edge[dx, dy][: edge_ref.shape[1]]
        wg_acc[...] += wg
        bg_acc[...] += jnp.sum(bg, axis=1, keepdims=True)
        for m in range(pieces):
            pooled = jnp.dot(
                totals[2 * m], q_ref[0], preferred_element_type=jnp.float32,
                precision=lax.Precision.HIGHEST,
            ) + jnp.dot(
                totals[2 * m + 1], q_ref[1], preferred_element_type=jnp.float32,
                precision=lax.Precision.HIGHEST,
            )
            at = pl.multiple_of((j * pieces + m) * rows, rows)
            pooled_ref[:, pl.ds(at, rows)] = (pooled * 0.125).astype(pooled_ref.dtype)

    @pl.when(step == pl.num_programs(0) - 1)
    def _():
        wg_ref[...] = wg_acc[...]
        bg_ref[...] = bg_acc[...]


def forward(weight, bias, patches, cot, pairs, wide_x, wide_y):
    lines, taps, rows = patches.shape
    chan_out, chan_in = weight.shape[:2]
    weight_mat = weight.reshape(chan_out, taps)
    slots = 8
    spread_w = jnp.transpose(weight, (2, 3, 4, 1, 0))
    spread_w = jnp.pad(spread_w, ((0, 0), (0, 0), (0, 0), (0, slots - chan_in), (0, 0)))
    spread_w = spread_w.reshape(27 * slots, chan_out)
    half = rows // 2
    z = jnp.arange(rows)
    k = jnp.arange(rows)
    pool = jnp.stack(
        [(k[None, :] == z[:, None] // 2), (k[None, :] == half + z[:, None] // 2)]
    ).astype(jnp.float32)
    spread = jnp.stack(
        [(z[None, :] // 2 == k[:, None]), (z[None, :] // 2 + half == k[:, None])]
    ).astype(jnp.bfloat16)
    full = lambda shape: pl.BlockSpec(shape, lambda p: (0,) * len(shape))
    block = lines // pairs
    acc_shape = (wide_x * wide_y, chan_in, rows)
    return pl.pallas_call(
        lambda *refs: forward_kernel(rows, wide_y, *refs),
        grid=(pairs,),
        out_shape=(
            jax.ShapeDtypeStruct(cot.shape, jnp.bfloat16),
            jax.ShapeDtypeStruct((chan_out, taps), jnp.float32),
            jax.ShapeDtypeStruct((chan_out, 1), jnp.float32),
            jax.ShapeDtypeStruct(acc_shape, jnp.float32),
            jax.ShapeDtypeStruct(acc_shape, jnp.float32),
        ),
        in_specs=[
            full((chan_out, taps)),
            full((chan_out, 1)),
            full((2, rows, rows)),
            full((2, rows, rows)),
            full((27 * slots, chan_out)),
            pl.BlockSpec((block, taps, rows), lambda p: (p, 0, 0)),
            pl.BlockSpec((chan_out, cot.shape[1] // pairs), lambda p: (0, p)),
        ],
        out_specs=(
            pl.BlockSpec((chan_out, cot.shape[1] // pairs), lambda p: (0, p)),
            full((chan_out, taps)),
            full((chan_out, 1)),
            full(acc_shape),
            full(acc_shape),
        ),
        scratch_shapes=[
            pltpu.VMEM((chan_out, taps), jnp.float32),
            pltpu.VMEM((chan_out, 1), jnp.float32),
        ],
    )(weight_mat, bias, pool, spread, spread_w, patches, cot)


def fold_halo(main, axis, dim, width):
    count = lax.axis_size(axis)
    size = main.shape[dim]
    head = lax.slice_in_dim(main, 0, width, axis=dim)
    tail = lax.slice_in_dim(main, size - width, size, axis=dim)
    from_left = lax.ppermute(tail, axis, [(i, (i + 1) % count) for i in range(count)])
    from_right = lax.ppermute(head, axis, [((i + 1) % count, i) for i in range(count)])
    inner = lax.slice_in_dim(main, width, size - width, axis=dim)
    inner_size = size - 2 * width
    start = [0] * main.ndim
    inner = lax.dynamic_update_slice(
        inner, lax.slice_in_dim(inner, 0, width, axis=dim) + from_left, start
    )
    start[dim] = inner_size - width
    inner = lax.dynamic_update_slice(
        inner, lax.slice_in_dim(inner, inner_size - width, inner_size, axis=dim) + from_right, start
    )
    return inner


def on_device(cells, weight, bias, cotangent):
    chan_in, cells_x, cells_y, cells_z = cells.shape
    chan_out = weight.shape[0]
    stencil = [
        (shift_a, shift_b, shift_e)
        for shift_a in range(3)
        for shift_b in range(3)
        for shift_e in range(3)
    ]
    widened = extended(cells, (("gz", 3), ("gy", 2), ("gx", 1)), 1)
    patches = jnp.stack(
        [
            jnp.transpose(
                widened[:, sa : sa + cells_x, sb : sb + cells_y, se : se + cells_z], (1, 2, 0, 3)
            )
            for sa, sb, se in stencil
        ],
        axis=3,
    )
    patches = patches.reshape(cells_x * cells_y, chan_in * 27, cells_z)
    cot = cotangent.reshape(chan_out, -1)
    wide_x, wide_y = cells_x + 2, cells_y + 2
    pooled, weight_local, bias_local, main, edge = forward(
        weight, bias.reshape(chan_out, 1), patches, cot, cells_x // 2, wide_x, wide_y
    )
    pooled = pooled.reshape(cotangent.shape)
    taps = chan_in * 27
    width = -(-(taps + 1) // 128) * 128
    partial = jnp.concatenate(
        [weight_local, bias_local, jnp.zeros((chan_out, width - taps - 1), jnp.float32)],
        axis=1,
    )
    sizes = tuple(lax.axis_size(a) for a in AXES)
    both = allreduce(partial, sizes)
    weight_grad = both[:, :taps].reshape(chan_out, chan_in, 3, 3, 3)
    bias_grad = both[:, taps]
    main = main.reshape(wide_x, wide_y, chan_in, cells_z)
    edge = edge.reshape(wide_x, wide_y, chan_in, cells_z)
    lo = edge[..., cells_z - 1 :]
    hi = edge[..., :1]
    count = lax.axis_size("gz")
    from_left = lax.ppermute(hi, "gz", [(i, (i + 1) % count) for i in range(count)])
    from_right = lax.ppermute(lo, "gz", [((i + 1) % count, i) for i in range(count)])
    main = jnp.concatenate(
        [
            main[..., :1] + from_left,
            main[..., 1 : cells_z - 1],
            main[..., cells_z - 1 :] + from_right,
        ],
        axis=3,
    )
    main = fold_halo(main, "gy", 1, 1)
    main = fold_halo(main, "gx", 0, 1)
    input_grad = jnp.transpose(main, (2, 0, 1, 3))
    return (pooled, weight_grad, bias_grad, input_grad)


def solution(mesh):
    in_specs = (P(None, "gx", "gy", "gz"), P(), P(), P(None, "gx", "gy", "gz"))
    out_specs = (P(None, "gx", "gy", "gz"), P(), P(), P(None, "gx", "gy", "gz"))
    return jax.shard_map(
        on_device, mesh=mesh, in_specs=in_specs, out_specs=out_specs, check_vma=False
    )
```

```python
import jax
import jax.numpy as jnp
from jax import lax
from jax.experimental import pallas as pl
from jax.experimental.pallas import tpu as pltpu
from jax.sharding import PartitionSpec as P

MESH = pl.DeviceIdType.MESH
AXES = ("gx", "gy", "gz")

leak_slope = 0.3
soft_scale = 10.0


def extended(cells, sides, width):
    for axis, dim in sides:
        count = lax.axis_size(axis)
        head = lax.slice_in_dim(cells, 0, width, axis=dim)
        tail = lax.slice_in_dim(cells, cells.shape[dim] - width, cells.shape[dim], axis=dim)
        cells = jnp.concatenate(
            [
                lax.ppermute(tail, axis, [(i, (i + 1) % count) for i in range(count)]),
                cells,
                lax.ppermute(head, axis, [((i + 1) % count, i) for i in range(count)]),
            ],
            axis=dim,
        )
    return cells


def allreduce_kernel(sizes, x_ref, o_ref, slots_a, slots_b, acc_a, send_a, recv_a, send_b, recv_b):
    me = tuple(lax.axis_index(a) for a in AXES)
    groups = (
        [(k,) for k in range(sizes[0])],
        [(k, m) for k in range(sizes[1]) for m in range(sizes[2])],
    )
    places = ((0,), (1, 2))

    def device(phase, member):
        coords = list(me)
        for axis, value in zip(places[phase], member):
            coords[axis] = value
        return tuple(coords)

    def rank(phase):
        out = 0
        for axis in places[phase]:
            out = out * sizes[axis] + me[axis]
        return out

    def member_of(phase, index):
        out = []
        for axis in reversed(places[phase]):
            out.append(lax.rem(index, sizes[axis]))
            index = index // sizes[axis]
        return tuple(reversed(out))

    barrier = pltpu.get_barrier_semaphore()
    count = 0
    for phase in range(2):
        n = len(groups[phase])
        for d in range(1, n):
            target = member_of(phase, lax.rem(rank(phase) + d, n))
            pl.semaphore_signal(barrier, inc=1, device_id=device(phase, target), device_id_type=MESH)
            count += 1
    pl.semaphore_wait(barrier, count)

    slots = (slots_a, slots_b)
    sends = (send_a, send_b)
    recvs = (recv_a, recv_b)
    sources = (x_ref, acc_a)
    sinks = (acc_a, o_ref)
    for phase in range(2):
        n = len(groups[phase])
        src, held, sink = sources[phase], slots[phase], sinks[phase]
        mine = rank(phase)
        copies = []
        for d in range(1, n):
            target = member_of(phase, lax.rem(mine + d, n))
            copy = pltpu.make_async_remote_copy(
                src_ref=src,
                dst_ref=held.at[mine],
                send_sem=sends[phase].at[d],
                recv_sem=recvs[phase].at[mine],
                device_id=device(phase, target),
                device_id_type=MESH,
            )
            copy.start()
            copies.append(copy)
        held[mine] = src[...]
        for d in range(1, n):
            origin = lax.rem(mine + n - d, n)
            incoming = pltpu.make_async_remote_copy(
                src_ref=src,
                dst_ref=held.at[origin],
                send_sem=sends[phase].at[d],
                recv_sem=recvs[phase].at[origin],
                device_id=device(phase, member_of(phase, origin)),
                device_id_type=MESH,
            )
            incoming.wait_recv()
        for copy in copies:
            copy.wait_send()
        total = held[0]
        for k in range(1, n):
            total = total + held[k]
        sink[...] = total


def allreduce(x, sizes):
    shape = x.shape
    first, second = sizes[0], sizes[1] * sizes[2]
    return pl.pallas_call(
        lambda *refs: allreduce_kernel(sizes, *refs),
        out_shape=jax.ShapeDtypeStruct(shape, jnp.float32),
        in_specs=[pl.BlockSpec(memory_space=pltpu.VMEM)],
        out_specs=pl.BlockSpec(memory_space=pltpu.VMEM),
        scratch_shapes=[
            pltpu.VMEM((first,) + shape, jnp.float32),
            pltpu.VMEM((second,) + shape, jnp.float32),
            pltpu.VMEM(shape, jnp.float32),
            pltpu.SemaphoreType.DMA((first,)),
            pltpu.SemaphoreType.DMA((first,)),
            pltpu.SemaphoreType.DMA((second,)),
            pltpu.SemaphoreType.DMA((second,)),
        ],
        compiler_params=pltpu.CompilerParams(collective_id=0, has_side_effects=True),
    )(x)


def forward_kernel(rows, wide_y, w_ref, b_ref, q_ref, u_ref, wt_ref, p_ref, cot_ref,
                   pooled_ref, wg_ref, bg_ref, main_ref, edge_ref, wg_acc, bg_acc):
    step = pl.program_id(0)
    plane = p_ref.shape[0] // 2
    lines = plane // 4

    @pl.when(step == 0)
    def _():
        wg_acc[...] = jnp.zeros_like(wg_acc)
        bg_acc[...] = jnp.zeros_like(bg_acc)
        main_ref[...] = jnp.zeros_like(main_ref)
        edge_ref[...] = jnp.zeros_like(edge_ref)

    weight = w_ref[...]
    bias = b_ref[...]
    spread_w = wt_ref[...]
    slots = spread_w.shape[0] // 27
    lane = lax.broadcasted_iota(jnp.int32, (slots, rows), 1)
    first = lane == 0
    last = lane == rows - 1

    group = 32
    pooled_rows = group // 2
    pieces = pooled_rows // 2

    @pl.loop(0, plane // group)
    def _(j):
        ups = []
        for m in range(pieces):
            cot = cot_ref[:, pl.ds(pl.multiple_of((j * pieces + m) * rows, rows), rows)]
            ups.append(jnp.dot(cot, u_ref[0], preferred_element_type=jnp.float32) * 0.125)
            ups.append(jnp.dot(cot, u_ref[1], preferred_element_type=jnp.float32) * 0.125)
        spread_all = jnp.concatenate([ups[r // 2] for r in range(group)], axis=1)
        totals = [None] * pooled_rows
        wg = None
        bg = None
        spreads = []
        for px, base in enumerate((0, plane)):
            patches = [
                jnp.concatenate([p_ref[base + j * group + r, c] for r in range(group)], axis=1)
                for c in range(p_ref.shape[1])
            ]
            preact = bias
            for c, patch in enumerate(patches):
                preact = preact + jnp.dot(weight[c], patch, preferred_element_type=jnp.float32)
            scaled = soft_scale * preact
            e = jnp.exp(-jnp.abs(scaled))
            softplus = jnp.maximum(scaled, 0.0) + jnp.log1p(e)
            activated = leak_slope * preact + (1.0 - leak_slope) / soft_scale * softplus
            for h in range(pooled_rows):
                pair = (
                    activated[:, 2 * h * rows : (2 * h + 1) * rows]
                    + activated[:, (2 * h + 1) * rows : (2 * h + 2) * rows]
                )
                totals[h] = pair if totals[h] is None else totals[h] + pair
            sigmoid = jnp.where(scaled >= 0.0, 1.0, e) / (1.0 + e)
            slope = leak_slope + (1.0 - leak_slope) * sigmoid
            delta = (slope * spread_all).astype(jnp.bfloat16)
            term = jnp.stack(
                [
                    lax.dot_general(
                        delta, patch, (((1,), (1,)), ((), ())), preferred_element_type=jnp.float32
                    )
                    for patch in patches
                ]
            )
            wg = term if wg is None else wg + term
            part = delta.astype(jnp.float32)
            bg = part if bg is None else bg + part
            spreads.append(jnp.dot(spread_w, delta, preferred_element_type=jnp.float32))
        acc_main = {}
        acc_edge = {}
        for px in range(2):
            for r in range(group):
                cols = slice(r * rows, (r + 1) * rows)
                for a in range(3):
                    for b in range(3):
                        at = (a * 3 + b) * 3 * slots
                        g = spreads[px]
                        v0 = pltpu.roll(g[at : at + slots, cols], rows - 1, 1)
                        v1 = g[at + slots : at + 2 * slots, cols]
                        v2 = pltpu.roll(g[at + 2 * slots : at + 3 * slots, cols], 1, 1)
                        inner = jnp.where(last, 0.0, v0) + v1 + jnp.where(first, 0.0, v2)
                        edge = jnp.where(last, v0, 0.0) + jnp.where(first, v2, 0.0)
                        key = (px + a, r + b)
                        if key in acc_main:
                            acc_main[key] = acc_main[key] + inner
                            acc_edge[key] = acc_edge[key] + edge
                        else:
                            acc_main[key] = inner
                            acc_edge[key] = edge
        for (dx, dy), value in acc_main.items():
            out = (step * 2 + dx) * wide_y + (j * group + dy)
            main_ref[out] += value[: main_ref.shape[1]]
            edge_ref[out] += acc_edge[dx, dy][: edge_ref.shape[1]]
        wg_acc[...] += wg
        bg_acc[...] += jnp.sum(bg, axis=1, keepdims=True)
        for m in range(pieces):
            pooled = jnp.dot(
                totals[2 * m], q_ref[0], preferred_element_type=jnp.float32,
                precision=lax.Precision.HIGHEST,
            ) + jnp.dot(
                totals[2 * m + 1], q_ref[1], preferred_element_type=jnp.float32,
                precision=lax.Precision.HIGHEST,
            )
            at = pl.multiple_of((j * pieces + m) * rows, rows)
            pooled_ref[:, pl.ds(at, rows)] = (pooled * 0.125).astype(pooled_ref.dtype)

    @pl.when(step == pl.num_programs(0) - 1)
    def _():
        wg_ref[...] = wg_acc[...]
        bg_ref[...] = bg_acc[...]


def forward(weight, bias, patches, cot, pairs, wide_x, wide_y):
    lines, chan_in, window, rows = patches.shape
    chan_out = weight.shape[0]
    weight_mat = jnp.transpose(weight.reshape(chan_out, chan_in, window), (1, 0, 2))
    slots = 8
    spread_w = jnp.transpose(weight, (2, 3, 4, 1, 0))
    spread_w = jnp.pad(spread_w, ((0, 0), (0, 0), (0, 0), (0, slots - chan_in), (0, 0)))
    spread_w = spread_w.reshape(27 * slots, chan_out)
    half = rows // 2
    z = jnp.arange(rows)
    k = jnp.arange(rows)
    pool = jnp.stack(
        [(k[None, :] == z[:, None] // 2), (k[None, :] == half + z[:, None] // 2)]
    ).astype(jnp.float32)
    spread = jnp.stack(
        [(z[None, :] // 2 == k[:, None]), (z[None, :] // 2 + half == k[:, None])]
    ).astype(jnp.bfloat16)
    full = lambda shape: pl.BlockSpec(shape, lambda p: (0,) * len(shape))
    block = lines // pairs
    acc_shape = (wide_x * wide_y, chan_in, rows)
    return pl.pallas_call(
        lambda *refs: forward_kernel(rows, wide_y, *refs),
        grid=(pairs,),
        out_shape=(
            jax.ShapeDtypeStruct(cot.shape, jnp.bfloat16),
            jax.ShapeDtypeStruct((chan_in, chan_out, window), jnp.float32),
            jax.ShapeDtypeStruct((chan_out, 1), jnp.float32),
            jax.ShapeDtypeStruct(acc_shape, jnp.float32),
            jax.ShapeDtypeStruct(acc_shape, jnp.float32),
        ),
        in_specs=[
            full((chan_in, chan_out, window)),
            full((chan_out, 1)),
            full((2, rows, rows)),
            full((2, rows, rows)),
            full((27 * slots, chan_out)),
            pl.BlockSpec((block, chan_in, window, rows), lambda p: (p, 0, 0, 0)),
            pl.BlockSpec((chan_out, cot.shape[1] // pairs), lambda p: (0, p)),
        ],
        out_specs=(
            pl.BlockSpec((chan_out, cot.shape[1] // pairs), lambda p: (0, p)),
            full((chan_in, chan_out, window)),
            full((chan_out, 1)),
            full(acc_shape),
            full(acc_shape),
        ),
        scratch_shapes=[
            pltpu.VMEM((chan_in, chan_out, window), jnp.float32),
            pltpu.VMEM((chan_out, 1), jnp.float32),
        ],
    )(weight_mat, bias, pool, spread, spread_w, patches, cot)


def fold_halo(main, axis, dim, width):
    count = lax.axis_size(axis)
    size = main.shape[dim]
    head = lax.slice_in_dim(main, 0, width, axis=dim)
    tail = lax.slice_in_dim(main, size - width, size, axis=dim)
    from_left = lax.ppermute(tail, axis, [(i, (i + 1) % count) for i in range(count)])
    from_right = lax.ppermute(head, axis, [((i + 1) % count, i) for i in range(count)])
    inner = lax.slice_in_dim(main, width, size - width, axis=dim)
    inner_size = size - 2 * width
    start = [0] * main.ndim
    inner = lax.dynamic_update_slice(
        inner, lax.slice_in_dim(inner, 0, width, axis=dim) + from_left, start
    )
    start[dim] = inner_size - width
    inner = lax.dynamic_update_slice(
        inner, lax.slice_in_dim(inner, inner_size - width, inner_size, axis=dim) + from_right, start
    )
    return inner


def on_device(cells, weight, bias, cotangent):
    chan_in, cells_x, cells_y, cells_z = cells.shape
    chan_out = weight.shape[0]
    stencil = [
        (shift_a, shift_b, shift_e)
        for shift_a in range(3)
        for shift_b in range(3)
        for shift_e in range(3)
    ]
    widened = extended(cells, (("gx", 1), ("gy", 2), ("gz", 3)), 1)
    patches = jnp.stack(
        [
            jnp.transpose(
                widened[:, sa : sa + cells_x, sb : sb + cells_y, se : se + cells_z], (1, 2, 0, 3)
            )
            for sa, sb, se in stencil
        ],
        axis=3,
    )
    patches = patches.reshape(cells_x * cells_y, chan_in, 27, cells_z)
    cot = cotangent.reshape(chan_out, -1)
    wide_x, wide_y = cells_x + 2, cells_y + 2
    pooled, weight_local, bias_local, main, edge = forward(
        weight, bias.reshape(chan_out, 1), patches, cot, cells_x // 2, wide_x, wide_y
    )
    pooled = pooled.reshape(cotangent.shape)
    weight_local = jnp.transpose(weight_local, (1, 0, 2)).reshape(chan_out, -1)
    taps = chan_in * 27
    width = -(-(taps + 1) // 128) * 128
    partial = jnp.concatenate(
        [weight_local, bias_local, jnp.zeros((chan_out, width - taps - 1), jnp.float32)],
        axis=1,
    )
    sizes = tuple(lax.axis_size(a) for a in AXES)
    both = allreduce(partial, sizes)
    weight_grad = both[:, :taps].reshape(chan_out, chan_in, 3, 3, 3)
    bias_grad = both[:, taps]
    main = main.reshape(wide_x, wide_y, chan_in, cells_z)
    edge = edge.reshape(wide_x, wide_y, chan_in, cells_z)
    lo = edge[..., cells_z - 1 :]
    hi = edge[..., :1]
    count = lax.axis_size("gz")
    from_left = lax.ppermute(hi, "gz", [(i, (i + 1) % count) for i in range(count)])
    from_right = lax.ppermute(lo, "gz", [((i + 1) % count, i) for i in range(count)])
    main = jnp.concatenate(
        [
            main[..., :1] + from_left,
            main[..., 1 : cells_z - 1],
            main[..., cells_z - 1 :] + from_right,
        ],
        axis=3,
    )
    main = fold_halo(main, "gy", 1, 1)
    main = fold_halo(main, "gx", 0, 1)
    input_grad = jnp.transpose(main, (2, 0, 1, 3))
    return (pooled, weight_grad, bias_grad, input_grad)


def solution(mesh):
    in_specs = (P(None, "gx", "gy", "gz"), P(), P(), P(None, "gx", "gy", "gz"))
    out_specs = (P(None, "gx", "gy", "gz"), P(), P(), P(None, "gx", "gy", "gz"))
    return jax.shard_map(
        on_device, mesh=mesh, in_specs=in_specs, out_specs=out_specs, check_vma=False
    )
```

```python
import jax
import jax.numpy as jnp
from jax import lax
from jax.experimental import pallas as pl
from jax.experimental.pallas import tpu as pltpu
from jax.sharding import PartitionSpec as P

MESH = pl.DeviceIdType.MESH
AXES = ("gx", "gy", "gz")

leak_slope = 0.3
soft_scale = 10.0


def extended(cells, sides, width):
    for axis, dim in sides:
        count = lax.axis_size(axis)
        head = lax.slice_in_dim(cells, 0, width, axis=dim)
        tail = lax.slice_in_dim(cells, cells.shape[dim] - width, cells.shape[dim], axis=dim)
        cells = jnp.concatenate(
            [
                lax.ppermute(tail, axis, [(i, (i + 1) % count) for i in range(count)]),
                cells,
                lax.ppermute(head, axis, [((i + 1) % count, i) for i in range(count)]),
            ],
            axis=dim,
        )
    return cells


def allreduce_kernel(sizes, x_ref, o_ref, slots_a, slots_b, acc_a, send_a, recv_a, send_b, recv_b):
    me = tuple(lax.axis_index(a) for a in AXES)
    groups = (
        [(k,) for k in range(sizes[0])],
        [(k, m) for k in range(sizes[1]) for m in range(sizes[2])],
    )
    places = ((0,), (1, 2))

    def device(phase, member):
        coords = list(me)
        for axis, value in zip(places[phase], member):
            coords[axis] = value
        return tuple(coords)

    def rank(phase):
        out = 0
        for axis in places[phase]:
            out = out * sizes[axis] + me[axis]
        return out

    def member_of(phase, index):
        out = []
        for axis in reversed(places[phase]):
            out.append(lax.rem(index, sizes[axis]))
            index = index // sizes[axis]
        return tuple(reversed(out))

    barrier = pltpu.get_barrier_semaphore()
    count = 0
    for phase in range(2):
        n = len(groups[phase])
        for d in range(1, n):
            target = member_of(phase, lax.rem(rank(phase) + d, n))
            pl.semaphore_signal(barrier, inc=1, device_id=device(phase, target), device_id_type=MESH)
            count += 1
    pl.semaphore_wait(barrier, count)

    slots = (slots_a, slots_b)
    sends = (send_a, send_b)
    recvs = (recv_a, recv_b)
    sources = (x_ref, acc_a)
    sinks = (acc_a, o_ref)
    for phase in range(2):
        n = len(groups[phase])
        src, held, sink = sources[phase], slots[phase], sinks[phase]
        mine = rank(phase)
        copies = []
        for d in range(1, n):
            target = member_of(phase, lax.rem(mine + d, n))
            copy = pltpu.make_async_remote_copy(
                src_ref=src,
                dst_ref=held.at[mine],
                send_sem=sends[phase].at[d],
                recv_sem=recvs[phase].at[mine],
                device_id=device(phase, target),
                device_id_type=MESH,
            )
            copy.start()
            copies.append(copy)
        held[mine] = src[...]
        for d in range(1, n):
            origin = lax.rem(mine + n - d, n)
            incoming = pltpu.make_async_remote_copy(
                src_ref=src,
                dst_ref=held.at[origin],
                send_sem=sends[phase].at[d],
                recv_sem=recvs[phase].at[origin],
                device_id=device(phase, member_of(phase, origin)),
                device_id_type=MESH,
            )
            incoming.wait_recv()
        for copy in copies:
            copy.wait_send()
        total = held[0]
        for k in range(1, n):
            total = total + held[k]
        sink[...] = total


def allreduce(x, sizes):
    shape = x.shape
    first, second = sizes[0], sizes[1] * sizes[2]
    return pl.pallas_call(
        lambda *refs: allreduce_kernel(sizes, *refs),
        out_shape=jax.ShapeDtypeStruct(shape, jnp.float32),
        in_specs=[pl.BlockSpec(memory_space=pltpu.VMEM)],
        out_specs=pl.BlockSpec(memory_space=pltpu.VMEM),
        scratch_shapes=[
            pltpu.VMEM((first,) + shape, jnp.float32),
            pltpu.VMEM((second,) + shape, jnp.float32),
            pltpu.VMEM(shape, jnp.float32),
            pltpu.SemaphoreType.DMA((first,)),
            pltpu.SemaphoreType.DMA((first,)),
            pltpu.SemaphoreType.DMA((second,)),
            pltpu.SemaphoreType.DMA((second,)),
        ],
        compiler_params=pltpu.CompilerParams(collective_id=0, has_side_effects=True),
    )(x)


def forward_kernel(rows, wide_y, w_ref, b_ref, q_ref, u_ref, wt_ref, p_ref, cot_ref,
                   pooled_ref, wg_ref, bg_ref, main_ref, edge_ref, wg_acc, bg_acc):
    step = pl.program_id(0)
    plane = p_ref.shape[0] // 2
    lines = plane // 4

    @pl.when(step == 0)
    def _():
        wg_acc[...] = jnp.zeros_like(wg_acc)
        bg_acc[...] = jnp.zeros_like(bg_acc)
        main_ref[...] = jnp.zeros_like(main_ref)
        edge_ref[...] = jnp.zeros_like(edge_ref)

    weight = w_ref[...]
    bias = b_ref[...]
    spread_w = wt_ref[...]
    slots = spread_w.shape[0] // 27
    lane = lax.broadcasted_iota(jnp.int32, (slots, rows), 1)
    first = lane == 0
    last = lane == rows - 1

    group = 32
    pooled_rows = group // 2
    pieces = pooled_rows // 2

    @pl.loop(0, plane // group)
    def _(j):
        ups = []
        for m in range(pieces):
            cot = cot_ref[:, pl.ds(pl.multiple_of((j * pieces + m) * rows, rows), rows)]
            ups.append(jnp.dot(cot, u_ref[0], preferred_element_type=jnp.float32) * 0.125)
            ups.append(jnp.dot(cot, u_ref[1], preferred_element_type=jnp.float32) * 0.125)
        spread_all = jnp.concatenate([ups[r // 2] for r in range(group)], axis=1)
        totals = [None] * pooled_rows
        wg = None
        bg = None
        spreads = []
        for px, base in enumerate((0, plane)):
            patch = jnp.concatenate([p_ref[base + j * group + r] for r in range(group)], axis=1)
            preact = jnp.dot(weight, patch, preferred_element_type=jnp.float32) + bias
            scaled = soft_scale * preact
            e = jnp.exp(-jnp.abs(scaled))
            softplus = jnp.maximum(scaled, 0.0) + jnp.log1p(e)
            activated = leak_slope * preact + (1.0 - leak_slope) / soft_scale * softplus
            for h in range(pooled_rows):
                pair = (
                    activated[:, 2 * h * rows : (2 * h + 1) * rows]
                    + activated[:, (2 * h + 1) * rows : (2 * h + 2) * rows]
                )
                totals[h] = pair if totals[h] is None else totals[h] + pair
            sigmoid = jnp.where(scaled >= 0.0, 1.0, e) / (1.0 + e)
            slope = leak_slope + (1.0 - leak_slope) * sigmoid
            delta = (slope * spread_all).astype(jnp.bfloat16)
            term = lax.dot_general(
                delta, patch, (((1,), (1,)), ((), ())), preferred_element_type=jnp.float32
            )
            wg = term if wg is None else wg + term
            part = delta.astype(jnp.float32)
            bg = part if bg is None else bg + part
            spreads.append(jnp.dot(spread_w, delta, preferred_element_type=jnp.float32))
        acc_main = {}
        acc_edge = {}
        for px in range(2):
            for r in range(group):
                cols = slice(r * rows, (r + 1) * rows)
                for a in range(3):
                    for b in range(3):
                        at = (a * 3 + b) * 3 * slots
                        g = spreads[px]
                        v0 = pltpu.roll(g[at : at + slots, cols], rows - 1, 1)
                        v1 = g[at + slots : at + 2 * slots, cols]
                        v2 = pltpu.roll(g[at + 2 * slots : at + 3 * slots, cols], 1, 1)
                        inner = jnp.where(last, 0.0, v0) + v1 + jnp.where(first, 0.0, v2)
                        edge = jnp.where(last, v0, 0.0) + jnp.where(first, v2, 0.0)
                        key = (px + a, r + b)
                        if key in acc_main:
                            acc_main[key] = acc_main[key] + inner
                            acc_edge[key] = acc_edge[key] + edge
                        else:
                            acc_main[key] = inner
                            acc_edge[key] = edge
        for (dx, dy), value in acc_main.items():
            out = (step * 2 + dx) * wide_y + (j * group + dy)
            main_ref[out] += value[: main_ref.shape[1]]
            edge_ref[out] += acc_edge[dx, dy][: edge_ref.shape[1]]
        wg_acc[...] += wg
        bg_acc[...] += jnp.sum(bg, axis=1, keepdims=True)
        for m in range(pieces):
            pooled = None
            for half in range(2):
                value = totals[2 * m + half]
                high = value.astype(jnp.bfloat16)
                low = (value - high.astype(jnp.float32)).astype(jnp.bfloat16)
                both = jnp.concatenate([high, low], axis=0)
                part = jnp.dot(both, q_ref[half], preferred_element_type=jnp.float32)
                part = part[: value.shape[0]] + part[value.shape[0] :]
                pooled = part if pooled is None else pooled + part
            at = pl.multiple_of((j * pieces + m) * rows, rows)
            pooled_ref[:, pl.ds(at, rows)] = (pooled * 0.125).astype(pooled_ref.dtype)

    @pl.when(step == pl.num_programs(0) - 1)
    def _():
        wg_ref[...] = wg_acc[...]
        bg_ref[...] = bg_acc[...]


def forward(weight, bias, patches, cot, pairs, wide_x, wide_y):
    lines, taps, rows = patches.shape
    chan_out, chan_in = weight.shape[:2]
    weight_mat = weight.reshape(chan_out, taps)
    slots = 8
    spread_w = jnp.transpose(weight, (2, 3, 4, 1, 0))
    spread_w = jnp.pad(spread_w, ((0, 0), (0, 0), (0, 0), (0, slots - chan_in), (0, 0)))
    spread_w = spread_w.reshape(27 * slots, chan_out)
    half = rows // 2
    z = jnp.arange(rows)
    k = jnp.arange(rows)
    pool = jnp.stack(
        [(k[None, :] == z[:, None] // 2), (k[None, :] == half + z[:, None] // 2)]
    ).astype(jnp.bfloat16)
    spread = jnp.stack(
        [(z[None, :] // 2 == k[:, None]), (z[None, :] // 2 + half == k[:, None])]
    ).astype(jnp.bfloat16)
    full = lambda shape: pl.BlockSpec(shape, lambda p: (0,) * len(shape))
    block = lines // pairs
    acc_shape = (wide_x * wide_y, chan_in, rows)
    return pl.pallas_call(
        lambda *refs: forward_kernel(rows, wide_y, *refs),
        grid=(pairs,),
        out_shape=(
            jax.ShapeDtypeStruct(cot.shape, jnp.bfloat16),
            jax.ShapeDtypeStruct((chan_out, taps), jnp.float32),
            jax.ShapeDtypeStruct((chan_out, 1), jnp.float32),
            jax.ShapeDtypeStruct(acc_shape, jnp.float32),
            jax.ShapeDtypeStruct(acc_shape, jnp.float32),
        ),
        in_specs=[
            full((chan_out, taps)),
            full((chan_out, 1)),
            full((2, rows, rows)),
            full((2, rows, rows)),
            full((27 * slots, chan_out)),
            pl.BlockSpec((block, taps, rows), lambda p: (p, 0, 0)),
            pl.BlockSpec((chan_out, cot.shape[1] // pairs), lambda p: (0, p)),
        ],
        out_specs=(
            pl.BlockSpec((chan_out, cot.shape[1] // pairs), lambda p: (0, p)),
            full((chan_out, taps)),
            full((chan_out, 1)),
            full(acc_shape),
            full(acc_shape),
        ),
        scratch_shapes=[
            pltpu.VMEM((chan_out, taps), jnp.float32),
            pltpu.VMEM((chan_out, 1), jnp.float32),
        ],
    )(weight_mat, bias, pool, spread, spread_w, patches, cot)


def fold_halo(main, axis, dim, width):
    count = lax.axis_size(axis)
    size = main.shape[dim]
    head = lax.slice_in_dim(main, 0, width, axis=dim)
    tail = lax.slice_in_dim(main, size - width, size, axis=dim)
    from_left = lax.ppermute(tail, axis, [(i, (i + 1) % count) for i in range(count)])
    from_right = lax.ppermute(head, axis, [((i + 1) % count, i) for i in range(count)])
    inner = lax.slice_in_dim(main, width, size - width, axis=dim)
    inner_size = size - 2 * width
    start = [0] * main.ndim
    inner = lax.dynamic_update_slice(
        inner, lax.slice_in_dim(inner, 0, width, axis=dim) + from_left, start
    )
    start[dim] = inner_size - width
    inner = lax.dynamic_update_slice(
        inner, lax.slice_in_dim(inner, inner_size - width, inner_size, axis=dim) + from_right, start
    )
    return inner


def on_device(cells, weight, bias, cotangent):
    chan_in, cells_x, cells_y, cells_z = cells.shape
    chan_out = weight.shape[0]
    stencil = [
        (shift_a, shift_b, shift_e)
        for shift_a in range(3)
        for shift_b in range(3)
        for shift_e in range(3)
    ]
    widened = extended(cells, (("gx", 1), ("gy", 2), ("gz", 3)), 1)
    patches = jnp.stack(
        [
            jnp.transpose(
                widened[:, sa : sa + cells_x, sb : sb + cells_y, se : se + cells_z], (1, 2, 0, 3)
            )
            for sa, sb, se in stencil
        ],
        axis=3,
    )
    patches = patches.reshape(cells_x * cells_y, chan_in * 27, cells_z)
    cot = cotangent.reshape(chan_out, -1)
    wide_x, wide_y = cells_x + 2, cells_y + 2
    pooled, weight_local, bias_local, main, edge = forward(
        weight, bias.reshape(chan_out, 1), patches, cot, cells_x // 2, wide_x, wide_y
    )
    pooled = pooled.reshape(cotangent.shape)
    taps = chan_in * 27
    width = -(-(taps + 1) // 128) * 128
    partial = jnp.concatenate(
        [weight_local, bias_local, jnp.zeros((chan_out, width - taps - 1), jnp.float32)],
        axis=1,
    )
    sizes = tuple(lax.axis_size(a) for a in AXES)
    both = allreduce(partial, sizes)
    weight_grad = both[:, :taps].reshape(chan_out, chan_in, 3, 3, 3)
    bias_grad = both[:, taps]
    main = main.reshape(wide_x, wide_y, chan_in, cells_z)
    edge = edge.reshape(wide_x, wide_y, chan_in, cells_z)
    lo = edge[..., cells_z - 1 :]
    hi = edge[..., :1]
    count = lax.axis_size("gz")
    from_left = lax.ppermute(hi, "gz", [(i, (i + 1) % count) for i in range(count)])
    from_right = lax.ppermute(lo, "gz", [((i + 1) % count, i) for i in range(count)])
    main = jnp.concatenate(
        [
            main[..., :1] + from_left,
            main[..., 1 : cells_z - 1],
            main[..., cells_z - 1 :] + from_right,
        ],
        axis=3,
    )
    main = fold_halo(main, "gy", 1, 1)
    main = fold_halo(main, "gx", 0, 1)
    input_grad = jnp.transpose(main, (2, 0, 1, 3))
    return (pooled, weight_grad, bias_grad, input_grad)


def solution(mesh):
    in_specs = (P(None, "gx", "gy", "gz"), P(), P(), P(None, "gx", "gy", "gz"))
    out_specs = (P(None, "gx", "gy", "gz"), P(), P(), P(None, "gx", "gy", "gz"))
    return jax.shard_map(
        on_device, mesh=mesh, in_specs=in_specs, out_specs=out_specs, check_vma=False
    )
```

```python
import jax
import jax.numpy as jnp
from jax import lax
from jax.experimental import pallas as pl
from jax.experimental.pallas import tpu as pltpu
from jax.sharding import PartitionSpec as P

MESH = pl.DeviceIdType.MESH
AXES = ("gx", "gy", "gz")

leak_slope = 0.3
soft_scale = 10.0


def extended(cells, sides, width):
    for axis, dim in sides:
        count = lax.axis_size(axis)
        head = lax.slice_in_dim(cells, 0, width, axis=dim)
        tail = lax.slice_in_dim(cells, cells.shape[dim] - width, cells.shape[dim], axis=dim)
        cells = jnp.concatenate(
            [
                lax.ppermute(tail, axis, [(i, (i + 1) % count) for i in range(count)]),
                cells,
                lax.ppermute(head, axis, [((i + 1) % count, i) for i in range(count)]),
            ],
            axis=dim,
        )
    return cells


def allreduce_kernel(sizes, x_ref, o_ref, slots_a, slots_b, acc_a, send_a, recv_a, send_b, recv_b):
    me = tuple(lax.axis_index(a) for a in AXES)
    groups = (
        [(k,) for k in range(sizes[0])],
        [(k, m) for k in range(sizes[1]) for m in range(sizes[2])],
    )
    places = ((0,), (1, 2))

    def device(phase, member):
        coords = list(me)
        for axis, value in zip(places[phase], member):
            coords[axis] = value
        return tuple(coords)

    def rank(phase):
        out = 0
        for axis in places[phase]:
            out = out * sizes[axis] + me[axis]
        return out

    def member_of(phase, index):
        out = []
        for axis in reversed(places[phase]):
            out.append(lax.rem(index, sizes[axis]))
            index = index // sizes[axis]
        return tuple(reversed(out))

    barrier = pltpu.get_barrier_semaphore()
    count = 0
    for phase in range(2):
        n = len(groups[phase])
        for d in range(1, n):
            target = member_of(phase, lax.rem(rank(phase) + d, n))
            pl.semaphore_signal(barrier, inc=1, device_id=device(phase, target), device_id_type=MESH)
            count += 1
    pl.semaphore_wait(barrier, count)

    slots = (slots_a, slots_b)
    sends = (send_a, send_b)
    recvs = (recv_a, recv_b)
    sources = (x_ref, acc_a)
    sinks = (acc_a, o_ref)
    for phase in range(2):
        n = len(groups[phase])
        src, held, sink = sources[phase], slots[phase], sinks[phase]
        mine = rank(phase)
        copies = []
        for d in range(1, n):
            target = member_of(phase, lax.rem(mine + d, n))
            copy = pltpu.make_async_remote_copy(
                src_ref=src,
                dst_ref=held.at[mine],
                send_sem=sends[phase].at[d],
                recv_sem=recvs[phase].at[mine],
                device_id=device(phase, target),
                device_id_type=MESH,
            )
            copy.start()
            copies.append(copy)
        held[mine] = src[...]
        for d in range(1, n):
            origin = lax.rem(mine + n - d, n)
            incoming = pltpu.make_async_remote_copy(
                src_ref=src,
                dst_ref=held.at[origin],
                send_sem=sends[phase].at[d],
                recv_sem=recvs[phase].at[origin],
                device_id=device(phase, member_of(phase, origin)),
                device_id_type=MESH,
            )
            incoming.wait_recv()
        for copy in copies:
            copy.wait_send()
        total = held[0]
        for k in range(1, n):
            total = total + held[k]
        sink[...] = total


def allreduce(x, sizes):
    shape = x.shape
    first, second = sizes[0], sizes[1] * sizes[2]
    return pl.pallas_call(
        lambda *refs: allreduce_kernel(sizes, *refs),
        out_shape=jax.ShapeDtypeStruct(shape, jnp.float32),
        in_specs=[pl.BlockSpec(memory_space=pltpu.VMEM)],
        out_specs=pl.BlockSpec(memory_space=pltpu.VMEM),
        scratch_shapes=[
            pltpu.VMEM((first,) + shape, jnp.float32),
            pltpu.VMEM((second,) + shape, jnp.float32),
            pltpu.VMEM(shape, jnp.float32),
            pltpu.SemaphoreType.DMA((first,)),
            pltpu.SemaphoreType.DMA((first,)),
            pltpu.SemaphoreType.DMA((second,)),
            pltpu.SemaphoreType.DMA((second,)),
        ],
        compiler_params=pltpu.CompilerParams(collective_id=0, has_side_effects=True),
    )(x)


def forward_kernel(rows, wide_y, w_ref, b_ref, q_ref, u_ref, wt_ref, p_ref, cot_ref,
                   pooled_ref, wg_ref, bg_ref, main_ref, edge_ref, wg_acc, bg_acc):
    step = pl.program_id(0)
    plane = p_ref.shape[0] // 2
    lines = plane // 4

    @pl.when(step == 0)
    def _():
        wg_acc[...] = jnp.zeros_like(wg_acc)
        bg_acc[...] = jnp.zeros_like(bg_acc)
        main_ref[...] = jnp.zeros_like(main_ref)
        edge_ref[...] = jnp.zeros_like(edge_ref)

    weight = w_ref[...]
    bias = b_ref[...]
    spread_w = wt_ref[...]
    slots = spread_w.shape[0] // 27
    lane = lax.broadcasted_iota(jnp.int32, (slots, rows), 1)
    first = lane == 0
    last = lane == rows - 1

    group = 32
    pooled_rows = group // 2
    pieces = pooled_rows // 2

    @pl.loop(0, plane // group)
    def _(j):
        ups = []
        for m in range(pieces):
            cot = cot_ref[:, pl.ds(pl.multiple_of((j * pieces + m) * rows, rows), rows)]
            ups.append(jnp.dot(cot, u_ref[0], preferred_element_type=jnp.float32) * 0.125)
            ups.append(jnp.dot(cot, u_ref[1], preferred_element_type=jnp.float32) * 0.125)
        spread_all = jnp.concatenate([ups[r // 2] for r in range(group)], axis=1)
        totals = [None] * pooled_rows
        wg = None
        bg = None
        spreads = []
        for px, base in enumerate((0, plane)):
            patch = jnp.concatenate([p_ref[base + j * group + r] for r in range(group)], axis=1)
            preact = jnp.dot(weight, patch, preferred_element_type=jnp.float32) + bias
            scaled = soft_scale * preact
            e = jnp.exp(-jnp.abs(scaled))
            softplus = jnp.maximum(scaled, 0.0) + jnp.log1p(e)
            activated = leak_slope * preact + (1.0 - leak_slope) / soft_scale * softplus
            for h in range(pooled_rows):
                pair = (
                    activated[:, 2 * h * rows : (2 * h + 1) * rows]
                    + activated[:, (2 * h + 1) * rows : (2 * h + 2) * rows]
                )
                totals[h] = pair if totals[h] is None else totals[h] + pair
            sigmoid = jnp.where(scaled >= 0.0, 1.0, e) / (1.0 + e)
            slope = leak_slope + (1.0 - leak_slope) * sigmoid
            delta = (slope * spread_all).astype(jnp.bfloat16)
            term = lax.dot_general(
                patch, delta, (((1,), (1,)), ((), ())), preferred_element_type=jnp.float32
            )
            wg = term if wg is None else wg + term
            part = delta.astype(jnp.float32)
            bg = part if bg is None else bg + part
            spreads.append(jnp.dot(spread_w, delta, preferred_element_type=jnp.float32))
        acc_main = {}
        acc_edge = {}
        for px in range(2):
            for r in range(group):
                cols = slice(r * rows, (r + 1) * rows)
                for a in range(3):
                    for b in range(3):
                        at = (a * 3 + b) * 3 * slots
                        g = spreads[px]
                        v0 = pltpu.roll(g[at : at + slots, cols], rows - 1, 1)
                        v1 = g[at + slots : at + 2 * slots, cols]
                        v2 = pltpu.roll(g[at + 2 * slots : at + 3 * slots, cols], 1, 1)
                        inner = jnp.where(last, 0.0, v0) + v1 + jnp.where(first, 0.0, v2)
                        edge = jnp.where(last, v0, 0.0) + jnp.where(first, v2, 0.0)
                        key = (px + a, r + b)
                        if key in acc_main:
                            acc_main[key] = acc_main[key] + inner
                            acc_edge[key] = acc_edge[key] + edge
                        else:
                            acc_main[key] = inner
                            acc_edge[key] = edge
        for (dx, dy), value in acc_main.items():
            out = (step * 2 + dx) * wide_y + (j * group + dy)
            main_ref[out] += value[: main_ref.shape[1]]
            edge_ref[out] += acc_edge[dx, dy][: edge_ref.shape[1]]
        wg_acc[...] += wg
        bg_acc[...] += jnp.sum(bg, axis=1, keepdims=True)
        for m in range(pieces):
            pooled = None
            for half in range(2):
                value = totals[2 * m + half]
                high = value.astype(jnp.bfloat16)
                low = (value - high.astype(jnp.float32)).astype(jnp.bfloat16)
                both = jnp.concatenate([high, low], axis=0)
                part = jnp.dot(both, q_ref[half], preferred_element_type=jnp.float32)
                part = part[: value.shape[0]] + part[value.shape[0] :]
                pooled = part if pooled is None else pooled + part
            at = pl.multiple_of((j * pieces + m) * rows, rows)
            pooled_ref[:, pl.ds(at, rows)] = (pooled * 0.125).astype(pooled_ref.dtype)

    @pl.when(step == pl.num_programs(0) - 1)
    def _():
        wg_ref[...] = wg_acc[...]
        bg_ref[...] = bg_acc[...]


def forward(weight, bias, patches, cot, pairs, wide_x, wide_y):
    lines, taps, rows = patches.shape
    chan_out, chan_in = weight.shape[:2]
    weight_mat = weight.reshape(chan_out, taps)
    slots = 8
    spread_w = jnp.transpose(weight, (2, 3, 4, 1, 0))
    spread_w = jnp.pad(spread_w, ((0, 0), (0, 0), (0, 0), (0, slots - chan_in), (0, 0)))
    spread_w = spread_w.reshape(27 * slots, chan_out)
    half = rows // 2
    z = jnp.arange(rows)
    k = jnp.arange(rows)
    pool = jnp.stack(
        [(k[None, :] == z[:, None] // 2), (k[None, :] == half + z[:, None] // 2)]
    ).astype(jnp.bfloat16)
    spread = jnp.stack(
        [(z[None, :] // 2 == k[:, None]), (z[None, :] // 2 + half == k[:, None])]
    ).astype(jnp.bfloat16)
    full = lambda shape: pl.BlockSpec(shape, lambda p: (0,) * len(shape))
    block = lines // pairs
    acc_shape = (wide_x * wide_y, chan_in, rows)
    return pl.pallas_call(
        lambda *refs: forward_kernel(rows, wide_y, *refs),
        grid=(pairs,),
        out_shape=(
            jax.ShapeDtypeStruct(cot.shape, jnp.bfloat16),
            jax.ShapeDtypeStruct((taps, chan_out), jnp.float32),
            jax.ShapeDtypeStruct((chan_out, 1), jnp.float32),
            jax.ShapeDtypeStruct(acc_shape, jnp.float32),
            jax.ShapeDtypeStruct(acc_shape, jnp.float32),
        ),
        in_specs=[
            full((chan_out, taps)),
            full((chan_out, 1)),
            full((2, rows, rows)),
            full((2, rows, rows)),
            full((27 * slots, chan_out)),
            pl.BlockSpec((block, taps, rows), lambda p: (p, 0, 0)),
            pl.BlockSpec((chan_out, cot.shape[1] // pairs), lambda p: (0, p)),
        ],
        out_specs=(
            pl.BlockSpec((chan_out, cot.shape[1] // pairs), lambda p: (0, p)),
            full((taps, chan_out)),
            full((chan_out, 1)),
            full(acc_shape),
            full(acc_shape),
        ),
        scratch_shapes=[
            pltpu.VMEM((taps, chan_out), jnp.float32),
            pltpu.VMEM((chan_out, 1), jnp.float32),
        ],
    )(weight_mat, bias, pool, spread, spread_w, patches, cot)


def fold_halo(main, axis, dim, width):
    count = lax.axis_size(axis)
    size = main.shape[dim]
    head = lax.slice_in_dim(main, 0, width, axis=dim)
    tail = lax.slice_in_dim(main, size - width, size, axis=dim)
    from_left = lax.ppermute(tail, axis, [(i, (i + 1) % count) for i in range(count)])
    from_right = lax.ppermute(head, axis, [((i + 1) % count, i) for i in range(count)])
    inner = lax.slice_in_dim(main, width, size - width, axis=dim)
    inner_size = size - 2 * width
    start = [0] * main.ndim
    inner = lax.dynamic_update_slice(
        inner, lax.slice_in_dim(inner, 0, width, axis=dim) + from_left, start
    )
    start[dim] = inner_size - width
    inner = lax.dynamic_update_slice(
        inner, lax.slice_in_dim(inner, inner_size - width, inner_size, axis=dim) + from_right, start
    )
    return inner


def on_device(cells, weight, bias, cotangent):
    chan_in, cells_x, cells_y, cells_z = cells.shape
    chan_out = weight.shape[0]
    stencil = [
        (shift_a, shift_b, shift_e)
        for shift_a in range(3)
        for shift_b in range(3)
        for shift_e in range(3)
    ]
    widened = extended(cells, (("gx", 1), ("gy", 2), ("gz", 3)), 1)
    patches = jnp.stack(
        [
            jnp.transpose(
                widened[:, sa : sa + cells_x, sb : sb + cells_y, se : se + cells_z], (1, 2, 0, 3)
            )
            for sa, sb, se in stencil
        ],
        axis=3,
    )
    patches = patches.reshape(cells_x * cells_y, chan_in * 27, cells_z)
    cot = cotangent.reshape(chan_out, -1)
    wide_x, wide_y = cells_x + 2, cells_y + 2
    pooled, weight_local, bias_local, main, edge = forward(
        weight, bias.reshape(chan_out, 1), patches, cot, cells_x // 2, wide_x, wide_y
    )
    pooled = pooled.reshape(cotangent.shape)
    weight_local = weight_local.T
    taps = chan_in * 27
    width = -(-(taps + 1) // 128) * 128
    partial = jnp.concatenate(
        [weight_local, bias_local, jnp.zeros((chan_out, width - taps - 1), jnp.float32)],
        axis=1,
    )
    sizes = tuple(lax.axis_size(a) for a in AXES)
    both = allreduce(partial, sizes)
    weight_grad = both[:, :taps].reshape(chan_out, chan_in, 3, 3, 3)
    bias_grad = both[:, taps]
    main = main.reshape(wide_x, wide_y, chan_in, cells_z)
    edge = edge.reshape(wide_x, wide_y, chan_in, cells_z)
    lo = edge[..., cells_z - 1 :]
    hi = edge[..., :1]
    count = lax.axis_size("gz")
    from_left = lax.ppermute(hi, "gz", [(i, (i + 1) % count) for i in range(count)])
    from_right = lax.ppermute(lo, "gz", [((i + 1) % count, i) for i in range(count)])
    main = jnp.concatenate(
        [
            main[..., :1] + from_left,
            main[..., 1 : cells_z - 1],
            main[..., cells_z - 1 :] + from_right,
        ],
        axis=3,
    )
    main = fold_halo(main, "gy", 1, 1)
    main = fold_halo(main, "gx", 0, 1)
    input_grad = jnp.transpose(main, (2, 0, 1, 3))
    return (pooled, weight_grad, bias_grad, input_grad)


def solution(mesh):
    in_specs = (P(None, "gx", "gy", "gz"), P(), P(), P(None, "gx", "gy", "gz"))
    out_specs = (P(None, "gx", "gy", "gz"), P(), P(), P(None, "gx", "gy", "gz"))
    return jax.shard_map(
        on_device, mesh=mesh, in_specs=in_specs, out_specs=out_specs, check_vma=False
    )
```

```python
import jax
import jax.numpy as jnp
from jax import lax
from jax.experimental import pallas as pl
from jax.experimental.pallas import tpu as pltpu
from jax.sharding import PartitionSpec as P

MESH = pl.DeviceIdType.MESH
BLOCK_ROWS = 32
AXES = ("gx", "gy", "gz")

leak_slope = 0.3
soft_scale = 10.0


def extended(cells, sides, width):
    for axis, dim in sides:
        count = lax.axis_size(axis)
        head = lax.slice_in_dim(cells, 0, width, axis=dim)
        tail = lax.slice_in_dim(cells, cells.shape[dim] - width, cells.shape[dim], axis=dim)
        cells = jnp.concatenate(
            [
                lax.ppermute(tail, axis, [(i, (i + 1) % count) for i in range(count)]),
                cells,
                lax.ppermute(head, axis, [((i + 1) % count, i) for i in range(count)]),
            ],
            axis=dim,
        )
    return cells


def allreduce_kernel(sizes, x_ref, o_ref, slots_a, slots_b, acc_a, send_a, recv_a, send_b, recv_b):
    me = tuple(lax.axis_index(a) for a in AXES)
    groups = (
        [(k,) for k in range(sizes[0])],
        [(k, m) for k in range(sizes[1]) for m in range(sizes[2])],
    )
    places = ((0,), (1, 2))

    def device(phase, member):
        coords = list(me)
        for axis, value in zip(places[phase], member):
            coords[axis] = value
        return tuple(coords)

    def rank(phase):
        out = 0
        for axis in places[phase]:
            out = out * sizes[axis] + me[axis]
        return out

    def member_of(phase, index):
        out = []
        for axis in reversed(places[phase]):
            out.append(lax.rem(index, sizes[axis]))
            index = index // sizes[axis]
        return tuple(reversed(out))

    barrier = pltpu.get_barrier_semaphore()
    count = 0
    for phase in range(2):
        n = len(groups[phase])
        for d in range(1, n):
            target = member_of(phase, lax.rem(rank(phase) + d, n))
            pl.semaphore_signal(barrier, inc=1, device_id=device(phase, target), device_id_type=MESH)
            count += 1
    pl.semaphore_wait(barrier, count)

    slots = (slots_a, slots_b)
    sends = (send_a, send_b)
    recvs = (recv_a, recv_b)
    sources = (x_ref, acc_a)
    sinks = (acc_a, o_ref)
    for phase in range(2):
        n = len(groups[phase])
        src, held, sink = sources[phase], slots[phase], sinks[phase]
        mine = rank(phase)
        copies = []
        for d in range(1, n):
            target = member_of(phase, lax.rem(mine + d, n))
            copy = pltpu.make_async_remote_copy(
                src_ref=src,
                dst_ref=held.at[mine],
                send_sem=sends[phase].at[d],
                recv_sem=recvs[phase].at[mine],
                device_id=device(phase, target),
                device_id_type=MESH,
            )
            copy.start()
            copies.append(copy)
        held[mine] = src[...]
        for d in range(1, n):
            origin = lax.rem(mine + n - d, n)
            incoming = pltpu.make_async_remote_copy(
                src_ref=src,
                dst_ref=held.at[origin],
                send_sem=sends[phase].at[d],
                recv_sem=recvs[phase].at[origin],
                device_id=device(phase, member_of(phase, origin)),
                device_id_type=MESH,
            )
            incoming.wait_recv()
        for copy in copies:
            copy.wait_send()
        total = held[0]
        for k in range(1, n):
            total = total + held[k]
        sink[...] = total


def allreduce(x, sizes):
    shape = x.shape
    first, second = sizes[0], sizes[1] * sizes[2]
    return pl.pallas_call(
        lambda *refs: allreduce_kernel(sizes, *refs),
        out_shape=jax.ShapeDtypeStruct(shape, jnp.float32),
        in_specs=[pl.BlockSpec(memory_space=pltpu.VMEM)],
        out_specs=pl.BlockSpec(memory_space=pltpu.VMEM),
        scratch_shapes=[
            pltpu.VMEM((first,) + shape, jnp.float32),
            pltpu.VMEM((second,) + shape, jnp.float32),
            pltpu.VMEM(shape, jnp.float32),
            pltpu.SemaphoreType.DMA((first,)),
            pltpu.SemaphoreType.DMA((first,)),
            pltpu.SemaphoreType.DMA((second,)),
            pltpu.SemaphoreType.DMA((second,)),
        ],
        compiler_params=pltpu.CompilerParams(collective_id=0, has_side_effects=True),
    )(x)


def forward_kernel(rows, wide_y, w_ref, b_ref, q_ref, u_ref, wt_ref, ones_ref, p_ref, cot_ref,
                   pooled_ref, wg_ref, bg_ref, main_ref, edge_ref, wg_acc, bg_acc):
    step = pl.program_id(0)
    plane = p_ref.shape[0] // 2
    lines = plane // 4

    @pl.when(step == 0)
    def _():
        wg_acc[...] = jnp.zeros_like(wg_acc)
        bg_acc[...] = jnp.zeros_like(bg_acc)
        main_ref[...] = jnp.zeros_like(main_ref)
        edge_ref[...] = jnp.zeros_like(edge_ref)

    weight = w_ref[...]
    bias = b_ref[...]
    spread_w = wt_ref[...]
    slots = spread_w.shape[0] // 27
    lane = lax.broadcasted_iota(jnp.int32, (slots, rows), 1)
    first = lane == 0
    last = lane == rows - 1

    group = BLOCK_ROWS
    pooled_rows = group // 2
    pieces = pooled_rows // 2

    @pl.loop(0, plane // group)
    def _(j):
        ups = []
        for m in range(pieces):
            cot = cot_ref[:, pl.ds(pl.multiple_of((j * pieces + m) * rows, rows), rows)]
            ups.append(jnp.dot(cot, u_ref[0], preferred_element_type=jnp.float32) * 0.125)
            ups.append(jnp.dot(cot, u_ref[1], preferred_element_type=jnp.float32) * 0.125)
        spread_all = jnp.concatenate([ups[r // 2] for r in range(group)], axis=1)
        totals = [None] * pooled_rows
        wg = None
        bg = None
        spreads = []
        for px, base in enumerate((0, plane)):
            patch = jnp.concatenate([p_ref[base + j * group + r] for r in range(group)], axis=1)
            preact = jnp.dot(weight, patch, preferred_element_type=jnp.float32) + bias
            scaled = soft_scale * preact
            e = jnp.exp(-jnp.abs(scaled))
            softplus = jnp.maximum(scaled, 0.0) + jnp.log1p(e)
            activated = leak_slope * preact + (1.0 - leak_slope) / soft_scale * softplus
            for h in range(pooled_rows):
                pair = (
                    activated[:, 2 * h * rows : (2 * h + 1) * rows]
                    + activated[:, (2 * h + 1) * rows : (2 * h + 2) * rows]
                )
                totals[h] = pair if totals[h] is None else totals[h] + pair
            sigmoid = jnp.where(scaled >= 0.0, 1.0, e) / (1.0 + e)
            slope = leak_slope + (1.0 - leak_slope) * sigmoid
            delta = (slope * spread_all).astype(jnp.bfloat16)
            term = lax.dot_general(
                delta, patch, (((1,), (1,)), ((), ())), preferred_element_type=jnp.float32
            )
            wg = term if wg is None else wg + term
            part = jnp.dot(delta, ones_ref[...], preferred_element_type=jnp.float32)
            bg = part if bg is None else bg + part
            spreads.append(jnp.dot(spread_w, delta, preferred_element_type=jnp.float32))
        acc_main = {}
        acc_edge = {}
        for px in range(2):
            for r in range(group):
                cols = slice(r * rows, (r + 1) * rows)
                for a in range(3):
                    for b in range(3):
                        at = (a * 3 + b) * 3 * slots
                        g = spreads[px]
                        v0 = pltpu.roll(g[at : at + slots, cols], rows - 1, 1)
                        v1 = g[at + slots : at + 2 * slots, cols]
                        v2 = pltpu.roll(g[at + 2 * slots : at + 3 * slots, cols], 1, 1)
                        inner = jnp.where(last, 0.0, v0) + v1 + jnp.where(first, 0.0, v2)
                        edge = jnp.where(last, v0, 0.0) + jnp.where(first, v2, 0.0)
                        key = (px + a, r + b)
                        if key in acc_main:
                            acc_main[key] = acc_main[key] + inner
                            acc_edge[key] = acc_edge[key] + edge
                        else:
                            acc_main[key] = inner
                            acc_edge[key] = edge
        for (dx, dy), value in acc_main.items():
            out = (step * 2 + dx) * wide_y + (j * group + dy)
            main_ref[out] += value[: main_ref.shape[1]]
            edge_ref[out] += acc_edge[dx, dy][: edge_ref.shape[1]]
        wg_acc[...] += wg
        bg_acc[...] += bg[:, :1]
        for m in range(pieces):
            pooled = None
            for half in range(2):
                value = totals[2 * m + half]
                high = value.astype(jnp.bfloat16)
                low = (value - high.astype(jnp.float32)).astype(jnp.bfloat16)
                both = jnp.concatenate([high, low], axis=0)
                part = jnp.dot(both, q_ref[half], preferred_element_type=jnp.float32)
                part = part[: value.shape[0]] + part[value.shape[0] :]
                pooled = part if pooled is None else pooled + part
            at = pl.multiple_of((j * pieces + m) * rows, rows)
            pooled_ref[:, pl.ds(at, rows)] = (pooled * 0.125).astype(pooled_ref.dtype)

    @pl.when(step == pl.num_programs(0) - 1)
    def _():
        wg_ref[...] = wg_acc[...]
        bg_ref[...] = bg_acc[...]


def forward(weight, bias, patches, cot, pairs, wide_x, wide_y):
    lines, taps, rows = patches.shape
    chan_out, chan_in = weight.shape[:2]
    weight_mat = weight.reshape(chan_out, taps)
    slots = 8
    spread_w = jnp.transpose(weight, (2, 3, 4, 1, 0))
    spread_w = jnp.pad(spread_w, ((0, 0), (0, 0), (0, 0), (0, slots - chan_in), (0, 0)))
    spread_w = spread_w.reshape(27 * slots, chan_out)
    half = rows // 2
    z = jnp.arange(rows)
    k = jnp.arange(rows)
    pool = jnp.stack(
        [(k[None, :] == z[:, None] // 2), (k[None, :] == half + z[:, None] // 2)]
    ).astype(jnp.bfloat16)
    spread = jnp.stack(
        [(z[None, :] // 2 == k[:, None]), (z[None, :] // 2 + half == k[:, None])]
    ).astype(jnp.bfloat16)
    full = lambda shape: pl.BlockSpec(shape, lambda p: (0,) * len(shape))
    block = lines // pairs
    acc_shape = (wide_x * wide_y, chan_in, rows)
    return pl.pallas_call(
        lambda *refs: forward_kernel(rows, wide_y, *refs),
        grid=(pairs,),
        out_shape=(
            jax.ShapeDtypeStruct(cot.shape, jnp.bfloat16),
            jax.ShapeDtypeStruct((chan_out, taps), jnp.float32),
            jax.ShapeDtypeStruct((chan_out, 1), jnp.float32),
            jax.ShapeDtypeStruct(acc_shape, jnp.float32),
            jax.ShapeDtypeStruct(acc_shape, jnp.float32),
        ),
        in_specs=[
            full((chan_out, taps)),
            full((chan_out, 1)),
            full((2, rows, rows)),
            full((2, rows, rows)),
            full((27 * slots, chan_out)),
            full((BLOCK_ROWS * rows, rows)),
            pl.BlockSpec((block, taps, rows), lambda p: (p, 0, 0)),
            pl.BlockSpec((chan_out, cot.shape[1] // pairs), lambda p: (0, p)),
        ],
        out_specs=(
            pl.BlockSpec((chan_out, cot.shape[1] // pairs), lambda p: (0, p)),
            full((chan_out, taps)),
            full((chan_out, 1)),
            full(acc_shape),
            full(acc_shape),
        ),
        scratch_shapes=[
            pltpu.VMEM((chan_out, taps), jnp.float32),
            pltpu.VMEM((chan_out, 1), jnp.float32),
        ],
    )(weight_mat, bias, pool, spread, spread_w, jnp.ones((BLOCK_ROWS * rows, rows), jnp.bfloat16),
      patches, cot)


def fold_halo(main, axis, dim, width):
    count = lax.axis_size(axis)
    size = main.shape[dim]
    head = lax.slice_in_dim(main, 0, width, axis=dim)
    tail = lax.slice_in_dim(main, size - width, size, axis=dim)
    from_left = lax.ppermute(tail, axis, [(i, (i + 1) % count) for i in range(count)])
    from_right = lax.ppermute(head, axis, [((i + 1) % count, i) for i in range(count)])
    inner = lax.slice_in_dim(main, width, size - width, axis=dim)
    inner_size = size - 2 * width
    start = [0] * main.ndim
    inner = lax.dynamic_update_slice(
        inner, lax.slice_in_dim(inner, 0, width, axis=dim) + from_left, start
    )
    start[dim] = inner_size - width
    inner = lax.dynamic_update_slice(
        inner, lax.slice_in_dim(inner, inner_size - width, inner_size, axis=dim) + from_right, start
    )
    return inner


def on_device(cells, weight, bias, cotangent):
    chan_in, cells_x, cells_y, cells_z = cells.shape
    chan_out = weight.shape[0]
    stencil = [
        (shift_a, shift_b, shift_e)
        for shift_a in range(3)
        for shift_b in range(3)
        for shift_e in range(3)
    ]
    widened = extended(cells, (("gx", 1), ("gy", 2), ("gz", 3)), 1)
    patches = jnp.stack(
        [
            jnp.transpose(
                widened[:, sa : sa + cells_x, sb : sb + cells_y, se : se + cells_z], (1, 2, 0, 3)
            )
            for sa, sb, se in stencil
        ],
        axis=3,
    )
    patches = patches.reshape(cells_x * cells_y, chan_in * 27, cells_z)
    cot = cotangent.reshape(chan_out, -1)
    wide_x, wide_y = cells_x + 2, cells_y + 2
    pooled, weight_local, bias_local, main, edge = forward(
        weight, bias.reshape(chan_out, 1), patches, cot, cells_x // 2, wide_x, wide_y
    )
    pooled = pooled.reshape(cotangent.shape)
    taps = chan_in * 27
    width = -(-(taps + 1) // 128) * 128
    partial = jnp.concatenate(
        [weight_local, bias_local, jnp.zeros((chan_out, width - taps - 1), jnp.float32)],
        axis=1,
    )
    sizes = tuple(lax.axis_size(a) for a in AXES)
    both = allreduce(partial, sizes)
    weight_grad = both[:, :taps].reshape(chan_out, chan_in, 3, 3, 3)
    bias_grad = both[:, taps]
    main = main.reshape(wide_x, wide_y, chan_in, cells_z)
    edge = edge.reshape(wide_x, wide_y, chan_in, cells_z)
    lo = edge[..., cells_z - 1 :]
    hi = edge[..., :1]
    count = lax.axis_size("gz")
    from_left = lax.ppermute(hi, "gz", [(i, (i + 1) % count) for i in range(count)])
    from_right = lax.ppermute(lo, "gz", [((i + 1) % count, i) for i in range(count)])
    main = jnp.concatenate(
        [
            main[..., :1] + from_left,
            main[..., 1 : cells_z - 1],
            main[..., cells_z - 1 :] + from_right,
        ],
        axis=3,
    )
    main = fold_halo(main, "gy", 1, 1)
    main = fold_halo(main, "gx", 0, 1)
    input_grad = jnp.transpose(main, (2, 0, 1, 3))
    return (pooled, weight_grad, bias_grad, input_grad)


def solution(mesh):
    in_specs = (P(None, "gx", "gy", "gz"), P(), P(), P(None, "gx", "gy", "gz"))
    out_specs = (P(None, "gx", "gy", "gz"), P(), P(), P(None, "gx", "gy", "gz"))
    return jax.shard_map(
        on_device, mesh=mesh, in_specs=in_specs, out_specs=out_specs, check_vma=False
    )
```

```python
import jax
import jax.numpy as jnp
from jax import lax
from jax.experimental import pallas as pl
from jax.experimental.pallas import tpu as pltpu
from jax.sharding import PartitionSpec as P

MESH = pl.DeviceIdType.MESH
AXES = ("gx", "gy", "gz")

leak_slope = 0.3
soft_scale = 10.0


def extended(cells, sides, width):
    for axis, dim in sides:
        count = lax.axis_size(axis)
        head = lax.slice_in_dim(cells, 0, width, axis=dim)
        tail = lax.slice_in_dim(cells, cells.shape[dim] - width, cells.shape[dim], axis=dim)
        cells = jnp.concatenate(
            [
                lax.ppermute(tail, axis, [(i, (i + 1) % count) for i in range(count)]),
                cells,
                lax.ppermute(head, axis, [((i + 1) % count, i) for i in range(count)]),
            ],
            axis=dim,
        )
    return cells


def allreduce_kernel(sizes, x_ref, o_ref, slots_a, slots_b, acc_a, send_a, recv_a, send_b, recv_b):
    me = tuple(lax.axis_index(a) for a in AXES)
    groups = (
        [(k,) for k in range(sizes[0])],
        [(k, m) for k in range(sizes[1]) for m in range(sizes[2])],
    )
    places = ((0,), (1, 2))

    def device(phase, member):
        coords = list(me)
        for axis, value in zip(places[phase], member):
            coords[axis] = value
        return tuple(coords)

    def rank(phase):
        out = 0
        for axis in places[phase]:
            out = out * sizes[axis] + me[axis]
        return out

    def member_of(phase, index):
        out = []
        for axis in reversed(places[phase]):
            out.append(lax.rem(index, sizes[axis]))
            index = index // sizes[axis]
        return tuple(reversed(out))

    barrier = pltpu.get_barrier_semaphore()
    count = 0
    for phase in range(2):
        n = len(groups[phase])
        for d in range(1, n):
            target = member_of(phase, lax.rem(rank(phase) + d, n))
            pl.semaphore_signal(barrier, inc=1, device_id=device(phase, target), device_id_type=MESH)
            count += 1
    pl.semaphore_wait(barrier, count)

    slots = (slots_a, slots_b)
    sends = (send_a, send_b)
    recvs = (recv_a, recv_b)
    sources = (x_ref, acc_a)
    sinks = (acc_a, o_ref)
    for phase in range(2):
        n = len(groups[phase])
        src, held, sink = sources[phase], slots[phase], sinks[phase]
        mine = rank(phase)
        copies = []
        for d in range(1, n):
            target = member_of(phase, lax.rem(mine + d, n))
            copy = pltpu.make_async_remote_copy(
                src_ref=src,
                dst_ref=held.at[mine],
                send_sem=sends[phase].at[d],
                recv_sem=recvs[phase].at[mine],
                device_id=device(phase, target),
                device_id_type=MESH,
            )
            copy.start()
            copies.append(copy)
        held[mine] = src[...]
        for d in range(1, n):
            origin = lax.rem(mine + n - d, n)
            incoming = pltpu.make_async_remote_copy(
                src_ref=src,
                dst_ref=held.at[origin],
                send_sem=sends[phase].at[d],
                recv_sem=recvs[phase].at[origin],
                device_id=device(phase, member_of(phase, origin)),
                device_id_type=MESH,
            )
            incoming.wait_recv()
        for copy in copies:
            copy.wait_send()
        total = held[0]
        for k in range(1, n):
            total = total + held[k]
        sink[...] = total


def allreduce(x, sizes):
    shape = x.shape
    first, second = sizes[0], sizes[1] * sizes[2]
    return pl.pallas_call(
        lambda *refs: allreduce_kernel(sizes, *refs),
        out_shape=jax.ShapeDtypeStruct(shape, jnp.float32),
        in_specs=[pl.BlockSpec(memory_space=pltpu.VMEM)],
        out_specs=pl.BlockSpec(memory_space=pltpu.VMEM),
        scratch_shapes=[
            pltpu.VMEM((first,) + shape, jnp.float32),
            pltpu.VMEM((second,) + shape, jnp.float32),
            pltpu.VMEM(shape, jnp.float32),
            pltpu.SemaphoreType.DMA((first,)),
            pltpu.SemaphoreType.DMA((first,)),
            pltpu.SemaphoreType.DMA((second,)),
            pltpu.SemaphoreType.DMA((second,)),
        ],
        compiler_params=pltpu.CompilerParams(collective_id=0, has_side_effects=True),
    )(x)


def forward_kernel(rows, wide_y, w_ref, b_ref, q_ref, u_ref, wt_ref, p_ref, cot_ref,
                   pooled_ref, wg_ref, bg_ref, main_ref, edge_ref, wg_acc, bg_acc):
    step = pl.program_id(0)
    plane = p_ref.shape[0] // 2
    lines = plane // 4

    @pl.when(step == 0)
    def _():
        wg_acc[...] = jnp.zeros_like(wg_acc)
        bg_acc[...] = jnp.zeros_like(bg_acc)
        main_ref[...] = jnp.zeros_like(main_ref)
        edge_ref[...] = jnp.zeros_like(edge_ref)

    weight = w_ref[...]
    bias = b_ref[...]
    spread_w = wt_ref[...]
    slots = spread_w.shape[0] // 27
    lane = lax.broadcasted_iota(jnp.int32, (slots, rows), 1)
    first = lane == 0
    last = lane == rows - 1

    group = 32
    up_both = jnp.concatenate([u_ref[0], u_ref[1]], axis=1)
    pool_both = jnp.concatenate([q_ref[0], q_ref[1]], axis=0)
    pooled_rows = group // 2
    pieces = pooled_rows // 2

    @pl.loop(0, plane // group)
    def _(j):
        ups = []
        for m in range(pieces):
            cot = cot_ref[:, pl.ds(pl.multiple_of((j * pieces + m) * rows, rows), rows)]
            up = jnp.dot(cot, up_both, preferred_element_type=jnp.float32) * 0.125
            ups.append(up[:, :rows])
            ups.append(up[:, rows:])
        spread_all = jnp.concatenate([ups[r // 2] for r in range(group)], axis=1)
        totals = [None] * pooled_rows
        wg = None
        bg = None
        spreads = []
        for px, base in enumerate((0, plane)):
            patch = jnp.concatenate([p_ref[base + j * group + r] for r in range(group)], axis=1)
            preact = jnp.dot(weight, patch, preferred_element_type=jnp.float32) + bias
            scaled = soft_scale * preact
            e = jnp.exp(-jnp.abs(scaled))
            softplus = jnp.maximum(scaled, 0.0) + jnp.log1p(e)
            activated = leak_slope * preact + (1.0 - leak_slope) / soft_scale * softplus
            for h in range(pooled_rows):
                pair = (
                    activated[:, 2 * h * rows : (2 * h + 1) * rows]
                    + activated[:, (2 * h + 1) * rows : (2 * h + 2) * rows]
                )
                totals[h] = pair if totals[h] is None else totals[h] + pair
            sigmoid = jnp.where(scaled >= 0.0, 1.0, e) / (1.0 + e)
            slope = leak_slope + (1.0 - leak_slope) * sigmoid
            delta = (slope * spread_all).astype(jnp.bfloat16)
            term = lax.dot_general(
                delta, patch, (((1,), (1,)), ((), ())), preferred_element_type=jnp.float32
            )
            wg = term if wg is None else wg + term
            part = delta.astype(jnp.float32)
            bg = part if bg is None else bg + part
            spreads.append(jnp.dot(spread_w, delta, preferred_element_type=jnp.float32))
        acc_main = {}
        acc_edge = {}
        for px in range(2):
            for r in range(group):
                cols = slice(r * rows, (r + 1) * rows)
                for a in range(3):
                    for b in range(3):
                        at = (a * 3 + b) * 3 * slots
                        g = spreads[px]
                        v0 = pltpu.roll(g[at : at + slots, cols], rows - 1, 1)
                        v1 = g[at + slots : at + 2 * slots, cols]
                        v2 = pltpu.roll(g[at + 2 * slots : at + 3 * slots, cols], 1, 1)
                        inner = jnp.where(last, 0.0, v0) + v1 + jnp.where(first, 0.0, v2)
                        edge = jnp.where(last, v0, 0.0) + jnp.where(first, v2, 0.0)
                        key = (px + a, r + b)
                        if key in acc_main:
                            acc_main[key] = acc_main[key] + inner
                            acc_edge[key] = acc_edge[key] + edge
                        else:
                            acc_main[key] = inner
                            acc_edge[key] = edge
        for (dx, dy), value in acc_main.items():
            out = (step * 2 + dx) * wide_y + (j * group + dy)
            main_ref[out] += value[: main_ref.shape[1]]
            edge_ref[out] += acc_edge[dx, dy][: edge_ref.shape[1]]
        wg_acc[...] += wg
        bg_acc[...] += jnp.sum(bg, axis=1, keepdims=True)
        for m in range(pieces):
            value = jnp.concatenate([totals[2 * m], totals[2 * m + 1]], axis=1)
            high = value.astype(jnp.bfloat16)
            low = (value - high.astype(jnp.float32)).astype(jnp.bfloat16)
            part = jnp.dot(
                jnp.concatenate([high, low], axis=0), pool_both, preferred_element_type=jnp.float32
            )
            pooled = part[: value.shape[0]] + part[value.shape[0] :]
            at = pl.multiple_of((j * pieces + m) * rows, rows)
            pooled_ref[:, pl.ds(at, rows)] = (pooled * 0.125).astype(pooled_ref.dtype)

    @pl.when(step == pl.num_programs(0) - 1)
    def _():
        wg_ref[...] = wg_acc[...]
        bg_ref[...] = bg_acc[...]


def forward(weight, bias, patches, cot, pairs, wide_x, wide_y):
    lines, taps, rows = patches.shape
    chan_out, chan_in = weight.shape[:2]
    weight_mat = weight.reshape(chan_out, taps)
    slots = 8
    spread_w = jnp.transpose(weight, (2, 3, 4, 1, 0))
    spread_w = jnp.pad(spread_w, ((0, 0), (0, 0), (0, 0), (0, slots - chan_in), (0, 0)))
    spread_w = spread_w.reshape(27 * slots, chan_out)
    half = rows // 2
    z = jnp.arange(rows)
    k = jnp.arange(rows)
    pool = jnp.stack(
        [(k[None, :] == z[:, None] // 2), (k[None, :] == half + z[:, None] // 2)]
    ).astype(jnp.bfloat16)
    spread = jnp.stack(
        [(z[None, :] // 2 == k[:, None]), (z[None, :] // 2 + half == k[:, None])]
    ).astype(jnp.bfloat16)
    full = lambda shape: pl.BlockSpec(shape, lambda p: (0,) * len(shape))
    block = lines // pairs
    acc_shape = (wide_x * wide_y, chan_in, rows)
    return pl.pallas_call(
        lambda *refs: forward_kernel(rows, wide_y, *refs),
        grid=(pairs,),
        out_shape=(
            jax.ShapeDtypeStruct(cot.shape, jnp.bfloat16),
            jax.ShapeDtypeStruct((chan_out, taps), jnp.float32),
            jax.ShapeDtypeStruct((chan_out, 1), jnp.float32),
            jax.ShapeDtypeStruct(acc_shape, jnp.float32),
            jax.ShapeDtypeStruct(acc_shape, jnp.float32),
        ),
        in_specs=[
            full((chan_out, taps)),
            full((chan_out, 1)),
            full((2, rows, rows)),
            full((2, rows, rows)),
            full((27 * slots, chan_out)),
            pl.BlockSpec((block, taps, rows), lambda p: (p, 0, 0)),
            pl.BlockSpec((chan_out, cot.shape[1] // pairs), lambda p: (0, p)),
        ],
        out_specs=(
            pl.BlockSpec((chan_out, cot.shape[1] // pairs), lambda p: (0, p)),
            full((chan_out, taps)),
            full((chan_out, 1)),
            full(acc_shape),
            full(acc_shape),
        ),
        scratch_shapes=[
            pltpu.VMEM((chan_out, taps), jnp.float32),
            pltpu.VMEM((chan_out, 1), jnp.float32),
        ],
    )(weight_mat, bias, pool, spread, spread_w, patches, cot)


def fold_halo(main, axis, dim, width):
    count = lax.axis_size(axis)
    size = main.shape[dim]
    head = lax.slice_in_dim(main, 0, width, axis=dim)
    tail = lax.slice_in_dim(main, size - width, size, axis=dim)
    from_left = lax.ppermute(tail, axis, [(i, (i + 1) % count) for i in range(count)])
    from_right = lax.ppermute(head, axis, [((i + 1) % count, i) for i in range(count)])
    inner = lax.slice_in_dim(main, width, size - width, axis=dim)
    inner_size = size - 2 * width
    start = [0] * main.ndim
    inner = lax.dynamic_update_slice(
        inner, lax.slice_in_dim(inner, 0, width, axis=dim) + from_left, start
    )
    start[dim] = inner_size - width
    inner = lax.dynamic_update_slice(
        inner, lax.slice_in_dim(inner, inner_size - width, inner_size, axis=dim) + from_right, start
    )
    return inner


def on_device(cells, weight, bias, cotangent):
    chan_in, cells_x, cells_y, cells_z = cells.shape
    chan_out = weight.shape[0]
    stencil = [
        (shift_a, shift_b, shift_e)
        for shift_a in range(3)
        for shift_b in range(3)
        for shift_e in range(3)
    ]
    widened = extended(cells, (("gx", 1), ("gy", 2), ("gz", 3)), 1)
    patches = jnp.stack(
        [
            jnp.transpose(
                widened[:, sa : sa + cells_x, sb : sb + cells_y, se : se + cells_z], (1, 2, 0, 3)
            )
            for sa, sb, se in stencil
        ],
        axis=3,
    )
    patches = patches.reshape(cells_x * cells_y, chan_in * 27, cells_z)
    cot = cotangent.reshape(chan_out, -1)
    wide_x, wide_y = cells_x + 2, cells_y + 2
    pooled, weight_local, bias_local, main, edge = forward(
        weight, bias.reshape(chan_out, 1), patches, cot, cells_x // 2, wide_x, wide_y
    )
    pooled = pooled.reshape(cotangent.shape)
    taps = chan_in * 27
    width = -(-(taps + 1) // 128) * 128
    partial = jnp.concatenate(
        [weight_local, bias_local, jnp.zeros((chan_out, width - taps - 1), jnp.float32)],
        axis=1,
    )
    sizes = tuple(lax.axis_size(a) for a in AXES)
    both = allreduce(partial, sizes)
    weight_grad = both[:, :taps].reshape(chan_out, chan_in, 3, 3, 3)
    bias_grad = both[:, taps]
    main = main.reshape(wide_x, wide_y, chan_in, cells_z)
    edge = edge.reshape(wide_x, wide_y, chan_in, cells_z)
    lo = edge[..., cells_z - 1 :]
    hi = edge[..., :1]
    count = lax.axis_size("gz")
    from_left = lax.ppermute(hi, "gz", [(i, (i + 1) % count) for i in range(count)])
    from_right = lax.ppermute(lo, "gz", [((i + 1) % count, i) for i in range(count)])
    main = jnp.concatenate(
        [
            main[..., :1] + from_left,
            main[..., 1 : cells_z - 1],
            main[..., cells_z - 1 :] + from_right,
        ],
        axis=3,
    )
    main = fold_halo(main, "gy", 1, 1)
    main = fold_halo(main, "gx", 0, 1)
    input_grad = jnp.transpose(main, (2, 0, 1, 3))
    return (pooled, weight_grad, bias_grad, input_grad)


def solution(mesh):
    in_specs = (P(None, "gx", "gy", "gz"), P(), P(), P(None, "gx", "gy", "gz"))
    out_specs = (P(None, "gx", "gy", "gz"), P(), P(), P(None, "gx", "gy", "gz"))
    return jax.shard_map(
        on_device, mesh=mesh, in_specs=in_specs, out_specs=out_specs, check_vma=False
    )
```
